128 devices in a mesh: row: 8 (over z_hi, x), col: 16 (over z_lo, y, core).
Axes of the slice: x: 4, y: 4, z: 4 (z_hi: 2, z_lo: 2; z = z_hi * 2 + z_lo), core: 2. Of those that a mesh axis runs over, the one named last changes fastest.
Arguments:
- samples: bfloat16 [16, 8, 256, 16384], P('col', 'row'), may hold values from -6 to 6
- w_start: float32 [32768, 256], P(('row', 'col')), may hold values from 0.005 to 2
- h_start: float32 [256, 8192], P('row', 'col'), may hold values from 0.005 to 2
Outputs:
- w_final: float32 [32768, 256], P(('row', 'col'))
- h_final: float32 [256, 8192], P('row', 'col')
The draws below stay inside these ranges and needn't reach their ends.
All inputs are finite; a program needn't handle non-finite values.
Results may differ from the reference program's by a relative error of at most 0.0013.
Values may be sent and summed in bfloat16 or wider, within the bound.
No kernel may reach another device: no remote copies, remote signals or barrier semaphores. Data moves between devices by JAX's collectives and lax.ppermute only.
A program may use at most 128 MiB of HBM per device.

```python
import math
import jax
import jax.numpy as jnp
from jax import lax

CH = 256
BINS = 128
RANK = 256
FR = 64
ITERS = 2
WIN = 256
CHB = 32768
FRAMES = 8192
N_ROW = 8
N_COL = 16


def draw_samples(key, part):
    subkeys = [jax.random.fold_in(key, 101 + index) for index in range(7)]
    full_shape = (N_COL, N_ROW, CH, FR, WIN)
    white_noise = jax.random.normal(subkeys[0], full_shape, jnp.float32)
    block_level = jax.random.uniform(subkeys[1], (N_COL, N_ROW, CH, 1, 1), jnp.float32, -0.9, 0.9)
    frame_level = jax.random.uniform(subkeys[2], (N_COL, N_ROW, CH, FR, 1), jnp.float32, -0.6, 0.6)
    tone_bins = jax.random.randint(subkeys[3], (CH, 3), 1, BINS).astype(jnp.int32)
    amplitude = jax.random.uniform(subkeys[4], (CH, 3, 1), jnp.float32, 0.3, 1.0)
    offset = jax.random.uniform(subkeys[5], (CH, 3, 1), jnp.float32, -math.pi, math.pi)
    sample_idx = jnp.arange(WIN, dtype=jnp.int32)
    phase_steps = tone_bins[:, :, None] * sample_idx[None, None, :] % WIN
    tone_wave = jnp.sum(amplitude * jnp.cos(phase_steps.astype(jnp.float32) * (2.0 * math.pi / WIN) + offset), axis=1)
    tone_level = jnp.exp(jax.random.uniform(subkeys[6], (N_COL, N_ROW, CH, 1, 1), jnp.float32, -1.0, 1.0))
    values = white_noise * jnp.exp(block_level + frame_level) + tone_level * tone_wave[None, None, :, None, :]
    values = jnp.clip(values, -6.0, 6.0)
    return values.reshape(N_COL, N_ROW, CH, FR * WIN).astype(jnp.bfloat16)


def draw_w_start(key, part):
    base_key = jax.random.fold_in(key, 201)
    choose_key = jax.random.fold_in(key, 202)
    base = jnp.exp(jax.random.uniform(base_key, (CHB, RANK), jnp.float32, math.log(0.01), math.log(0.1)))
    boost = 20.0
    chosen = jax.random.randint(choose_key, (CH, 1, RANK), 0, 16) == 0
    favour = jnp.broadcast_to(jnp.where(chosen, boost, 1.0).astype(jnp.float32), (CH, BINS, RANK)).reshape(CHB, RANK)
    return (base * favour).astype(jnp.float32)


def draw_h_start(key, part):
    base_key = jax.random.fold_in(key, 301)
    choose_key = jax.random.fold_in(key, 302)
    base = jnp.exp(jax.random.uniform(base_key, (RANK, FRAMES), jnp.float32, math.log(0.01), math.log(0.1)))
    boost = 20.0
    block_count = FRAMES // FR
    chosen = jax.random.randint(choose_key, (RANK, block_count, 1), 0, 16) == 0
    favour = jnp.broadcast_to(jnp.where(chosen, boost, 1.0).astype(jnp.float32), (RANK, block_count, FR)).reshape(RANK, FRAMES)
    return (base * favour).astype(jnp.float32)


def setup_inputs(seed: int = 0) -> dict:
    splits = jax.random.split(jax.random.key(seed), 4)
    samples = draw_samples(jax.random.fold_in(splits[3], 71), 0)
    w_start = draw_w_start(jax.random.fold_in(splits[3], 71), 0)
    h_start = draw_h_start(jax.random.fold_in(splits[3], 71), 0)
    return {"samples": samples, "w_start": w_start, "h_start": h_start}


def dft_table():
    sample_idx = jnp.arange(WIN, dtype=jnp.int32)
    bin_idx = jnp.arange(BINS, dtype=jnp.int32)
    phases = sample_idx[:, None] * bin_idx[None, :] % WIN
    phases = phases.astype(jnp.float32) * (2.0 * math.pi / WIN)
    shaping = 0.5 - 0.5 * jnp.cos(sample_idx.astype(jnp.float32) * (2.0 * math.pi / WIN))
    shaping = shaping / math.sqrt(3.0 * WIN / 8.0)
    both = jnp.concatenate([shaping[:, None] * jnp.cos(phases), -shaping[:, None] * jnp.sin(phases)], axis=1)
    return both.astype(jnp.bfloat16)

def reference(samples, w_start, h_start):
    table = dft_table()
    record = samples.transpose(2, 0, 1, 3).reshape(CH, FRAMES, WIN)

    def channel_energy(trace):
        spectrum = jnp.dot(trace, table, preferred_element_type=jnp.float32)
        real_part = spectrum[:, :BINS]
        imag_part = spectrum[:, BINS:]
        return (real_part * real_part + imag_part * imag_part).astype(jnp.bfloat16)
    energy = lax.map(channel_energy, record)
    spectra = energy.transpose(0, 2, 1).reshape(CHB, FRAMES)
    block_rows = CHB // N_ROW
    spectra_blocks = spectra.reshape(N_ROW, block_rows, FRAMES)
    w_state = w_start
    h_state = h_start
    for sweep in range(ITERS):
        w_b = w_state.astype(jnp.bfloat16)
        h_b = h_state.astype(jnp.bfloat16)

        def block_step(running, inputs):
            spectra_part, w_part = inputs
            recon = jnp.dot(w_part, h_b, preferred_element_type=jnp.float32)
            quotient = (spectra_part / recon).astype(jnp.bfloat16)
            h_add = jnp.dot(w_part.T, quotient, preferred_element_type=jnp.float32)
            w_part_numer = jnp.dot(quotient, h_b.T, preferred_element_type=jnp.float32)
            return (running + h_add, w_part_numer)
        h_numer, w_numer = lax.scan(block_step, jnp.zeros((RANK, FRAMES), jnp.float32), (spectra_blocks, w_b.reshape(N_ROW, block_rows, RANK)))
        w_numer = w_numer.reshape(CHB, RANK)
        w_colsum = lax.optimization_barrier(jnp.sum(w_b.astype(jnp.float32), axis=0))
        h_rowsum = lax.optimization_barrier(jnp.sum(h_b.astype(jnp.float32), axis=1))
        h_state = h_state * h_numer / w_colsum[:, None]
        w_state = w_state * w_numer / h_rowsum[None, :]
    return (w_state, h_state)
```

```python
import math

import jax
import jax.numpy as jnp
import numpy as np
from jax import lax
from jax.experimental import pallas as pl
from jax.experimental.pallas import tpu as pltpu
from jax.sharding import Mesh
from jax.sharding import PartitionSpec as P

BINS = 128
ITERS = 2
WIN = 256

AXES = ("zh", "x", "zl", "y", "core")
SIZES = (2, 4, 2, 4, 2)
ROWS = ("core", "zh", "x")
COLS = ("zl", "y")
N_ROWS = 16
N_COLS = 8


def dft_table():
    n = np.arange(WIN, dtype=np.int32)
    k = np.arange(BINS, dtype=np.int32)
    phases = (n[:, None] * k[None, :] % WIN).astype(np.float32) * np.float32(2.0 * math.pi / WIN)
    taper = np.float32(0.5) - np.float32(0.5) * np.cos(n.astype(np.float32) * np.float32(2.0 * math.pi / WIN))
    taper = (taper / np.float32(math.sqrt(3.0 * WIN / 8.0))).astype(np.float32)
    both = np.concatenate([taper[:, None] * np.cos(phases), -taper[:, None] * np.sin(phases)], axis=1)
    return jnp.asarray(both.astype(np.float32)).astype(jnp.bfloat16)


def energy_kernel(x_ref, table_ref, out_ref, flat_ref):
    chans = x_ref.shape[0]
    frames = x_ref.shape[1] // WIN
    table = table_ref[...]
    group = 16
    for g in range(frames // group):
        x = jnp.concatenate(
            [x_ref[:, (g * group + f) * WIN : (g * group + f + 1) * WIN] for f in range(group)], axis=0
        )
        spec = jnp.dot(x, table, preferred_element_type=jnp.float32)
        re, im = spec[:, :BINS], spec[:, BINS:]
        flat_ref[g * group * chans : (g + 1) * group * chans, :] = re * re + im * im
    for c in range(chans):
        q, core, j = c // 4, (c // 2) % 2, c % 2
        at = (q * 2 + j) * BINS
        out_ref[core, 0, :, at : at + BINS] = flat_ref[pl.ds(c, frames, stride=chans), :].astype(jnp.bfloat16)


def energies(record, table):
    channels, samples = record.shape
    frames = samples // WIN
    per_row = channels // (N_ROWS // 2)
    rows = channels * BINS // N_ROWS
    return pl.pallas_call(
        energy_kernel,
        grid=(N_ROWS // 2,),
        in_specs=[
            pl.BlockSpec((per_row, samples), lambda r: (r, 0)),
            pl.BlockSpec((WIN, 2 * BINS), lambda r: (0, 0)),
        ],
        out_specs=pl.BlockSpec((2, 1, frames, rows), lambda r: (0, r, 0, 0)),
        out_shape=jax.ShapeDtypeStruct((2, N_ROWS // 2, frames, rows), jnp.bfloat16),
        scratch_shapes=[pltpu.VMEM((frames * per_row, BINS), jnp.float32)],
        compiler_params=pltpu.CompilerParams(vmem_limit_bytes=40 << 20),
        cost_estimate=pl.CostEstimate(
            flops=2 * channels * frames * WIN * WIN, bytes_accessed=12 << 20, transcendentals=0
        ),
        name="energy",
    )(record, table)


def split(x):
    hi = x.astype(jnp.bfloat16)
    return hi, (x - hi.astype(jnp.float32)).astype(jnp.bfloat16)


def sweep_kernel(s_ref, h_ref, w_ref, wn_ref, hn_ref, ht_ref, acc_ref, cs_ref, rs_ref):
    q = pl.program_id(0)
    rank = w_ref.shape[2]
    half = h_ref.shape[2]

    @pl.when(q == 0)
    def _():
        for c in range(2):
            ht_ref[c * half : (c + 1) * half, :] = h_ref[c].T
        ones = jnp.ones((16, 2 * half), jnp.bfloat16)
        rs_ref[...] = jnp.dot(ones, ht_ref[...], preferred_element_type=jnp.float32)
        cs_ref[...] = jnp.zeros_like(cs_ref)

    w = w_ref[0]
    recon = lax.dot_general(ht_ref[...], w, (((1,), (1,)), ((), ())), preferred_element_type=jnp.float32)
    quotient = (s_ref[...].astype(jnp.float32) / recon).astype(jnp.bfloat16)
    wn = jnp.dot(h_ref[0], quotient[:half], preferred_element_type=jnp.float32)
    wn = wn + jnp.dot(h_ref[1], quotient[half:], preferred_element_type=jnp.float32)
    wn_ref[0, :rank, :] = wn.astype(jnp.bfloat16)
    hi, lo = split(rs_ref[...])
    wn_ref[0, rank:, :] = jnp.where(lax.broadcasted_iota(jnp.int32, hi.shape, 0) == 0, hi, lo)
    cs_ref[...] += jnp.sum(w.astype(jnp.float32), axis=0, keepdims=True)
    hn = jnp.dot(quotient, w, preferred_element_type=jnp.float32)

    @pl.when(q == 0)
    def _():
        acc_ref[...] = hn

    @pl.when(q > 0)
    def _():
        acc_ref[...] += hn

    @pl.when(q == N_COLS - 1)
    def _():
        column = jnp.broadcast_to(cs_ref[0:1, :], (128, rank)).T
        hi, lo = split(column)
        sums = jnp.where(lax.broadcasted_iota(jnp.int32, hi.shape, 1) == 0, hi, lo)
        each = rank // (N_ROWS // 2)
        for c in range(2):
            hn = acc_ref[c * half : (c + 1) * half, :].T.astype(jnp.bfloat16)
            for r in range(N_ROWS // 2):
                hn_ref[c * 8 + r, :, :half] = hn[r * each : (r + 1) * each, :]
                hn_ref[c * 8 + r, :, half:] = sums[r * each : (r + 1) * each, :]


def sweep(spectra, h, w):
    frames, rows = spectra.shape
    rank, half = h.shape[1], h.shape[2]
    block = rows // N_COLS
    each = rank // (N_ROWS // 2)
    return pl.pallas_call(
        sweep_kernel,
        grid=(N_COLS,),
        in_specs=[
            pl.BlockSpec((frames, block), lambda q: (0, q)),
            pl.BlockSpec((2, rank, half), lambda q: (0, 0, 0)),
            pl.BlockSpec((1, block, rank), lambda q: (q, 0, 0)),
        ],
        out_specs=[
            pl.BlockSpec((1, rank + 16, block), lambda q: (q, 0, 0)),
            pl.BlockSpec((N_ROWS, each, half + 128), lambda q: (0, 0, 0)),
        ],
        out_shape=[
            jax.ShapeDtypeStruct((N_COLS, rank + 16, block), jnp.bfloat16),
            jax.ShapeDtypeStruct((N_ROWS, each, half + 128), jnp.bfloat16),
        ],
        scratch_shapes=[
            pltpu.VMEM((frames, rank), jnp.bfloat16),
            pltpu.VMEM((frames, rank), jnp.float32),
            pltpu.VMEM((8, rank), jnp.float32),
            pltpu.VMEM((16, rank), jnp.float32),
        ],
        compiler_params=pltpu.CompilerParams(vmem_limit_bytes=48 << 20),
        cost_estimate=pl.CostEstimate(flops=6 * frames * rows * rank, bytes_accessed=8 << 20, transcendentals=0),
        name="sweep",
    )(spectra, h, w)


def w_update_kernel(parts_ref, w_ref, new_ref, low_ref):
    rank = w_ref.shape[1]
    total = parts_ref[0].astype(jnp.float32)
    for i in range(1, N_COLS):
        total = total + parts_ref[i].astype(jnp.float32)
    rowsum = total[rank : rank + 1, :] + total[rank + 1 : rank + 2, :]
    new = w_ref[...] * total[:rank, :].T / rowsum
    new_ref[...] = new
    low_ref[...] = new.astype(jnp.bfloat16)


def w_update(parts, w):
    return pl.pallas_call(
        w_update_kernel,
        out_shape=[jax.ShapeDtypeStruct(w.shape, jnp.float32), jax.ShapeDtypeStruct(w.shape, jnp.bfloat16)],
        name="w_update",
    )(parts, w)


def h_update_kernel(parts_ref, h_ref, new_ref, low_ref):
    half = h_ref.shape[1]
    total = parts_ref[0].astype(jnp.float32)
    for i in range(1, N_ROWS):
        total = total + parts_ref[i].astype(jnp.float32)
    colsum = total[:, half : half + 1] + total[:, half + 1 : half + 2]
    new = h_ref[...] * total[:, :half] / colsum
    new_ref[...] = new
    low_ref[...] = new.astype(jnp.bfloat16)


def h_update(parts, h):
    return pl.pallas_call(
        h_update_kernel,
        out_shape=[jax.ShapeDtypeStruct(h.shape, jnp.float32), jax.ShapeDtypeStruct(h.shape, jnp.bfloat16)],
        name="h_update",
    )(parts, h)


def exchange(x, axes):
    return lax.all_to_all(x, axes, 0, 0, tiled=True)


def spread(x, axes, peers):
    return exchange(jnp.broadcast_to(x[None], (peers, *x.shape)), axes)


def local(samples, w, h):
    rank = w.shape[1]
    record = samples.reshape(samples.shape[2], samples.shape[3])
    h_all = lax.all_gather(h.astype(jnp.bfloat16), ROWS, axis=0, tiled=False)
    w_all = lax.all_gather(w.astype(jnp.bfloat16), COLS, axis=0, tiled=False)
    energy = energies(record, dft_table())
    frames, rows = energy.shape[2:]
    spectra = exchange(energy.reshape(N_ROWS, frames, rows), ROWS).reshape(N_ROWS * frames, rows)
    for step in range(ITERS):
        w_parts, h_parts = sweep(spectra, h_all.reshape(2, rank, -1), w_all)
        h_parts = exchange(h_parts, ROWS)
        w_parts = exchange(w_parts, COLS)
        h, h_low = h_update(h_parts, h)
        w, w_low = w_update(w_parts, w)
        if step + 1 < ITERS:
            h_all = spread(h_low, ROWS, N_ROWS)
            w_all = spread(w_low, COLS, N_COLS)
    return (w, h)


def solution(mesh):
    fine = Mesh(mesh.devices.reshape(SIZES), AXES)
    row, col = ("zh", "x"), ("zl", "y", "core")
    return jax.shard_map(
        local,
        mesh=fine,
        in_specs=(P(col, row, None, None), P(row + col, None), P(row, col)),
        out_specs=(P(row + col, None), P(row, col)),
        check_vma=False,
    )
```

```python
import math

import jax
import jax.numpy as jnp
import numpy as np
from jax import lax
from jax.experimental import pallas as pl
from jax.experimental.pallas import tpu as pltpu
from jax.sharding import Mesh
from jax.sharding import PartitionSpec as P

BINS = 128
ITERS = 2
WIN = 256

AXES = ("zh", "x", "zl", "y", "core")
SIZES = (2, 4, 2, 4, 2)
TILE = ("core", "zl", "zh", "x")
RANKS = ("zl", "zh", "x")
N_Y = 4
N_R = 8
N_P = 16
PAD = 128


def dft_table():
    n = np.arange(WIN, dtype=np.int32)
    k = np.arange(BINS, dtype=np.int32)
    phases = (n[:, None] * k[None, :] % WIN).astype(np.float32) * np.float32(2.0 * math.pi / WIN)
    taper = np.float32(0.5) - np.float32(0.5) * np.cos(n.astype(np.float32) * np.float32(2.0 * math.pi / WIN))
    taper = (taper / np.float32(math.sqrt(3.0 * WIN / 8.0))).astype(np.float32)
    both = np.concatenate([taper[:, None] * np.cos(phases), -taper[:, None] * np.sin(phases)], axis=1)
    return jnp.asarray(both.astype(np.float32)).astype(jnp.bfloat16)


def whole(n, space=pltpu.VMEM):
    return [pl.BlockSpec(memory_space=space)] * n


def energy_kernel(x_ref, table_ref, out_ref, flat_ref):
    chans = x_ref.shape[0]
    frames = x_ref.shape[1] // WIN
    table = table_ref[...]
    group = 16
    for g in range(frames // group):
        x = jnp.concatenate(
            [x_ref[:, (g * group + f) * WIN : (g * group + f + 1) * WIN] for f in range(group)], axis=0
        )
        spec = jnp.dot(x, table, preferred_element_type=jnp.float32)
        re, im = spec[:, :BINS], spec[:, BINS:]
        flat_ref[g * group * chans : (g + 1) * group * chans, :] = re * re + im * im
    for c in range(chans):
        zl, y, core, j = c // 16, (c // 4) % 4, (c // 2) % 2, c % 2
        at = (y * 2 + j) * BINS
        out_ref[core, zl, 0, :, at : at + BINS] = flat_ref[pl.ds(c, frames, stride=chans), :].astype(jnp.bfloat16)


def energies(record, table):
    channels, samples = record.shape
    frames = samples // WIN
    per_row = channels // N_R
    rows = channels * BINS // (2 * N_P)
    return pl.pallas_call(
        energy_kernel,
        grid=(N_R,),
        in_specs=[
            pl.BlockSpec((per_row, samples), lambda r: (r, 0)),
            pl.BlockSpec((WIN, 2 * BINS), lambda r: (0, 0)),
        ],
        out_specs=pl.BlockSpec((2, 2, 1, frames, rows), lambda r: (0, 0, r, 0, 0)),
        out_shape=jax.ShapeDtypeStruct((2, 2, N_R, frames, rows), jnp.bfloat16),
        scratch_shapes=[pltpu.VMEM((frames * per_row, BINS), jnp.float32)],
        compiler_params=pltpu.CompilerParams(vmem_limit_bytes=58 << 20),
        cost_estimate=pl.CostEstimate(
            flops=2 * channels * frames * WIN * WIN, bytes_accessed=12 << 20, transcendentals=0
        ),
        name="energy",
    )(record, table)


def hi_lo(x, axis):
    hi = x.astype(jnp.bfloat16)
    lo = (x - hi.astype(jnp.float32)).astype(jnp.bfloat16)
    return jnp.where(lax.broadcasted_iota(jnp.int32, x.shape, axis) == 0, hi, lo)


def sweep_kernel(at_ref, s_ref, own_ref, oth_ref, w0, w1, w2, w3, n0, n1, n2, n3, hown_ref, hoth_ref, ht_ref):
    core, y = at_ref[0], at_ref[1]
    blocks, rank, half = own_ref.shape
    span = blocks * half
    h_refs, n_refs, out_refs = (own_ref, oth_ref), (n0, n1, n2, n3), (hown_ref, hoth_ref)
    for i, ref in enumerate(h_refs):
        for b in range(blocks):
            ht_ref[i, b * half : (b + 1) * half, :] = ref[b].T
    ones = jnp.ones((16, span), jnp.bfloat16)
    rowsum = jnp.dot(ones, ht_ref[0], preferred_element_type=jnp.float32)
    rowsum = rowsum + jnp.dot(ones, ht_ref[1], preferred_element_type=jnp.float32)
    colsum = jnp.zeros((rank, 1), jnp.float32)
    for p in range(2):
        wt = jnp.concatenate([w[...] for w in ((w0, w1), (w2, w3))[p]], axis=0).T
        colsum = colsum + jnp.sum(wt.astype(jnp.float32), axis=1, keepdims=True)
        wn = None
        for i in range(2):
            rows = pl.ds(pl.multiple_of((core if i == 0 else 1 - core) * span, span), span)
            columns = [
                pl.ds(pl.multiple_of(lax.rem(y + 2 * p + t, N_Y) * rank, rank), rank) for t in range(2)
            ]
            s = jnp.concatenate([s_ref[rows, c] for c in columns], axis=1)
            recon = jnp.dot(ht_ref[i], wt, preferred_element_type=jnp.float32)
            quotient = (s.astype(jnp.float32) / recon).astype(jnp.bfloat16)
            hn = lax.dot_general(wt, quotient, (((1,), (1,)), ((), ())), preferred_element_type=jnp.float32)
            if p == 0:
                out_refs[i][:, :span] = hn
            else:
                out_refs[i][:, :span] += hn
            for b in range(blocks):
                part = jnp.dot(
                    h_refs[i][b], quotient[b * half : (b + 1) * half], preferred_element_type=jnp.float32
                )
                wn = part if wn is None else wn + part
        for t in range(2):
            ref = n_refs[2 * p + t]
            ref[:rank, :] = wn[:, t * rank : (t + 1) * rank].astype(ref.dtype)
            if ref.dtype == jnp.float32:
                keep = lax.broadcasted_iota(jnp.int32, rowsum.shape, 0) == 0
                ref[rank:, :] = jnp.where(keep, rowsum, 0.0)
            else:
                ref[rank:, :] = hi_lo(rowsum, 0)
    for ref in out_refs:
        ref[:, span:] = jnp.broadcast_to(colsum, (rank, PAD))


def sweep(at, spectra, h_own, h_oth, ws):
    frames, rows = spectra.shape
    blocks, rank, half = h_own.shape
    part = (rank + 16, rank)
    sums = jax.ShapeDtypeStruct((rank, blocks * half + PAD), jnp.float32)
    return pl.pallas_call(
        sweep_kernel,
        in_specs=whole(1, pltpu.SMEM) + whole(7),
        out_specs=whole(6),
        out_shape=[jax.ShapeDtypeStruct(part, jnp.float32)]
        + [jax.ShapeDtypeStruct(part, jnp.bfloat16)] * 3
        + [sums, sums],
        scratch_shapes=[pltpu.VMEM((2, blocks * half, rank), jnp.bfloat16)],
        compiler_params=pltpu.CompilerParams(vmem_limit_bytes=32 << 20),
        cost_estimate=pl.CostEstimate(flops=6 * frames * rows * rank, bytes_accessed=8 << 20, transcendentals=0),
        name="sweep",
    )(at, spectra, h_own, h_oth, *ws)


def pair_kernel(a_ref, b_ref, out_ref):
    each, half = out_ref.shape[1], out_ref.shape[2] - PAD
    span = a_ref.shape[1] - PAD
    total = a_ref[...] + b_ref[...]
    sums = hi_lo(total[:, span:], 1)
    for zl in range(2):
        part = total[:, zl * half : (zl + 1) * half].astype(jnp.bfloat16)
        for r in range(N_R):
            out_ref[zl * N_R + r, :, :half] = part[r * each : (r + 1) * each, :]
            out_ref[zl * N_R + r, :, half:] = sums[r * each : (r + 1) * each, :]


def pair(a, b, each, half):
    return pl.pallas_call(
        pair_kernel,
        in_specs=whole(2),
        out_specs=whole(1)[0],
        out_shape=jax.ShapeDtypeStruct((N_P, each, half + PAD), jnp.bfloat16),
        compiler_params=pltpu.CompilerParams(vmem_limit_bytes=12 << 20),
        name="pair",
    )(a, b)


def h_update_kernel(parts_ref, h_ref, new_ref, low_ref):
    half = h_ref.shape[1]
    total = parts_ref[0].astype(jnp.float32)
    for i in range(1, N_P):
        total = total + parts_ref[i].astype(jnp.float32)
    colsum = total[:, half : half + 1] + total[:, half + 1 : half + 2]
    new = h_ref[...] * total[:, :half] / colsum
    new_ref[...] = new
    low = new.astype(jnp.bfloat16)
    for i in range(N_P):
        low_ref[i] = low


def h_update(parts, h):
    return pl.pallas_call(
        h_update_kernel,
        in_specs=whole(2),
        out_specs=whole(2),
        out_shape=[jax.ShapeDtypeStruct(h.shape, jnp.float32), jax.ShapeDtypeStruct((N_P, *h.shape), jnp.bfloat16)],
        compiler_params=pltpu.CompilerParams(vmem_limit_bytes=12 << 20),
        name="h_update",
    )(parts, h)


def w_update_kernel(p0, p1, p2, p3, w_ref, new_ref, low_ref):
    rank = w_ref.shape[1]
    total = p0[...] + p1[...].astype(jnp.float32) + p2[...].astype(jnp.float32) + p3[...].astype(jnp.float32)
    rowsum = total[rank : rank + 1, :] + total[rank + 1 : rank + 2, :]
    new = w_ref[...] * total[:rank, :].T / rowsum
    new_ref[...] = new
    low_ref[...] = new.astype(jnp.bfloat16)


def w_update(parts, w):
    return pl.pallas_call(
        w_update_kernel,
        in_specs=whole(5),
        out_specs=whole(2),
        out_shape=[jax.ShapeDtypeStruct(w.shape, jnp.float32), jax.ShapeDtypeStruct(w.shape, jnp.bfloat16)],
        compiler_params=pltpu.CompilerParams(vmem_limit_bytes=12 << 20),
        name="w_update",
    )(*parts, w)


def exchange(x, axes):
    return lax.all_to_all(x, axes, 0, 0, tiled=True)


def from_sibling(x):
    return lax.ppermute(x, "core", [(0, 1), (1, 0)])


def sent_ahead(x, t):
    return lax.ppermute(x, "y", [(i, (i + t) % N_Y) for i in range(N_Y)])


def taken_ahead(x):
    return [x] + [lax.ppermute(x, "y", [(i, (i - t) % N_Y) for i in range(N_Y)]) for t in range(1, N_Y)]


def gathered(low, rank):
    own = exchange(low, RANKS).reshape(2, rank, -1)
    return own, from_sibling(own)


def local(samples, w, h):
    rank = w.shape[1]
    record = samples.reshape(samples.shape[2], samples.shape[3])
    at = jnp.stack([lax.axis_index("core"), lax.axis_index("y")]).astype(jnp.int32)
    h_own, h_oth = gathered(jnp.broadcast_to(h.astype(jnp.bfloat16)[None], (N_P, *h.shape)), rank)
    energy = energies(record, dft_table())
    frames, rows = energy.shape[3:]
    energy, w_low = lax.optimization_barrier((energy, w.astype(jnp.bfloat16)))
    ws = taken_ahead(w_low)
    spectra = exchange(energy.reshape(2 * N_P, frames, rows), TILE).reshape(2 * N_P * frames, rows)
    for step in range(ITERS):
        n0, n1, n2, n3, s_own, s_oth = sweep(at, spectra, h_own, h_oth, ws)
        s_own = pair(s_own, from_sibling(s_oth), *h.shape)
        h_parts = exchange(s_own, RANKS)
        w_parts = [n0] + [sent_ahead(n, t + 1) for t, n in enumerate((n1, n2, n3))]
        h, low = h_update(h_parts, h)
        w, w_low = w_update(w_parts, w)
        if step + 1 < ITERS:
            h_own, h_oth = gathered(low, rank)
            ws = taken_ahead(w_low)
    return (w, h)


def solution(mesh):
    fine = Mesh(mesh.devices.reshape(SIZES), AXES)
    row, col = ("zh", "x"), ("zl", "y", "core")
    return jax.shard_map(
        local,
        mesh=fine,
        in_specs=(P(col, row, None, None), P(row + col, None), P(row, col)),
        out_specs=(P(row + col, None), P(row, col)),
        check_vma=False,
    )
```

```python
import math

import jax
import jax.numpy as jnp
import numpy as np
from jax import lax
from jax.experimental import pallas as pl
from jax.experimental.pallas import tpu as pltpu
from jax.sharding import Mesh
from jax.sharding import PartitionSpec as P

BINS = 128
ITERS = 2
WIN = 256

AXES = ("zh", "x", "zl", "y", "core")
SIZES = (2, 4, 2, 4, 2)
TILE = ("core", "zl", "zh", "x")
RANKS = ("zl", "zh", "x")
N_Y = 4
N_R = 8
N_P = 16
PAD = 128


def dft_table():
    n = np.arange(WIN, dtype=np.int32)
    k = np.arange(BINS, dtype=np.int32)
    phases = (n[:, None] * k[None, :] % WIN).astype(np.float32) * np.float32(2.0 * math.pi / WIN)
    taper = np.float32(0.5) - np.float32(0.5) * np.cos(n.astype(np.float32) * np.float32(2.0 * math.pi / WIN))
    taper = (taper / np.float32(math.sqrt(3.0 * WIN / 8.0))).astype(np.float32)
    both = np.concatenate([taper[:, None] * np.cos(phases), -taper[:, None] * np.sin(phases)], axis=1)
    return jnp.asarray(both.astype(np.float32)).astype(jnp.bfloat16)


def whole(n, space=pltpu.VMEM):
    return [pl.BlockSpec(memory_space=space)] * n


def energy_kernel(x_hbm, table_ref, out_hbm, x_ref, out_ref, in_sem, out_sem):
    blocks, chans, samples = x_ref.shape
    frames = samples // WIN
    group = 16

    def fetch(r):
        return pltpu.make_async_copy(x_hbm.at[pl.ds(r * chans, chans), :], x_ref.at[r], in_sem.at[r])

    def put(r):
        return pltpu.make_async_copy(out_ref.at[r], out_hbm.at[:, :, r], out_sem.at[r])

    for r in range(blocks):
        fetch(r).start()
    table = table_ref[...]

    @pl.loop(0, blocks)
    def _(r):
        fetch(r).wait()
        for g in range(frames // group):
            x = jnp.concatenate(
                [x_ref[r, :, (g * group + f) * WIN : (g * group + f + 1) * WIN] for f in range(group)], axis=0
            )
            spec = jnp.dot(x, table, preferred_element_type=jnp.float32)
            re, im = spec[:, :BINS], spec[:, BINS:]
            energy = (re * re + im * im).reshape(group, chans, BINS)
            energy = pltpu.einshape("fcb->cfb", energy).astype(jnp.bfloat16)
            for c in range(chans):
                zl, y, core, j = c // 16, (c // 4) % 4, (c // 2) % 2, c % 2
                at = (y * 2 + j) * BINS
                out_ref[r, core, zl, g * group : (g + 1) * group, at : at + BINS] = energy[c]
        put(r).start()

    for r in range(blocks):
        put(r).wait()


def energies(record, table):
    channels, samples = record.shape
    frames = samples // WIN
    per_row = channels // N_R
    rows = channels * BINS // (2 * N_P)
    return pl.pallas_call(
        energy_kernel,
        in_specs=[pl.BlockSpec(memory_space=pl.ANY), pl.BlockSpec(memory_space=pltpu.VMEM)],
        out_specs=pl.BlockSpec(memory_space=pl.ANY),
        out_shape=jax.ShapeDtypeStruct((2, 2, N_R, frames, rows), jnp.bfloat16),
        scratch_shapes=[
            pltpu.VMEM((N_R, per_row, samples), jnp.bfloat16),
            pltpu.VMEM((N_R, 2, 2, frames, rows), jnp.bfloat16),
            pltpu.SemaphoreType.DMA((N_R,)),
            pltpu.SemaphoreType.DMA((N_R,)),
        ],
        compiler_params=pltpu.CompilerParams(vmem_limit_bytes=58 << 20),
        cost_estimate=pl.CostEstimate(
            flops=2 * channels * frames * WIN * WIN, bytes_accessed=12 << 20, transcendentals=0
        ),
        name="energy",
    )(record, table)


def hi_lo(x, axis):
    hi = x.astype(jnp.bfloat16)
    lo = (x - hi.astype(jnp.float32)).astype(jnp.bfloat16)
    return jnp.where(lax.broadcasted_iota(jnp.int32, x.shape, axis) == 0, hi, lo)


def sweep_kernel(at_ref, s_ref, own_ref, oth_ref, w0, w1, w2, w3, n0, n1, n2, n3, hown_ref, hoth_ref, ht_ref):
    core, y = at_ref[0], at_ref[1]
    blocks, rank, half = own_ref.shape
    span = blocks * half
    h_refs, n_refs, out_refs = (own_ref, oth_ref), (n0, n1, n2, n3), (hown_ref, hoth_ref)
    for i, ref in enumerate(h_refs):
        for b in range(blocks):
            ht_ref[i, b * half : (b + 1) * half, :] = ref[b].T
    ones = jnp.ones((8, span), jnp.bfloat16)
    rowsum = jnp.dot(ones, ht_ref[0], preferred_element_type=jnp.float32)
    rowsum = rowsum + jnp.dot(ones, ht_ref[1], preferred_element_type=jnp.float32)
    colsum = jnp.zeros((rank, 1), jnp.float32)
    for p in range(2):
        wt = jnp.concatenate([w[...] for w in ((w0, w1), (w2, w3))[p]], axis=0).T
        colsum = colsum + jnp.sum(wt.astype(jnp.float32), axis=1, keepdims=True)
        wn = None
        for i in range(2):
            rows = pl.ds(pl.multiple_of((core if i == 0 else 1 - core) * span, span), span)
            columns = [
                pl.ds(pl.multiple_of(lax.rem(y + 2 * p + t, N_Y) * rank, rank), rank) for t in range(2)
            ]
            s = jnp.concatenate([s_ref[rows, c] for c in columns], axis=1)
            recon = jnp.dot(ht_ref[i], wt, preferred_element_type=jnp.float32)
            quotient = (s.astype(jnp.float32) / recon).astype(jnp.bfloat16)
            hn = lax.dot_general(wt, quotient, (((1,), (1,)), ((), ())), preferred_element_type=jnp.float32)
            if p == 0:
                out_refs[i][:, :span] = hn
            else:
                out_refs[i][:, :span] += hn
            for b in range(blocks):
                part = jnp.dot(
                    h_refs[i][b], quotient[b * half : (b + 1) * half], preferred_element_type=jnp.float32
                )
                wn = part if wn is None else wn + part
        for t in range(2):
            ref = n_refs[2 * p + t]
            ref[:rank, :] = wn[:, t * rank : (t + 1) * rank]
            ref[rank:, :] = rowsum
    for ref in out_refs:
        ref[:, span:] = jnp.broadcast_to(colsum, (rank, PAD))


def sweep(at, spectra, h_own, h_oth, ws):
    frames, rows = spectra.shape
    blocks, rank, half = h_own.shape
    part = (rank + 8, rank)
    sums = jax.ShapeDtypeStruct((rank, blocks * half + PAD), jnp.float32)
    return pl.pallas_call(
        sweep_kernel,
        in_specs=whole(1, pltpu.SMEM) + whole(7),
        out_specs=whole(6),
        out_shape=[jax.ShapeDtypeStruct(part, jnp.float32)] * 4 + [sums, sums],
        scratch_shapes=[pltpu.VMEM((2, blocks * half, rank), jnp.bfloat16)],
        compiler_params=pltpu.CompilerParams(vmem_limit_bytes=32 << 20),
        cost_estimate=pl.CostEstimate(flops=6 * frames * rows * rank, bytes_accessed=8 << 20, transcendentals=0),
        name="sweep",
    )(at, spectra, h_own, h_oth, *ws)


def pair_kernel(a_ref, b_ref, out_ref):
    each, half = out_ref.shape[1], out_ref.shape[2] - PAD
    span = a_ref.shape[1] - PAD
    total = a_ref[...] + b_ref[...]
    sums = hi_lo(total[:, span:], 1)
    for zl in range(2):
        part = total[:, zl * half : (zl + 1) * half].astype(jnp.bfloat16)
        for r in range(N_R):
            out_ref[zl * N_R + r, :, :half] = part[r * each : (r + 1) * each, :]
            out_ref[zl * N_R + r, :, half:] = sums[r * each : (r + 1) * each, :]


def pair(a, b, each, half):
    return pl.pallas_call(
        pair_kernel,
        in_specs=whole(2),
        out_specs=whole(1)[0],
        out_shape=jax.ShapeDtypeStruct((N_P, each, half + PAD), jnp.bfloat16),
        compiler_params=pltpu.CompilerParams(vmem_limit_bytes=12 << 20),
        name="pair",
    )(a, b)


def h_update_kernel(parts_ref, h_ref, new_ref, low_ref):
    half = h_ref.shape[1]
    total = parts_ref[0].astype(jnp.float32)
    for i in range(1, N_P):
        total = total + parts_ref[i].astype(jnp.float32)
    colsum = total[:, half : half + 1] + total[:, half + 1 : half + 2]
    new = h_ref[...] * total[:, :half] / colsum
    new_ref[...] = new
    low = new.astype(jnp.bfloat16)
    for i in range(N_P):
        low_ref[i] = low


def h_update(parts, h):
    return pl.pallas_call(
        h_update_kernel,
        in_specs=whole(2),
        out_specs=whole(2),
        out_shape=[jax.ShapeDtypeStruct(h.shape, jnp.float32), jax.ShapeDtypeStruct((N_P, *h.shape), jnp.bfloat16)],
        compiler_params=pltpu.CompilerParams(vmem_limit_bytes=12 << 20),
        name="h_update",
    )(parts, h)


def w_update_kernel(p0, p1, p2, p3, w_ref, new_ref, low_ref):
    rank = w_ref.shape[1]
    total = (p0[...] + p1[...]) + (p2[...] + p3[...])
    new = w_ref[...] * total[:rank, :].T / total[rank : rank + 1, :]
    new_ref[...] = new
    low_ref[...] = new.astype(jnp.bfloat16)


def w_update(parts, w):
    return pl.pallas_call(
        w_update_kernel,
        in_specs=whole(5),
        out_specs=whole(2),
        out_shape=[jax.ShapeDtypeStruct(w.shape, jnp.float32), jax.ShapeDtypeStruct(w.shape, jnp.bfloat16)],
        compiler_params=pltpu.CompilerParams(vmem_limit_bytes=12 << 20),
        name="w_update",
    )(*parts, w)


def exchange(x, axes):
    return lax.all_to_all(x, axes, 0, 0, tiled=True)


def from_sibling(x):
    return lax.ppermute(x, "core", [(0, 1), (1, 0)])


def sent_ahead(x, t):
    return lax.ppermute(x, "y", [(i, (i + t) % N_Y) for i in range(N_Y)])


def taken_ahead(x):
    return [x] + [lax.ppermute(x, "y", [(i, (i - t) % N_Y) for i in range(N_Y)]) for t in range(1, N_Y)]


def local(samples, w, h):
    rank = w.shape[1]
    record = samples.reshape(samples.shape[2], samples.shape[3])
    at = jnp.stack([lax.axis_index("core"), lax.axis_index("y")]).astype(jnp.int32)
    h_own = exchange(jnp.broadcast_to(h.astype(jnp.bfloat16)[None], (N_P, *h.shape)), RANKS)
    energy = energies(record, dft_table())
    frames, rows = energy.shape[3:]
    energy, w_low = lax.optimization_barrier((energy, w.astype(jnp.bfloat16)))
    ws = taken_ahead(w_low)
    h_own = h_own.reshape(2, rank, -1)
    h_oth = from_sibling(h_own)
    spectra = exchange(energy.reshape(2 * N_P, frames, rows), TILE).reshape(2 * N_P * frames, rows)
    for step in range(ITERS):
        n0, n1, n2, n3, s_own, s_oth = sweep(at, spectra, h_own, h_oth, ws)
        w_parts = [n0] + [sent_ahead(n, t + 1) for t, n in enumerate((n1, n2, n3))]
        h_parts = exchange(pair(s_own, from_sibling(s_oth), *h.shape), RANKS)
        w_parts, h_parts = lax.optimization_barrier((w_parts, h_parts))
        h, low = h_update(h_parts, h)
        w, w_low = w_update(w_parts, w)
        if step + 1 < ITERS:
            ws = taken_ahead(w_low)
            ws, h_own = lax.optimization_barrier((ws, exchange(low, RANKS)))
            h_own = h_own.reshape(2, rank, -1)
            h_oth = from_sibling(h_own)
    return (w, h)


def solution(mesh):
    fine = Mesh(mesh.devices.reshape(SIZES), AXES)
    row, col = ("zh", "x"), ("zl", "y", "core")
    return jax.shard_map(
        local,
        mesh=fine,
        in_specs=(P(col, row, None, None), P(row + col, None), P(row, col)),
        out_specs=(P(row + col, None), P(row, col)),
        check_vma=False,
    )
```

```python
import functools
import math

import jax
import jax.numpy as jnp
import numpy as np
from jax import lax
from jax.experimental import pallas as pl
from jax.experimental.pallas import tpu as pltpu
from jax.sharding import Mesh
from jax.sharding import PartitionSpec as P

BINS = 128
ITERS = 2
WIN = 256

AXES = ("zh", "x", "zl", "y", "core")
SIZES = (2, 4, 2, 4, 2)
TILE = ("core", "zl", "zh", "x")
RANKS = ("zl", "zh", "x")
N_Y = 4
N_R = 8
N_P = 16
PAD = 128


def dft_table():
    n = np.arange(WIN, dtype=np.int32)
    k = np.arange(BINS, dtype=np.int32)
    phases = (n[:, None] * k[None, :] % WIN).astype(np.float32) * np.float32(2.0 * math.pi / WIN)
    taper = np.float32(0.5) - np.float32(0.5) * np.cos(n.astype(np.float32) * np.float32(2.0 * math.pi / WIN))
    taper = (taper / np.float32(math.sqrt(3.0 * WIN / 8.0))).astype(np.float32)
    both = np.concatenate([taper[:, None] * np.cos(phases), -taper[:, None] * np.sin(phases)], axis=1)
    return jnp.asarray(both.astype(np.float32)).astype(jnp.bfloat16)


def whole(n, space=pltpu.VMEM):
    return [pl.BlockSpec(memory_space=space)] * n


def energy_kernel(x_hbm, table_ref, out_hbm, x_ref, out_ref, in_sem, out_sem):
    blocks, chans, samples = x_ref.shape
    frames = samples // WIN
    group = 16

    def fetch(r):
        return pltpu.make_async_copy(x_hbm.at[pl.ds(r * chans, chans), :], x_ref.at[r], in_sem.at[r])

    def put(r):
        return pltpu.make_async_copy(out_ref.at[r], out_hbm.at[:, :, r], out_sem.at[r])

    for r in range(blocks):
        fetch(r).start()
    table = table_ref[...]

    @pl.loop(0, blocks)
    def _(r):
        fetch(r).wait()
        for g in range(frames // group):
            x = jnp.concatenate(
                [x_ref[r, :, (g * group + f) * WIN : (g * group + f + 1) * WIN] for f in range(group)], axis=0
            )
            spec = jnp.dot(x, table, preferred_element_type=jnp.float32)
            re, im = spec[:, :BINS], spec[:, BINS:]
            energy = (re * re + im * im).reshape(group, chans, BINS)
            energy = pltpu.einshape("fcb->cfb", energy).astype(jnp.bfloat16)
            for c in range(chans):
                zl, y, core, j = c // 16, (c // 4) % 4, (c // 2) % 2, c % 2
                at = (y * 2 + j) * BINS
                out_ref[r, core, zl, g * group : (g + 1) * group, at : at + BINS] = energy[c]
        put(r).start()

    for r in range(blocks):
        put(r).wait()


def energies(record, table):
    channels, samples = record.shape
    frames = samples // WIN
    per_row = channels // N_R
    rows = channels * BINS // (2 * N_P)
    return pl.pallas_call(
        energy_kernel,
        in_specs=[pl.BlockSpec(memory_space=pl.ANY), pl.BlockSpec(memory_space=pltpu.VMEM)],
        out_specs=pl.BlockSpec(memory_space=pl.ANY),
        out_shape=jax.ShapeDtypeStruct((2, 2, N_R, frames, rows), jnp.bfloat16),
        scratch_shapes=[
            pltpu.VMEM((N_R, per_row, samples), jnp.bfloat16),
            pltpu.VMEM((N_R, 2, 2, frames, rows), jnp.bfloat16),
            pltpu.SemaphoreType.DMA((N_R,)),
            pltpu.SemaphoreType.DMA((N_R,)),
        ],
        compiler_params=pltpu.CompilerParams(vmem_limit_bytes=58 << 20),
        cost_estimate=pl.CostEstimate(
            flops=2 * channels * frames * WIN * WIN, bytes_accessed=12 << 20, transcendentals=0
        ),
        name="energy",
    )(record, table)


def hi_lo(x, axis):
    hi = x.astype(jnp.bfloat16)
    lo = (x - hi.astype(jnp.float32)).astype(jnp.bfloat16)
    return jnp.where(lax.broadcasted_iota(jnp.int32, x.shape, axis) == 0, hi, lo)


def sweep_kernel(first, at_ref, s_ref, h_ref, w0, w1, w2, w3, *refs):
    before, (n0, n1, n2, n3, sums_ref, ht_ref) = (() if first else refs[:4]), refs[-6:]
    blocks, rank, half = h_ref.shape
    span = blocks * half
    for b in range(blocks):
        ht_ref[b * half : (b + 1) * half, :] = h_ref[b].T
    rowsum = jnp.dot(jnp.ones((8, span), jnp.bfloat16), ht_ref[...], preferred_element_type=jnp.float32)
    colsum = jnp.zeros((rank, 1), jnp.float32)
    rows = pl.ds(pl.multiple_of(at_ref[0 if first else 1] * span, span), span)
    for p in range(2):
        wt = jnp.concatenate([w[...] for w in ((w0, w1), (w2, w3))[p]], axis=0).T
        colsum = colsum + jnp.sum(wt.astype(jnp.float32), axis=1, keepdims=True)
        columns = [
            pl.ds(pl.multiple_of(lax.rem(at_ref[2] + 2 * p + t, N_Y) * rank, rank), rank) for t in range(2)
        ]
        s = jnp.concatenate([s_ref[rows, c] for c in columns], axis=1)
        recon = jnp.dot(ht_ref[...], wt, preferred_element_type=jnp.float32)
        quotient = (s.astype(jnp.float32) / recon).astype(jnp.bfloat16)
        hn = lax.dot_general(wt, quotient, (((1,), (1,)), ((), ())), preferred_element_type=jnp.float32)
        if p == 0:
            sums_ref[:, :span] = hn
        else:
            sums_ref[:, :span] += hn
        wn = None
        for b in range(blocks):
            part = jnp.dot(h_ref[b], quotient[b * half : (b + 1) * half], preferred_element_type=jnp.float32)
            wn = part if wn is None else wn + part
        for t in range(2):
            ref = (n0, n1, n2, n3)[2 * p + t]
            part = wn[:, t * rank : (t + 1) * rank]
            if first:
                ref[:rank, :] = part
                ref[rank:, :] = rowsum
            else:
                ref[:rank, :] = part + before[2 * p + t][:rank, :]
                ref[rank:, :] = rowsum + before[2 * p + t][rank:, :]
    sums_ref[:, span:] = jnp.broadcast_to(colsum, (rank, PAD))


def half_sweep(at, spectra, h, ws, before=()):
    frames, rows = spectra.shape
    blocks, rank, half = h.shape
    return pl.pallas_call(
        functools.partial(sweep_kernel, not before),
        in_specs=whole(1, pltpu.SMEM) + whole(6 + len(before)),
        out_specs=whole(5),
        out_shape=[jax.ShapeDtypeStruct((rank + 8, rank), jnp.float32)] * 4
        + [jax.ShapeDtypeStruct((rank, blocks * half + PAD), jnp.float32)],
        scratch_shapes=[pltpu.VMEM((blocks * half, rank), jnp.bfloat16)],
        compiler_params=pltpu.CompilerParams(vmem_limit_bytes=28 << 20),
        cost_estimate=pl.CostEstimate(flops=3 * frames * rows * rank, bytes_accessed=4 << 20, transcendentals=0),
        name="sweep_a" if not before else "sweep_b",
    )(at, spectra, h, *ws, *before)


def pair_kernel(a_ref, b_ref, out_ref):
    each, half = out_ref.shape[1], out_ref.shape[2] - PAD
    span = a_ref.shape[1] - PAD
    total = a_ref[...] + b_ref[...]
    sums = hi_lo(total[:, span:], 1)
    for zl in range(2):
        part = total[:, zl * half : (zl + 1) * half].astype(jnp.bfloat16)
        for r in range(N_R):
            out_ref[zl * N_R + r, :, :half] = part[r * each : (r + 1) * each, :]
            out_ref[zl * N_R + r, :, half:] = sums[r * each : (r + 1) * each, :]


def pair(a, b, each, half):
    return pl.pallas_call(
        pair_kernel,
        in_specs=whole(2),
        out_specs=whole(1)[0],
        out_shape=jax.ShapeDtypeStruct((N_P, each, half + PAD), jnp.bfloat16),
        compiler_params=pltpu.CompilerParams(vmem_limit_bytes=12 << 20),
        name="pair",
    )(a, b)


def h_update_kernel(parts_ref, h_ref, new_ref, low_ref):
    half = h_ref.shape[1]
    total = parts_ref[0].astype(jnp.float32)
    for i in range(1, N_P):
        total = total + parts_ref[i].astype(jnp.float32)
    colsum = total[:, half : half + 1] + total[:, half + 1 : half + 2]
    new = h_ref[...] * total[:, :half] / colsum
    new_ref[...] = new
    low = new.astype(jnp.bfloat16)
    for i in range(N_P):
        low_ref[i] = low


def h_update(parts, h):
    return pl.pallas_call(
        h_update_kernel,
        in_specs=whole(2),
        out_specs=whole(2),
        out_shape=[jax.ShapeDtypeStruct(h.shape, jnp.float32), jax.ShapeDtypeStruct((N_P, *h.shape), jnp.bfloat16)],
        compiler_params=pltpu.CompilerParams(vmem_limit_bytes=12 << 20),
        name="h_update",
    )(parts, h)


def w_update_kernel(p0, p1, p2, p3, w_ref, new_ref, low_ref):
    rank = w_ref.shape[1]
    total = (p0[...] + p1[...]) + (p2[...] + p3[...])
    new = w_ref[...] * total[:rank, :].T / total[rank : rank + 1, :]
    new_ref[...] = new
    low_ref[...] = new.astype(jnp.bfloat16)


def w_update(parts, w):
    return pl.pallas_call(
        w_update_kernel,
        in_specs=whole(5),
        out_specs=whole(2),
        out_shape=[jax.ShapeDtypeStruct(w.shape, jnp.float32), jax.ShapeDtypeStruct(w.shape, jnp.bfloat16)],
        compiler_params=pltpu.CompilerParams(vmem_limit_bytes=12 << 20),
        name="w_update",
    )(*parts, w)


def exchange(x, axes):
    return lax.all_to_all(x, axes, 0, 0, tiled=True)


def from_sibling(x):
    return lax.ppermute(x, "core", [(0, 1), (1, 0)])


def sent_ahead(x, t):
    return lax.ppermute(x, "y", [(i, (i + t) % N_Y) for i in range(N_Y)])


def taken_ahead(x):
    return [x] + [lax.ppermute(x, "y", [(i, (i - t) % N_Y) for i in range(N_Y)]) for t in range(1, N_Y)]


def local(samples, w, h):
    rank = w.shape[1]
    record = samples.reshape(samples.shape[2], samples.shape[3])
    core, y = lax.axis_index("core"), lax.axis_index("y")
    at = jnp.stack([1 - core, core, y]).astype(jnp.int32)
    h_all = lax.all_gather(h.astype(jnp.bfloat16), ("zh", "x", "zl", "core"), axis=0, tiled=False)
    energy = energies(record, dft_table())
    frames, rows = energy.shape[3:]
    energy, w_low = lax.optimization_barrier((energy, w.astype(jnp.bfloat16)))
    ws = taken_ahead(w_low)
    h_all = h_all.reshape(N_R, 2, 2, *h.shape)
    h_oth, h_own = [
        lax.dynamic_index_in_dim(h_all, c, 2, keepdims=False).swapaxes(0, 1).reshape(2, rank, -1)
        for c in (1 - core, core)
    ]
    spectra = exchange(energy.reshape(2 * N_P, frames, rows), TILE).reshape(2 * N_P * frames, rows)
    for step in range(ITERS):
        *parts, s_oth = half_sweep(at, spectra, h_oth, ws)
        s_got = from_sibling(s_oth)
        n0, n1, n2, n3, s_own = half_sweep(at, spectra, h_own, ws, parts)
        w_parts = [n0] + [sent_ahead(n, t + 1) for t, n in enumerate((n1, n2, n3))]
        h_parts = exchange(pair(s_own, s_got, *h.shape), RANKS)
        w_parts, h_parts = lax.optimization_barrier((w_parts, h_parts))
        h, low = h_update(h_parts, h)
        w, w_low = w_update(w_parts, w)
        if step + 1 < ITERS:
            ws = taken_ahead(w_low)
            ws, h_own = lax.optimization_barrier((ws, exchange(low, RANKS)))
            h_own = h_own.reshape(2, rank, -1)
            h_oth = from_sibling(h_own)
    return (w, h)


def solution(mesh):
    fine = Mesh(mesh.devices.reshape(SIZES), AXES)
    row, col = ("zh", "x"), ("zl", "y", "core")
    return jax.shard_map(
        local,
        mesh=fine,
        in_specs=(P(col, row, None, None), P(row + col, None), P(row, col)),
        out_specs=(P(row + col, None), P(row, col)),
        check_vma=False,
    )
```

```python
import functools
import math

import jax
import jax.numpy as jnp
import numpy as np
from jax import lax
from jax.experimental import pallas as pl
from jax.experimental.pallas import tpu as pltpu
from jax.sharding import Mesh
from jax.sharding import PartitionSpec as P

BINS = 128
ITERS = 2
WIN = 256

AXES = ("zh", "x", "zl", "y", "core")
SIZES = (2, 4, 2, 4, 2)
TILE = ("zh", "zl", "core", "x")
RANKS = ("zl", "zh", "x")
N_Y = 4
N_R = 8
N_P = 16
PAD = 128


def dft_table():
    n = np.arange(WIN, dtype=np.int32)
    k = np.arange(BINS, dtype=np.int32)
    phases = (n[:, None] * k[None, :] % WIN).astype(np.float32) * np.float32(2.0 * math.pi / WIN)
    taper = np.float32(0.5) - np.float32(0.5) * np.cos(n.astype(np.float32) * np.float32(2.0 * math.pi / WIN))
    taper = (taper / np.float32(math.sqrt(3.0 * WIN / 8.0))).astype(np.float32)
    both = np.concatenate([taper[:, None] * np.cos(phases), -taper[:, None] * np.sin(phases)], axis=1)
    return jnp.asarray(both.astype(np.float32)).astype(jnp.bfloat16)


def whole(n, space=pltpu.VMEM):
    return [pl.BlockSpec(memory_space=space)] * n


def energy_kernel(x_hbm, table_ref, out_hbm, x_ref, out_ref, in_sem, out_sem):
    blocks, chans, samples = x_ref.shape
    frames = samples // WIN
    group = 16

    def fetch(r):
        return pltpu.make_async_copy(x_hbm.at[pl.ds(r * chans, chans), :], x_ref.at[r], in_sem.at[r])

    def put(r):
        return pltpu.make_async_copy(out_ref.at[r], out_hbm.at[r // 4, :, :, r % 4], out_sem.at[r])

    for r in range(blocks):
        fetch(r).start()
    table = table_ref[...]

    @pl.loop(0, blocks)
    def _(r):
        fetch(r).wait()
        for g in range(frames // group):
            x = jnp.concatenate(
                [x_ref[r, :, (g * group + f) * WIN : (g * group + f + 1) * WIN] for f in range(group)], axis=0
            )
            spec = jnp.dot(x, table, preferred_element_type=jnp.float32)
            re, im = spec[:, :BINS], spec[:, BINS:]
            energy = (re * re + im * im).reshape(group, chans, BINS)
            energy = pltpu.einshape("fcb->cfb", energy).astype(jnp.bfloat16)
            for c in range(chans):
                zl, y, core, j = c // 16, (c // 4) % 4, (c // 2) % 2, c % 2
                at = (y * 2 + j) * BINS
                out_ref[r, zl, core, g * group : (g + 1) * group, at : at + BINS] = energy[c]
        put(r).start()

    for r in range(blocks):
        put(r).wait()


def energies(record, table):
    channels, samples = record.shape
    frames = samples // WIN
    per_row = channels // N_R
    rows = channels * BINS // (2 * N_P)
    return pl.pallas_call(
        energy_kernel,
        in_specs=[pl.BlockSpec(memory_space=pl.ANY), pl.BlockSpec(memory_space=pltpu.VMEM)],
        out_specs=pl.BlockSpec(memory_space=pl.ANY),
        out_shape=jax.ShapeDtypeStruct((2, 2, 2, 4, frames, rows), jnp.bfloat16),
        scratch_shapes=[
            pltpu.VMEM((N_R, per_row, samples), jnp.bfloat16),
            pltpu.VMEM((N_R, 2, 2, frames, rows), jnp.bfloat16),
            pltpu.SemaphoreType.DMA((N_R,)),
            pltpu.SemaphoreType.DMA((N_R,)),
        ],
        compiler_params=pltpu.CompilerParams(vmem_limit_bytes=58 << 20),
        cost_estimate=pl.CostEstimate(
            flops=2 * channels * frames * WIN * WIN, bytes_accessed=12 << 20, transcendentals=0
        ),
        name="energy",
    )(record, table)


def sweep_kernel(first, at_ref, s_ref, h_ref, w0, w1, w2, w3, *refs):
    before, (n0, n1, n2, n3, sums_ref, ht_ref) = (() if first else refs[:4]), refs[-6:]
    blocks, rank, half = h_ref.shape
    span = blocks * half
    for b in range(blocks):
        ht_ref[b * half : (b + 1) * half, :] = h_ref[b].T
    rowsum = jnp.dot(jnp.ones((8, span), jnp.bfloat16), ht_ref[...], preferred_element_type=jnp.float32)
    colsum = jnp.zeros((rank, 1), jnp.float32)
    run = half // 2
    core = at_ref[0 if first else 1]
    rows = [
        pl.ds(pl.multiple_of(((zh * blocks + b) * 2 + core) * run, run), run) for b in range(blocks) for zh in range(2)
    ]
    for p in range(2):
        wt = jnp.concatenate([w[...] for w in ((w0, w1), (w2, w3))[p]], axis=0).T
        colsum = colsum + jnp.sum(wt.astype(jnp.float32), axis=1, keepdims=True)
        columns = [
            pl.ds(pl.multiple_of(lax.rem(at_ref[2] + 2 * p + t, N_Y) * rank, rank), rank) for t in range(2)
        ]
        s = jnp.concatenate([jnp.concatenate([s_ref[r, c] for c in columns], axis=1) for r in rows], axis=0)
        recon = jnp.dot(ht_ref[...], wt, preferred_element_type=jnp.float32)
        quotient = (s.astype(jnp.float32) / recon).astype(jnp.bfloat16)
        hn = lax.dot_general(wt, quotient, (((1,), (1,)), ((), ())), preferred_element_type=jnp.float32)
        if p == 0:
            sums_ref[:, :span] = hn
        else:
            sums_ref[:, :span] += hn
        wn = None
        for b in range(blocks):
            part = jnp.dot(h_ref[b], quotient[b * half : (b + 1) * half], preferred_element_type=jnp.float32)
            wn = part if wn is None else wn + part
        for t in range(2):
            ref = (n0, n1, n2, n3)[2 * p + t]
            part = wn[:, t * rank : (t + 1) * rank]
            if first:
                ref[:rank, :] = part
                ref[rank:, :] = rowsum
            else:
                ref[:rank, :] = part + before[2 * p + t][:rank, :]
                ref[rank:, :] = rowsum + before[2 * p + t][rank:, :]
    sums_ref[:, span:] = jnp.broadcast_to(colsum, (rank, PAD))


def half_sweep(at, spectra, h, ws, before=()):
    frames, rows = spectra.shape
    blocks, rank, half = h.shape
    return pl.pallas_call(
        functools.partial(sweep_kernel, not before),
        in_specs=whole(1, pltpu.SMEM) + whole(6 + len(before)),
        out_specs=whole(5),
        out_shape=[jax.ShapeDtypeStruct((rank + 8, rank), jnp.float32)] * 4
        + [jax.ShapeDtypeStruct((rank, blocks * half + PAD), jnp.float32)],
        scratch_shapes=[pltpu.VMEM((blocks * half, rank), jnp.bfloat16)],
        compiler_params=pltpu.CompilerParams(vmem_limit_bytes=28 << 20),
        cost_estimate=pl.CostEstimate(flops=3 * frames * rows * rank, bytes_accessed=4 << 20, transcendentals=0),
        name="sweep_a" if not before else "sweep_b",
    )(at, spectra, h, *ws, *before)


def pair_kernel(a_ref, b_ref, out_ref):
    each, half = out_ref.shape[1], out_ref.shape[2] - PAD
    span = a_ref.shape[1] - PAD
    for r in range(N_R):
        rows = slice(r * each, (r + 1) * each)
        sums = a_ref[rows, span:] + b_ref[rows, span:]
        for zl in range(2):
            columns = slice(zl * half, (zl + 1) * half)
            out_ref[zl * N_R + r, :, :half] = a_ref[rows, columns] + b_ref[rows, columns]
            out_ref[zl * N_R + r, :, half:] = sums


def pair(a, b, each, half):
    return pl.pallas_call(
        pair_kernel,
        in_specs=whole(2),
        out_specs=whole(1)[0],
        out_shape=jax.ShapeDtypeStruct((N_P, each, half + PAD), jnp.float32),
        compiler_params=pltpu.CompilerParams(vmem_limit_bytes=12 << 20),
        name="pair",
    )(a, b)


def h_update_kernel(parts_ref, h_ref, new_ref, low_ref):
    half = h_ref.shape[1]
    total = parts_ref[0]
    for i in range(1, N_P):
        total = total + parts_ref[i]
    new = h_ref[...] * total[:, :half] / total[:, half : half + 1]
    new_ref[...] = new
    low = new.astype(jnp.bfloat16)
    for i in range(N_P):
        low_ref[i] = low


def h_update(parts, h):
    return pl.pallas_call(
        h_update_kernel,
        in_specs=whole(2),
        out_specs=whole(2),
        out_shape=[jax.ShapeDtypeStruct(h.shape, jnp.float32), jax.ShapeDtypeStruct((N_P, *h.shape), jnp.bfloat16)],
        compiler_params=pltpu.CompilerParams(vmem_limit_bytes=12 << 20),
        name="h_update",
    )(parts, h)


def w_update_kernel(p0, p1, p2, p3, w_ref, new_ref, low_ref):
    rank = w_ref.shape[1]
    total = (p0[...] + p1[...]) + (p2[...] + p3[...])
    new = w_ref[...] * total[:rank, :].T / total[rank : rank + 1, :]
    new_ref[...] = new
    low_ref[...] = new.astype(jnp.bfloat16)


def w_update(parts, w):
    return pl.pallas_call(
        w_update_kernel,
        in_specs=whole(5),
        out_specs=whole(2),
        out_shape=[jax.ShapeDtypeStruct(w.shape, jnp.float32), jax.ShapeDtypeStruct(w.shape, jnp.bfloat16)],
        compiler_params=pltpu.CompilerParams(vmem_limit_bytes=12 << 20),
        name="w_update",
    )(*parts, w)


def spread_kernel(h_ref, low_ref):
    low = h_ref[...].astype(jnp.bfloat16)
    for i in range(N_P):
        low_ref[i] = low


def spread(h):
    return pl.pallas_call(
        spread_kernel,
        in_specs=whole(1),
        out_specs=whole(1)[0],
        out_shape=jax.ShapeDtypeStruct((N_P, *h.shape), jnp.bfloat16),
        compiler_params=pltpu.CompilerParams(vmem_limit_bytes=12 << 20),
        name="spread",
    )(h)


def exchange(x, axes):
    return lax.all_to_all(x, axes, 0, 0, tiled=True)


def from_sibling(x):
    return lax.ppermute(x, "core", [(0, 1), (1, 0)])


def sent_ahead(x, t):
    return lax.ppermute(x, "y", [(i, (i + t) % N_Y) for i in range(N_Y)])


def taken_ahead(x):
    return [x] + [lax.ppermute(x, "y", [(i, (i - t) % N_Y) for i in range(N_Y)]) for t in range(1, N_Y)]


def local(samples, w, h):
    rank = w.shape[1]
    record = samples.reshape(samples.shape[2], samples.shape[3])
    core, y = lax.axis_index("core"), lax.axis_index("y")
    at = jnp.stack([1 - core, core, y]).astype(jnp.int32)
    h_own = exchange(spread(h), RANKS)
    energy = energies(record, dft_table())
    frames, rows = energy.shape[4:]
    energy, w_low = lax.optimization_barrier((energy, w.astype(jnp.bfloat16)))
    ws = taken_ahead(w_low)
    h_own = h_own.reshape(2, rank, -1)
    h_oth = from_sibling(h_own)
    spectra = exchange(energy.reshape(2 * N_P, frames, rows), TILE).reshape(2 * N_P * frames, rows)
    for step in range(ITERS):
        *parts, s_oth = half_sweep(at, spectra, h_oth, ws)
        s_got = from_sibling(s_oth)
        n0, n1, n2, n3, s_own = half_sweep(at, spectra, h_own, ws, parts)
        w_parts = [n0] + [sent_ahead(n, t + 1) for t, n in enumerate((n1, n2, n3))]
        h_parts = exchange(pair(s_own, s_got, *h.shape), RANKS)
        h, low = h_update(h_parts, h)
        w_parts, low, h = lax.optimization_barrier((w_parts, low, h))
        w, w_low = w_update(w_parts, w)
        if step + 1 < ITERS:
            ws = taken_ahead(w_low)
            ws, h_own = lax.optimization_barrier((ws, exchange(low, RANKS)))
            h_own = h_own.reshape(2, rank, -1)
            h_oth = from_sibling(h_own)
    return (w, h)


def solution(mesh):
    fine = Mesh(mesh.devices.reshape(SIZES), AXES)
    row, col = ("zh", "x"), ("zl", "y", "core")
    return jax.shard_map(
        local,
        mesh=fine,
        in_specs=(P(col, row, None, None), P(row + col, None), P(row, col)),
        out_specs=(P(row + col, None), P(row, col)),
        check_vma=False,
    )
```

```python
import functools
import math

import jax
import jax.numpy as jnp
import numpy as np
from jax import lax
from jax.experimental import pallas as pl
from jax.experimental.pallas import tpu as pltpu
from jax.sharding import Mesh
from jax.sharding import PartitionSpec as P

BINS = 128
ITERS = 2
WIN = 256

AXES = ("zh", "x", "zl", "y", "core")
SIZES = (2, 4, 2, 4, 2)
TILE = ("zh", "zl", "core", "x")
RANKS = ("zl", "zh", "x")
N_Y = 4
N_R = 8
N_P = 16
LANES = 128
TAIL = 8


def dft_table():
    n = np.arange(WIN, dtype=np.int32)
    k = np.arange(BINS, dtype=np.int32)
    phases = (n[:, None] * k[None, :] % WIN).astype(np.float32) * np.float32(2.0 * math.pi / WIN)
    taper = np.float32(0.5) - np.float32(0.5) * np.cos(n.astype(np.float32) * np.float32(2.0 * math.pi / WIN))
    taper = (taper / np.float32(math.sqrt(3.0 * WIN / 8.0))).astype(np.float32)
    both = np.concatenate([taper[:, None] * np.cos(phases), -taper[:, None] * np.sin(phases)], axis=1)
    return jnp.asarray(both.astype(np.float32)).astype(jnp.bfloat16)


def whole(n, space=pltpu.VMEM):
    return [pl.BlockSpec(memory_space=space)] * n


def energy_kernel(x_hbm, table_ref, out_hbm, x_ref, out_ref, in_sem, out_sem):
    blocks, chans, samples = x_ref.shape
    frames = samples // WIN
    group = 16

    def fetch(r):
        return pltpu.make_async_copy(x_hbm.at[pl.ds(r * chans, chans), :], x_ref.at[r], in_sem.at[r])

    def put(r):
        return pltpu.make_async_copy(out_ref.at[r], out_hbm.at[r // 4, :, :, r % 4], out_sem.at[r])

    for r in range(blocks):
        fetch(r).start()
    table = table_ref[...]

    @pl.loop(0, blocks)
    def _(r):
        fetch(r).wait()
        for g in range(frames // group):
            x = jnp.concatenate(
                [x_ref[r, :, (g * group + f) * WIN : (g * group + f + 1) * WIN] for f in range(group)], axis=0
            )
            spec = jnp.dot(x, table, preferred_element_type=jnp.float32)
            re, im = spec[:, :BINS], spec[:, BINS:]
            energy = (re * re + im * im).reshape(group, chans, BINS)
            energy = pltpu.einshape("fcb->cfb", energy).astype(jnp.bfloat16)
            for c in range(chans):
                zl, y, core, j = c // 16, (c // 4) % 4, (c // 2) % 2, c % 2
                at = (y * 2 + j) * BINS
                out_ref[r, zl, core, g * group : (g + 1) * group, at : at + BINS] = energy[c]
        put(r).start()

    for r in range(blocks):
        put(r).wait()


def energies(record, table):
    channels, samples = record.shape
    frames = samples // WIN
    per_row = channels // N_R
    rows = channels * BINS // (2 * N_P)
    return pl.pallas_call(
        energy_kernel,
        in_specs=[pl.BlockSpec(memory_space=pl.ANY), pl.BlockSpec(memory_space=pltpu.VMEM)],
        out_specs=pl.BlockSpec(memory_space=pl.ANY),
        out_shape=jax.ShapeDtypeStruct((2, 2, 2, 4, frames, rows), jnp.bfloat16),
        scratch_shapes=[
            pltpu.VMEM((N_R, per_row, samples), jnp.bfloat16),
            pltpu.VMEM((N_R, 2, 2, frames, rows), jnp.bfloat16),
            pltpu.SemaphoreType.DMA((N_R,)),
            pltpu.SemaphoreType.DMA((N_R,)),
        ],
        compiler_params=pltpu.CompilerParams(vmem_limit_bytes=58 << 20),
        cost_estimate=pl.CostEstimate(
            flops=2 * channels * frames * WIN * WIN, bytes_accessed=12 << 20, transcendentals=0
        ),
        name="energy",
    )(record, table)


def sweep_kernel(first, at_ref, s_ref, h_ref, w0, w1, w2, w3, *refs):
    before, (n0, n1, n2, n3, sums_ref, ht_ref) = (() if first else refs[:4]), refs[-6:]
    blocks, rank, half = h_ref.shape
    span = blocks * half
    for b in range(blocks):
        ht_ref[b * half : (b + 1) * half, :] = h_ref[b].T
    rowsum = jnp.dot(jnp.ones((8, span), jnp.bfloat16), ht_ref[...], preferred_element_type=jnp.float32)
    colsum = jnp.zeros((rank, 1), jnp.float32)
    run = half // 2
    core = at_ref[0 if first else 1]
    rows = [
        pl.ds(pl.multiple_of(((zh * blocks + b) * 2 + core) * run, run), run) for b in range(blocks) for zh in range(2)
    ]
    for p in range(2):
        wt = jnp.concatenate([w[...] for w in ((w0, w1), (w2, w3))[p]], axis=0).T
        colsum = colsum + jnp.sum(wt.astype(jnp.float32), axis=1, keepdims=True)
        columns = [
            pl.ds(pl.multiple_of(lax.rem(at_ref[2] + 2 * p + t, N_Y) * rank, rank), rank) for t in range(2)
        ]
        s = jnp.concatenate([jnp.concatenate([s_ref[r, c] for c in columns], axis=1) for r in rows], axis=0)
        recon = jnp.dot(ht_ref[...], wt, preferred_element_type=jnp.float32)
        quotient = (s.astype(jnp.float32) / recon).astype(jnp.bfloat16)
        hn = lax.dot_general(wt, quotient, (((1,), (1,)), ((), ())), preferred_element_type=jnp.float32)
        if p == 0:
            sums_ref[:, :span] = hn
        else:
            sums_ref[:, :span] += hn
        wn = None
        for b in range(blocks):
            part = jnp.dot(h_ref[b], quotient[b * half : (b + 1) * half], preferred_element_type=jnp.float32)
            wn = part if wn is None else wn + part
        for t in range(2):
            ref = (n0, n1, n2, n3)[2 * p + t]
            part = wn[:, t * rank : (t + 1) * rank]
            if first:
                ref[:rank, :] = part
                ref[rank:, :] = rowsum
            else:
                ref[:rank, :] = part + before[2 * p + t][:rank, :]
                ref[rank:, :] = rowsum + before[2 * p + t][rank:, :]
    sums_ref[:, span:] = jnp.broadcast_to(colsum, (rank, LANES))


def half_sweep(at, spectra, h, ws, before=()):
    frames, rows = spectra.shape
    blocks, rank, half = h.shape
    return pl.pallas_call(
        functools.partial(sweep_kernel, not before),
        in_specs=whole(1, pltpu.SMEM) + whole(6 + len(before)),
        out_specs=whole(5),
        out_shape=[jax.ShapeDtypeStruct((rank + 8, rank), jnp.float32)] * 4
        + [jax.ShapeDtypeStruct((rank, blocks * half + LANES), jnp.float32)],
        scratch_shapes=[pltpu.VMEM((blocks * half, rank), jnp.bfloat16)],
        compiler_params=pltpu.CompilerParams(vmem_limit_bytes=28 << 20),
        cost_estimate=pl.CostEstimate(flops=3 * frames * rows * rank, bytes_accessed=4 << 20, transcendentals=0),
        name="sweep_a" if not before else "sweep_b",
    )(at, spectra, h, *ws, *before)


def pair_kernel(a_ref, b_ref, out_ref):
    each = (out_ref.shape[1] - TAIL) // 4
    half, span = 4 * LANES, a_ref.shape[1] - LANES
    group = lax.broadcasted_iota(jnp.int32, (TAIL, LANES), 1) // each
    for r in range(N_R):
        rows = slice(r * each, (r + 1) * each)
        sums = a_ref[rows, span:] + b_ref[rows, span:]
        tail = sums[:TAIL]
        for j in range(1, each // TAIL):
            tail = jnp.where(group == j, sums[j * TAIL : (j + 1) * TAIL], tail)
        for zl in range(2):
            for c in range(4):
                columns = slice(zl * half + c * LANES, zl * half + (c + 1) * LANES)
                out_ref[zl * N_R + r, c * each : (c + 1) * each, :] = a_ref[rows, columns] + b_ref[rows, columns]
            out_ref[zl * N_R + r, 4 * each :, :] = tail


def pair(a, b, each):
    return pl.pallas_call(
        pair_kernel,
        in_specs=whole(2),
        out_specs=whole(1)[0],
        out_shape=jax.ShapeDtypeStruct((N_P, 4 * each + TAIL, LANES), jnp.float32),
        compiler_params=pltpu.CompilerParams(vmem_limit_bytes=12 << 20),
        name="pair",
    )(a, b)


def h_update_kernel(parts_ref, h_ref, new_ref, low_ref):
    each = h_ref.shape[0]
    total = parts_ref[0]
    for i in range(1, N_P):
        total = total + parts_ref[i]
    numer = jnp.concatenate([total[c * each : (c + 1) * each] for c in range(4)], axis=1)
    tail = total[4 * each :]
    colsum = jnp.concatenate([tail[:, j * each : j * each + 1] for j in range(each // TAIL)], axis=0)
    new = h_ref[...] * numer / colsum
    new_ref[...] = new
    low = new.astype(jnp.bfloat16)
    for i in range(N_P):
        low_ref[i] = low


def h_update(parts, h):
    return pl.pallas_call(
        h_update_kernel,
        in_specs=whole(2),
        out_specs=whole(2),
        out_shape=[jax.ShapeDtypeStruct(h.shape, jnp.float32), jax.ShapeDtypeStruct((N_P, *h.shape), jnp.bfloat16)],
        compiler_params=pltpu.CompilerParams(vmem_limit_bytes=12 << 20),
        name="h_update",
    )(parts, h)


def w_update_kernel(p0, p1, p2, p3, w_ref, new_ref, low_ref):
    rank = w_ref.shape[1]
    total = (p0[...] + p1[...]) + (p2[...] + p3[...])
    new = w_ref[...] * total[:rank, :].T / total[rank : rank + 1, :]
    new_ref[...] = new
    low_ref[...] = new.astype(jnp.bfloat16)


def w_update(parts, w):
    return pl.pallas_call(
        w_update_kernel,
        in_specs=whole(5),
        out_specs=whole(2),
        out_shape=[jax.ShapeDtypeStruct(w.shape, jnp.float32), jax.ShapeDtypeStruct(w.shape, jnp.bfloat16)],
        compiler_params=pltpu.CompilerParams(vmem_limit_bytes=12 << 20),
        name="w_update",
    )(*parts, w)


def assemble_kernel(at_ref, z0, z1, z2, z3, out_ref):
    each = z0.shape[1]
    for i, ref in enumerate((z0, z1, z2, z3)):
        z = lax.rem(at_ref[4] + i, 4)
        for t in range(4):
            r = (z // 2) * 4 + lax.rem(at_ref[3] + t, 4)
            out_ref[lax.rem(z, 2), pl.ds(pl.multiple_of(r * each, each), each), :] = ref[t]


def assemble(at, zs):
    _, each, half = zs[0].shape
    return pl.pallas_call(
        assemble_kernel,
        in_specs=whole(1, pltpu.SMEM) + whole(4),
        out_specs=whole(1)[0],
        out_shape=jax.ShapeDtypeStruct((2, N_R * each, half), jnp.bfloat16),
        compiler_params=pltpu.CompilerParams(vmem_limit_bytes=12 << 20),
        name="assemble",
    )(at, *zs)


def exchange(x, axes):
    return lax.all_to_all(x, axes, 0, 0, tiled=True)


def from_sibling(x):
    return lax.ppermute(x, "core", [(0, 1), (1, 0)])


def sent_ahead(x, t):
    return lax.ppermute(x, "y", [(i, (i + t) % N_Y) for i in range(N_Y)])


def taken_ahead(x, axes):
    return [x] + [lax.ppermute(x, axes, [(i, (i - t) % 4) for i in range(4)]) for t in range(1, 4)]


def local(samples, w, h):
    rank = w.shape[1]
    record = samples.reshape(samples.shape[2], samples.shape[3])
    core, y = lax.axis_index("core"), lax.axis_index("y")
    x, z = lax.axis_index("x"), lax.axis_index(("zh", "zl"))
    at = jnp.stack([1 - core, core, y, x, z]).astype(jnp.int32)
    energy = energies(record, dft_table())
    frames, rows = energy.shape[4:]
    energy, w_low, h_low = lax.optimization_barrier((energy, w.astype(jnp.bfloat16), h.astype(jnp.bfloat16)))
    h_own = assemble(at, taken_ahead(jnp.stack(taken_ahead(h_low, "x")), ("zh", "zl")))
    h_oth = from_sibling(h_own)
    ws = taken_ahead(w_low, "y")
    spectra = exchange(energy.reshape(2 * N_P, frames, rows), TILE).reshape(2 * N_P * frames, rows)
    for step in range(ITERS):
        *parts, s_oth = half_sweep(at, spectra, h_oth, ws)
        s_got = from_sibling(s_oth)
        n0, n1, n2, n3, s_own = half_sweep(at, spectra, h_own, ws, parts)
        w_parts = [n0] + [sent_ahead(n, t + 1) for t, n in enumerate((n1, n2, n3))]
        h_parts = exchange(pair(s_own, s_got, h.shape[0]), RANKS)
        h, low = h_update(h_parts, h)
        w_parts, low, h = lax.optimization_barrier((w_parts, low, h))
        w, w_low = w_update(w_parts, w)
        if step + 1 < ITERS:
            ws = taken_ahead(w_low, "y")
            ws, h_own = lax.optimization_barrier((ws, exchange(low, RANKS)))
            h_own = h_own.reshape(2, rank, -1)
            h_oth = from_sibling(h_own)
    return (w, h)


def solution(mesh):
    fine = Mesh(mesh.devices.reshape(SIZES), AXES)
    row, col = ("zh", "x"), ("zl", "y", "core")
    return jax.shard_map(
        local,
        mesh=fine,
        in_specs=(P(col, row, None, None), P(row + col, None), P(row, col)),
        out_specs=(P(row + col, None), P(row, col)),
        check_vma=False,
    )
```

```python
import functools
import math

import jax
import jax.numpy as jnp
import numpy as np
from jax import lax
from jax.experimental import pallas as pl
from jax.experimental.pallas import tpu as pltpu
from jax.sharding import Mesh
from jax.sharding import PartitionSpec as P

BINS = 128
ITERS = 2
WIN = 256

AXES = ("zh", "x", "zl", "y", "core")
SIZES = (2, 4, 2, 4, 2)
TILE = ("zh", "zl", "core", "x")
RANKS = ("zh", "x", "zl")
N_Y = 4
N_R = 8
N_P = 16
LANES = 128
TAIL = 8


def dft_table():
    n = np.arange(WIN, dtype=np.int32)
    k = np.arange(BINS, dtype=np.int32)
    phases = (n[:, None] * k[None, :] % WIN).astype(np.float32) * np.float32(2.0 * math.pi / WIN)
    taper = np.float32(0.5) - np.float32(0.5) * np.cos(n.astype(np.float32) * np.float32(2.0 * math.pi / WIN))
    taper = (taper / np.float32(math.sqrt(3.0 * WIN / 8.0))).astype(np.float32)
    both = np.concatenate([taper[:, None] * np.cos(phases), -taper[:, None] * np.sin(phases)], axis=1)
    return jnp.asarray(both.astype(np.float32)).astype(jnp.bfloat16)


def whole(n, space=pltpu.VMEM):
    return [pl.BlockSpec(memory_space=space)] * n


def energy_kernel(x_hbm, table_ref, out_hbm, x_ref, out_ref, in_sem, out_sem):
    blocks, chans, samples = x_ref.shape
    frames = samples // WIN
    group = 16

    def fetch(r):
        return pltpu.make_async_copy(x_hbm.at[pl.ds(r * chans, chans), :], x_ref.at[r], in_sem.at[r])

    def put(r):
        return pltpu.make_async_copy(out_ref.at[r], out_hbm.at[r // 4, :, :, r % 4], out_sem.at[r])

    for r in range(blocks):
        fetch(r).start()
    table = table_ref[...]

    @pl.loop(0, blocks)
    def _(r):
        fetch(r).wait()
        for g in range(frames // group):
            x = jnp.concatenate(
                [x_ref[r, :, (g * group + f) * WIN : (g * group + f + 1) * WIN] for f in range(group)], axis=0
            )
            spec = jnp.dot(x, table, preferred_element_type=jnp.float32)
            re, im = spec[:, :BINS], spec[:, BINS:]
            energy = (re * re + im * im).reshape(group, chans, BINS)
            energy = pltpu.einshape("fcb->cfb", energy).astype(jnp.bfloat16)
            for c in range(chans):
                zl, y, core, j = c // 16, (c // 4) % 4, (c // 2) % 2, c % 2
                at = (y * 2 + j) * BINS
                out_ref[r, zl, core, g * group : (g + 1) * group, at : at + BINS] = energy[c]
        put(r).start()

    for r in range(blocks):
        put(r).wait()


def energies(record, table):
    channels, samples = record.shape
    frames = samples // WIN
    per_row = channels // N_R
    rows = channels * BINS // (2 * N_P)
    return pl.pallas_call(
        energy_kernel,
        in_specs=[pl.BlockSpec(memory_space=pl.ANY), pl.BlockSpec(memory_space=pltpu.VMEM)],
        out_specs=pl.BlockSpec(memory_space=pl.ANY),
        out_shape=jax.ShapeDtypeStruct((2, 2, 2, 4, frames, rows), jnp.bfloat16),
        scratch_shapes=[
            pltpu.VMEM((N_R, per_row, samples), jnp.bfloat16),
            pltpu.VMEM((N_R, 2, 2, frames, rows), jnp.bfloat16),
            pltpu.SemaphoreType.DMA((N_R,)),
            pltpu.SemaphoreType.DMA((N_R,)),
        ],
        compiler_params=pltpu.CompilerParams(vmem_limit_bytes=58 << 20),
        cost_estimate=pl.CostEstimate(
            flops=2 * channels * frames * WIN * WIN, bytes_accessed=12 << 20, transcendentals=0
        ),
        name="energy",
    )(record, table)


def sweep_kernel(first, at_ref, s_hbm, h_ref, w0, w1, w2, w3, *refs):
    before, (n0, n1, n2, n3, sums_ref, ht_ref, s_ref, sem) = (() if first else refs[:4]), refs[-8:]
    blocks, half = h_ref.shape[1], h_ref.shape[3]
    rank, span = ht_ref.shape[1], blocks * half
    run = half // 2
    core = at_ref[0 if first else 1]

    def fetch(p, t, i):
        row = ((i % 2 * blocks + i // 2) * 2 + core) * run
        column = lax.rem(at_ref[2] + 2 * p + t, N_Y) * rank
        return pltpu.make_async_copy(
            s_hbm.at[pl.ds(pl.multiple_of(row, run), run), pl.ds(pl.multiple_of(column, rank), rank)],
            s_ref.at[p, i * run : (i + 1) * run, t * rank : (t + 1) * rank],
            sem.at[p, t, i],
        )

    pieces = [(t, i) for t in range(2) for i in range(2 * blocks)]
    for p in range(2):
        for t, i in pieces:
            fetch(p, t, i).start()
    h = [h_ref[:, b].reshape(rank, half) for b in range(blocks)]
    for b in range(blocks):
        ht_ref[b * half : (b + 1) * half, :] = h[b].T
    rowsum = jnp.dot(jnp.ones((8, span), jnp.bfloat16), ht_ref[...], preferred_element_type=jnp.float32)
    colsum = jnp.zeros((rank, 1), jnp.float32)
    for p in range(2):
        wt = jnp.concatenate([w[...] for w in ((w0, w1), (w2, w3))[p]], axis=0).T
        colsum = colsum + jnp.sum(wt.astype(jnp.float32), axis=1, keepdims=True)
        recon = jnp.dot(ht_ref[...], wt, preferred_element_type=jnp.float32)
        for t, i in pieces:
            fetch(p, t, i).wait()
        quotient = (s_ref[p].astype(jnp.float32) / recon).astype(jnp.bfloat16)
        hn = lax.dot_general(wt, quotient, (((1,), (1,)), ((), ())), preferred_element_type=jnp.float32)
        if p == 0:
            sums_ref[:, :span] = hn
        else:
            sums_ref[:, :span] += hn
        wn = None
        for b in range(blocks):
            part = jnp.dot(h[b], quotient[b * half : (b + 1) * half], preferred_element_type=jnp.float32)
            wn = part if wn is None else wn + part
        for t in range(2):
            ref = (n0, n1, n2, n3)[2 * p + t]
            part = wn[:, t * rank : (t + 1) * rank]
            if first:
                ref[:rank, :] = part
                ref[rank:, :] = rowsum
            else:
                ref[:rank, :] = part + before[2 * p + t][:rank, :]
                ref[rank:, :] = rowsum + before[2 * p + t][rank:, :]
    sums_ref[:, span:] = jnp.broadcast_to(colsum, (rank, LANES))


def half_sweep(at, spectra, h, ws, before=()):
    frames, rows = spectra.shape
    blocks, half, rank = h.shape[1], h.shape[3], ws[0].shape[1]
    return pl.pallas_call(
        functools.partial(sweep_kernel, not before),
        in_specs=whole(1, pltpu.SMEM) + whole(1, pl.ANY) + whole(5 + len(before)),
        out_specs=whole(5),
        out_shape=[jax.ShapeDtypeStruct((rank + 8, rank), jnp.float32)] * 4
        + [jax.ShapeDtypeStruct((rank, blocks * half + LANES), jnp.float32)],
        scratch_shapes=[
            pltpu.VMEM((blocks * half, rank), jnp.bfloat16),
            pltpu.VMEM((2, blocks * half, 2 * rank), jnp.bfloat16),
            pltpu.SemaphoreType.DMA((2, 2, 2 * blocks)),
        ],
        compiler_params=pltpu.CompilerParams(vmem_limit_bytes=28 << 20),
        cost_estimate=pl.CostEstimate(flops=3 * frames * rows * rank, bytes_accessed=4 << 20, transcendentals=0),
        name="sweep_a" if not before else "sweep_b",
    )(at, spectra, h, *ws, *before)


def pair_kernel(a_ref, b_ref, out_ref):
    each = (out_ref.shape[1] - TAIL) // 4
    half, span = 4 * LANES, a_ref.shape[1] - LANES
    group = lax.broadcasted_iota(jnp.int32, (TAIL, LANES), 1) // each
    for r in range(N_R):
        rows = slice(r * each, (r + 1) * each)
        sums = a_ref[rows, span:] + b_ref[rows, span:]
        tail = sums[:TAIL]
        for j in range(1, each // TAIL):
            tail = jnp.where(group == j, sums[j * TAIL : (j + 1) * TAIL], tail)
        for zl in range(2):
            for c in range(4):
                columns = slice(zl * half + c * LANES, zl * half + (c + 1) * LANES)
                out_ref[r * 2 + zl, c * each : (c + 1) * each, :] = a_ref[rows, columns] + b_ref[rows, columns]
            out_ref[r * 2 + zl, 4 * each :, :] = tail


def pair(a, b, each):
    return pl.pallas_call(
        pair_kernel,
        in_specs=whole(2),
        out_specs=whole(1)[0],
        out_shape=jax.ShapeDtypeStruct((N_P, 4 * each + TAIL, LANES), jnp.float32),
        compiler_params=pltpu.CompilerParams(vmem_limit_bytes=12 << 20),
        name="pair",
    )(a, b)


def h_update_kernel(parts_ref, h_ref, new_ref, low_ref):
    each = h_ref.shape[0]
    total = parts_ref[0]
    for i in range(1, N_P):
        total = total + parts_ref[i]
    numer = jnp.concatenate([total[c * each : (c + 1) * each] for c in range(4)], axis=1)
    tail = total[4 * each :]
    colsum = jnp.concatenate([tail[:, j * each : j * each + 1] for j in range(each // TAIL)], axis=0)
    new = h_ref[...] * numer / colsum
    new_ref[...] = new
    low = new.astype(jnp.bfloat16)
    for i in range(N_P):
        low_ref[i] = low


def h_update(parts, h):
    return pl.pallas_call(
        h_update_kernel,
        in_specs=whole(2),
        out_specs=whole(2),
        out_shape=[jax.ShapeDtypeStruct(h.shape, jnp.float32), jax.ShapeDtypeStruct((N_P, *h.shape), jnp.bfloat16)],
        compiler_params=pltpu.CompilerParams(vmem_limit_bytes=12 << 20),
        name="h_update",
    )(parts, h)


def w_update_kernel(p0, p1, p2, p3, w_ref, new_ref, low_ref):
    rank = w_ref.shape[1]
    total = (p0[...] + p1[...]) + (p2[...] + p3[...])
    new = w_ref[...] * total[:rank, :].T / total[rank : rank + 1, :]
    new_ref[...] = new
    low_ref[...] = new.astype(jnp.bfloat16)


def w_update(parts, w):
    return pl.pallas_call(
        w_update_kernel,
        in_specs=whole(5),
        out_specs=whole(2),
        out_shape=[jax.ShapeDtypeStruct(w.shape, jnp.float32), jax.ShapeDtypeStruct(w.shape, jnp.bfloat16)],
        compiler_params=pltpu.CompilerParams(vmem_limit_bytes=12 << 20),
        name="w_update",
    )(*parts, w)


def spread_kernel(at_ref, own_ref, oth_ref, out_ref):
    for i in range(N_R):
        out_ref[i, at_ref[3]] = own_ref[...]
        out_ref[i, 1 - at_ref[3]] = oth_ref[...]


def spread(at, own, oth):
    return pl.pallas_call(
        spread_kernel,
        in_specs=whole(1, pltpu.SMEM) + whole(2),
        out_specs=whole(1)[0],
        out_shape=jax.ShapeDtypeStruct((N_R, 2, *own.shape), jnp.bfloat16),
        compiler_params=pltpu.CompilerParams(vmem_limit_bytes=12 << 20),
        name="spread",
    )(at, own, oth)


def exchange(x, axes):
    return lax.all_to_all(x, axes, 0, 0, tiled=True)


def from_other(x, axis):
    return lax.ppermute(x, axis, [(0, 1), (1, 0)])


def sent_ahead(x, t):
    return lax.ppermute(x, "y", [(i, (i + t) % N_Y) for i in range(N_Y)])


def taken_ahead(x):
    return [x] + [lax.ppermute(x, "y", [(i, (i - t) % N_Y) for i in range(N_Y)]) for t in range(1, N_Y)]


def local(samples, w, h):
    record = samples.reshape(samples.shape[2], samples.shape[3])
    core, y, zl = lax.axis_index("core"), lax.axis_index("y"), lax.axis_index("zl")
    at = jnp.stack([1 - core, core, y, zl]).astype(jnp.int32)
    h_low = h.astype(jnp.bfloat16)
    h_own = exchange(spread(at, h_low, from_other(h_low, "zl")), ("zh", "x"))
    energy = energies(record, dft_table())
    frames, rows = energy.shape[4:]
    energy, w_low = lax.optimization_barrier((energy, w.astype(jnp.bfloat16)))
    ws = taken_ahead(w_low)
    h_oth = from_other(h_own, "core")
    spectra = exchange(energy.reshape(2 * N_P, frames, rows), TILE).reshape(2 * N_P * frames, rows)
    for step in range(ITERS):
        *parts, s_oth = half_sweep(at, spectra, h_oth, ws)
        s_got = from_other(s_oth, "core")
        n0, n1, n2, n3, s_own = half_sweep(at, spectra, h_own, ws, parts)
        w_parts = [n0] + [sent_ahead(n, t + 1) for t, n in enumerate((n1, n2, n3))]
        h_parts = exchange(pair(s_own, s_got, h.shape[0]), RANKS)
        h, low = h_update(h_parts, h)
        w_parts, low, h = lax.optimization_barrier((w_parts, low, h))
        w, w_low = w_update(w_parts, w)
        if step + 1 < ITERS:
            ws = taken_ahead(w_low)
            ws, h_own = lax.optimization_barrier((ws, exchange(low, RANKS)))
            h_own = h_own.reshape(N_R, 2, *h.shape)
            h_oth = from_other(h_own, "core")
    return (w, h)


def solution(mesh):
    fine = Mesh(mesh.devices.reshape(SIZES), AXES)
    row, col = ("zh", "x"), ("zl", "y", "core")
    return jax.shard_map(
        local,
        mesh=fine,
        in_specs=(P(col, row, None, None), P(row + col, None), P(row, col)),
        out_specs=(P(row + col, None), P(row, col)),
        check_vma=False,
    )
```

```python
import functools
import math
import operator

import jax
import jax.numpy as jnp
import numpy as np
from jax import lax
from jax.experimental import pallas as pl
from jax.experimental.pallas import tpu as pltpu
from jax.sharding import Mesh
from jax.sharding import PartitionSpec as P

BINS = 128
ITERS = 2
WIN = 256

AXES = ("zh", "x", "zl", "y", "core")
SIZES = (2, 4, 2, 4, 2)
TILE = ("zh", "zl", "core", "x")
RANKS = ("zh", "x", "zl")
N_Y = 4
N_R = 8
N_P = 16
LANES = 128
TAIL = 8


def dft_table():
    n = np.arange(WIN, dtype=np.int32)
    k = np.arange(BINS, dtype=np.int32)
    phases = (n[:, None] * k[None, :] % WIN).astype(np.float32) * np.float32(2.0 * math.pi / WIN)
    taper = np.float32(0.5) - np.float32(0.5) * np.cos(n.astype(np.float32) * np.float32(2.0 * math.pi / WIN))
    taper = (taper / np.float32(math.sqrt(3.0 * WIN / 8.0))).astype(np.float32)
    both = np.concatenate([taper[:, None] * np.cos(phases), -taper[:, None] * np.sin(phases)], axis=1)
    return jnp.asarray(both.astype(np.float32)).astype(jnp.bfloat16)


def whole(n, space=pltpu.VMEM):
    return [pl.BlockSpec(memory_space=space)] * n


def energy_kernel(x_hbm, table_ref, out_hbm, x_ref, out_ref, in_sem, out_sem):
    blocks, chans, samples = x_ref.shape
    frames = samples // WIN
    group = 16

    def fetch(r):
        return pltpu.make_async_copy(x_hbm.at[pl.ds(r * chans, chans), :], x_ref.at[r], in_sem.at[r])

    def put(r):
        return pltpu.make_async_copy(out_ref.at[r], out_hbm.at[r // 4, :, :, r % 4], out_sem.at[r])

    for r in range(blocks):
        fetch(r).start()
    table = table_ref[...]

    @pl.loop(0, blocks)
    def _(r):
        fetch(r).wait()
        for g in range(frames // group):
            x = jnp.concatenate(
                [x_ref[r, :, (g * group + f) * WIN : (g * group + f + 1) * WIN] for f in range(group)], axis=0
            )
            spec = jnp.dot(x, table, preferred_element_type=jnp.float32)
            re, im = spec[:, :BINS], spec[:, BINS:]
            energy = (re * re + im * im).reshape(group, chans, BINS)
            energy = pltpu.einshape("fcb->cfb", energy).astype(jnp.bfloat16)
            for c in range(chans):
                zl, y, core, j = c // 16, (c // 4) % 4, (c // 2) % 2, c % 2
                at = (y * 2 + j) * BINS
                out_ref[r, zl, core, g * group : (g + 1) * group, at : at + BINS] = energy[c]
        put(r).start()

    for r in range(blocks):
        put(r).wait()


def energies(record, table):
    channels, samples = record.shape
    frames = samples // WIN
    per_row = channels // N_R
    rows = channels * BINS // (2 * N_P)
    return pl.pallas_call(
        energy_kernel,
        in_specs=[pl.BlockSpec(memory_space=pl.ANY), pl.BlockSpec(memory_space=pltpu.VMEM)],
        out_specs=pl.BlockSpec(memory_space=pl.ANY),
        out_shape=jax.ShapeDtypeStruct((2, 2, 2, 4, frames, rows), jnp.bfloat16),
        scratch_shapes=[
            pltpu.VMEM((N_R, per_row, samples), jnp.bfloat16),
            pltpu.VMEM((N_R, 2, 2, frames, rows), jnp.bfloat16),
            pltpu.SemaphoreType.DMA((N_R,)),
            pltpu.SemaphoreType.DMA((N_R,)),
        ],
        compiler_params=pltpu.CompilerParams(vmem_limit_bytes=58 << 20),
        cost_estimate=pl.CostEstimate(
            flops=2 * channels * frames * WIN * WIN, bytes_accessed=12 << 20, transcendentals=0
        ),
        name="energy",
    )(record, table)


def added(terms):
    return functools.reduce(operator.add, terms)


def sweep_kernel(first, at_ref, s_hbm, h_ref, w0, w1, w2, w3, *refs):
    before, (n0, n1, n2, n3, sums_ref, ht_ref, s_ref, sem) = (() if first else refs[:4]), refs[-8:]
    blocks, half = h_ref.shape[1], h_ref.shape[3]
    rank, span = ht_ref.shape[1], blocks * half
    run = half // 2
    core = at_ref[0 if first else 1]

    def fetch(p, t, i):
        row = ((i % 2 * blocks + i // 2) * 2 + core) * run
        column = lax.rem(at_ref[2] + 2 * p + t, N_Y) * rank
        return pltpu.make_async_copy(
            s_hbm.at[pl.ds(pl.multiple_of(row, run), run), pl.ds(pl.multiple_of(column, rank), rank)],
            s_ref.at[p, i * run : (i + 1) * run, t * rank : (t + 1) * rank],
            sem.at[p, t, i],
        )

    pieces = [(t, i) for t in range(2) for i in range(2 * blocks)]
    for p in range(2):
        for t, i in pieces:
            fetch(p, t, i).start()
    h = [h_ref[:, b].reshape(rank, half) for b in range(blocks)]
    for b in range(blocks):
        ht_ref[b * half : (b + 1) * half, :] = h[b].T
    rowsum = jnp.dot(jnp.ones((8, span), jnp.bfloat16), ht_ref[...], preferred_element_type=jnp.float32)
    wts = [jnp.concatenate([w[...] for w in pair], axis=0).T for pair in ((w0, w1), (w2, w3))]
    colsum = added(jnp.sum(wt.astype(jnp.float32), axis=1, keepdims=True) for wt in wts)
    cuts = [slice(b * half, (b + 1) * half) for b in range(blocks)]
    recons = [[jnp.dot(ht_ref[cut, :], wt, preferred_element_type=jnp.float32) for cut in cuts] for wt in wts]
    for p in range(2):
        for t, i in pieces:
            fetch(p, t, i).wait()
    quotients = [
        [(s_ref[p, cut].astype(jnp.float32) / recons[p][b]).astype(jnp.bfloat16) for b, cut in enumerate(cuts)]
        for p in range(2)
    ]
    for b, cut in enumerate(cuts):
        sums_ref[:, cut] = added(
            lax.dot_general(wts[p], quotients[p][b], (((1,), (1,)), ((), ())), preferred_element_type=jnp.float32)
            for p in range(2)
        )
    for p in range(2):
        wn = added(jnp.dot(h[b], quotients[p][b], preferred_element_type=jnp.float32) for b in range(blocks))
        for t in range(2):
            ref = (n0, n1, n2, n3)[2 * p + t]
            part = wn[:, t * rank : (t + 1) * rank]
            if first:
                ref[:rank, :] = part
                ref[rank:, :] = rowsum
            else:
                ref[:rank, :] = part + before[2 * p + t][:rank, :]
                ref[rank:, :] = rowsum + before[2 * p + t][rank:, :]
    sums_ref[:, span:] = jnp.broadcast_to(colsum, (rank, LANES))


def half_sweep(at, spectra, h, ws, before=()):
    frames, rows = spectra.shape
    blocks, half, rank = h.shape[1], h.shape[3], ws[0].shape[1]
    return pl.pallas_call(
        functools.partial(sweep_kernel, not before),
        in_specs=whole(1, pltpu.SMEM) + whole(1, pl.ANY) + whole(5 + len(before)),
        out_specs=whole(5),
        out_shape=[jax.ShapeDtypeStruct((rank + 8, rank), jnp.float32)] * 4
        + [jax.ShapeDtypeStruct((rank, blocks * half + LANES), jnp.float32)],
        scratch_shapes=[
            pltpu.VMEM((blocks * half, rank), jnp.bfloat16),
            pltpu.VMEM((2, blocks * half, 2 * rank), jnp.bfloat16),
            pltpu.SemaphoreType.DMA((2, 2, 2 * blocks)),
        ],
        compiler_params=pltpu.CompilerParams(vmem_limit_bytes=28 << 20),
        cost_estimate=pl.CostEstimate(flops=3 * frames * rows * rank, bytes_accessed=4 << 20, transcendentals=0),
        name="sweep_a" if not before else "sweep_b",
    )(at, spectra, h, *ws, *before)


def pair_kernel(a_ref, b_ref, out_ref):
    each = (out_ref.shape[1] - TAIL) // 4
    half, span = 4 * LANES, a_ref.shape[1] - LANES
    group = lax.broadcasted_iota(jnp.int32, (TAIL, LANES), 1) // each
    for r in range(N_R):
        rows = slice(r * each, (r + 1) * each)
        sums = a_ref[rows, span:] + b_ref[rows, span:]
        tail = sums[:TAIL]
        for j in range(1, each // TAIL):
            tail = jnp.where(group == j, sums[j * TAIL : (j + 1) * TAIL], tail)
        for zl in range(2):
            for c in range(4):
                columns = slice(zl * half + c * LANES, zl * half + (c + 1) * LANES)
                out_ref[r * 2 + zl, c * each : (c + 1) * each, :] = a_ref[rows, columns] + b_ref[rows, columns]
            out_ref[r * 2 + zl, 4 * each :, :] = tail


def pair(a, b, each):
    return pl.pallas_call(
        pair_kernel,
        in_specs=whole(2),
        out_specs=whole(1)[0],
        out_shape=jax.ShapeDtypeStruct((N_P, 4 * each + TAIL, LANES), jnp.float32),
        compiler_params=pltpu.CompilerParams(vmem_limit_bytes=12 << 20),
        name="pair",
    )(a, b)


def h_update_kernel(parts_ref, h_ref, new_ref, low_ref):
    each = h_ref.shape[0]
    total = parts_ref[0]
    for i in range(1, N_P):
        total = total + parts_ref[i]
    numer = jnp.concatenate([total[c * each : (c + 1) * each] for c in range(4)], axis=1)
    tail = total[4 * each :]
    colsum = jnp.concatenate([tail[:, j * each : j * each + 1] for j in range(each // TAIL)], axis=0)
    new = h_ref[...] * numer / colsum
    new_ref[...] = new
    low = new.astype(jnp.bfloat16)
    for i in range(N_P):
        low_ref[i] = low


def h_update(parts, h):
    return pl.pallas_call(
        h_update_kernel,
        in_specs=whole(2),
        out_specs=whole(2),
        out_shape=[jax.ShapeDtypeStruct(h.shape, jnp.float32), jax.ShapeDtypeStruct((N_P, *h.shape), jnp.bfloat16)],
        compiler_params=pltpu.CompilerParams(vmem_limit_bytes=12 << 20),
        name="h_update",
    )(parts, h)


def w_update_kernel(p0, p1, p2, p3, w_ref, new_ref, low_ref):
    rank = w_ref.shape[1]
    total = (p0[...] + p1[...]) + (p2[...] + p3[...])
    new = w_ref[...] * total[:rank, :].T / total[rank : rank + 1, :]
    new_ref[...] = new
    low_ref[...] = new.astype(jnp.bfloat16)


def w_update(parts, w):
    return pl.pallas_call(
        w_update_kernel,
        in_specs=whole(5),
        out_specs=whole(2),
        out_shape=[jax.ShapeDtypeStruct(w.shape, jnp.float32), jax.ShapeDtypeStruct(w.shape, jnp.bfloat16)],
        compiler_params=pltpu.CompilerParams(vmem_limit_bytes=12 << 20),
        name="w_update",
    )(*parts, w)


def spread_kernel(h_hbm, out_hbm, h_ref, low_ref, in_sem, out_sem):
    fetch = pltpu.make_async_copy(h_hbm, h_ref, in_sem)
    fetch.start()
    fetch.wait()
    low_ref[...] = h_ref[...].astype(jnp.bfloat16)
    puts = [pltpu.make_async_copy(low_ref, out_hbm.at[i], out_sem.at[i]) for i in range(N_P)]
    for put in puts:
        put.start()
    for put in puts:
        put.wait()


def spread(h):
    return pl.pallas_call(
        spread_kernel,
        in_specs=whole(1, pl.ANY),
        out_specs=whole(1, pl.ANY)[0],
        out_shape=jax.ShapeDtypeStruct((N_P, *h.shape), jnp.bfloat16),
        scratch_shapes=[
            pltpu.VMEM(h.shape, jnp.float32),
            pltpu.VMEM(h.shape, jnp.bfloat16),
            pltpu.SemaphoreType.DMA,
            pltpu.SemaphoreType.DMA((N_P,)),
        ],
        compiler_params=pltpu.CompilerParams(vmem_limit_bytes=56 << 20),
        name="spread",
    )(h)


def exchange(x, axes):
    return lax.all_to_all(x, axes, 0, 0, tiled=True)


def from_sibling(x):
    return lax.ppermute(x, "core", [(0, 1), (1, 0)])


def sent_ahead(x, t):
    return lax.ppermute(x, "y", [(i, (i + t) % N_Y) for i in range(N_Y)])


def taken_ahead(x):
    return [x] + [lax.ppermute(x, "y", [(i, (i - t) % N_Y) for i in range(N_Y)]) for t in range(1, N_Y)]


def local(samples, w, h):
    record = samples.reshape(samples.shape[2], samples.shape[3])
    core, y = lax.axis_index("core"), lax.axis_index("y")
    at = jnp.stack([1 - core, core, y]).astype(jnp.int32)
    h_own = exchange(spread(h), RANKS).reshape(N_R, 2, *h.shape)
    energy = energies(record, dft_table())
    frames, rows = energy.shape[4:]
    energy, w_low = lax.optimization_barrier((energy, w.astype(jnp.bfloat16)))
    ws = taken_ahead(w_low)
    h_oth = from_sibling(h_own)
    spectra = exchange(energy.reshape(2 * N_P, frames, rows), TILE).reshape(2 * N_P * frames, rows)
    for step in range(ITERS):
        *parts, s_oth = half_sweep(at, spectra, h_oth, ws)
        s_got = from_sibling(s_oth)
        n0, n1, n2, n3, s_own = half_sweep(at, spectra, h_own, ws, parts)
        w_parts = [n0] + [sent_ahead(n, t + 1) for t, n in enumerate((n1, n2, n3))]
        h_parts = exchange(pair(s_own, s_got, h.shape[0]), RANKS)
        h, low = h_update(h_parts, h)
        w_parts, low, h = lax.optimization_barrier((w_parts, low, h))
        w, w_low = w_update(w_parts, w)
        if step + 1 < ITERS:
            ws = taken_ahead(w_low)
            ws, h_own = lax.optimization_barrier((ws, exchange(low, RANKS)))
            h_own = h_own.reshape(N_R, 2, *h.shape)
            h_oth = from_sibling(h_own)
    return (w, h)


def solution(mesh):
    fine = Mesh(mesh.devices.reshape(SIZES), AXES)
    row, col = ("zh", "x"), ("zl", "y", "core")
    return jax.shard_map(
        local,
        mesh=fine,
        in_specs=(P(col, row, None, None), P(row + col, None), P(row, col)),
        out_specs=(P(row + col, None), P(row, col)),
        check_vma=False,
    )
```

```python
import functools
import math

import jax
import jax.numpy as jnp
import numpy as np
from jax import lax
from jax.experimental import pallas as pl
from jax.experimental.pallas import tpu as pltpu
from jax.sharding import Mesh
from jax.sharding import PartitionSpec as P

BINS = 128
ITERS = 2
WIN = 256

AXES = ("zh", "x", "zl", "y", "core")
SIZES = (2, 4, 2, 4, 2)
TILE = ("zh", "zl", "core", "x")
RANKS = ("x", "zh", "zl")
N_Y = 4
N_R = 8
N_P = 16
LANES = 128
TAIL = 8


def dft_table():
    n = np.arange(WIN, dtype=np.int32)
    k = np.arange(BINS, dtype=np.int32)
    phases = (n[:, None] * k[None, :] % WIN).astype(np.float32) * np.float32(2.0 * math.pi / WIN)
    taper = np.float32(0.5) - np.float32(0.5) * np.cos(n.astype(np.float32) * np.float32(2.0 * math.pi / WIN))
    taper = (taper / np.float32(math.sqrt(3.0 * WIN / 8.0))).astype(np.float32)
    both = np.concatenate([taper[:, None] * np.cos(phases), -taper[:, None] * np.sin(phases)], axis=1)
    return jnp.asarray(both.astype(np.float32)).astype(jnp.bfloat16)


def whole(n, space=pltpu.VMEM):
    return [pl.BlockSpec(memory_space=space)] * n


def energy_kernel(x_hbm, table_ref, out_hbm, x_ref, out_ref, in_sem, out_sem):
    blocks, chans, samples = x_ref.shape
    frames = samples // WIN
    group = 16

    def fetch(r):
        return pltpu.make_async_copy(x_hbm.at[pl.ds(r * chans, chans), :], x_ref.at[r], in_sem.at[r])

    def put(r):
        return pltpu.make_async_copy(out_ref.at[r], out_hbm.at[r // 4, :, :, r % 4], out_sem.at[r])

    for r in range(blocks):
        fetch(r).start()
    table = table_ref[...]

    @pl.loop(0, blocks)
    def _(r):
        fetch(r).wait()
        for g in range(frames // group):
            x = jnp.concatenate(
                [x_ref[r, :, (g * group + f) * WIN : (g * group + f + 1) * WIN] for f in range(group)], axis=0
            )
            spec = jnp.dot(x, table, preferred_element_type=jnp.float32)
            re, im = spec[:, :BINS], spec[:, BINS:]
            energy = (re * re + im * im).reshape(group, chans, BINS)
            energy = pltpu.einshape("fcb->cfb", energy).astype(jnp.bfloat16)
            for c in range(chans):
                zl, y, core, j = c // 16, (c // 4) % 4, (c // 2) % 2, c % 2
                at = (y * 2 + j) * BINS
                out_ref[r, zl, core, g * group : (g + 1) * group, at : at + BINS] = energy[c]
        put(r).start()

    for r in range(blocks):
        put(r).wait()


def energies(record, table):
    channels, samples = record.shape
    frames = samples // WIN
    per_row = channels // N_R
    rows = channels * BINS // (2 * N_P)
    return pl.pallas_call(
        energy_kernel,
        in_specs=[pl.BlockSpec(memory_space=pl.ANY), pl.BlockSpec(memory_space=pltpu.VMEM)],
        out_specs=pl.BlockSpec(memory_space=pl.ANY),
        out_shape=jax.ShapeDtypeStruct((2, 2, 2, 4, frames, rows), jnp.bfloat16),
        scratch_shapes=[
            pltpu.VMEM((N_R, per_row, samples), jnp.bfloat16),
            pltpu.VMEM((N_R, 2, 2, frames, rows), jnp.bfloat16),
            pltpu.SemaphoreType.DMA((N_R,)),
            pltpu.SemaphoreType.DMA((N_R,)),
        ],
        compiler_params=pltpu.CompilerParams(vmem_limit_bytes=58 << 20),
        cost_estimate=pl.CostEstimate(
            flops=2 * channels * frames * WIN * WIN, bytes_accessed=12 << 20, transcendentals=0
        ),
        name="energy",
    )(record, table)


def sweep_kernel(first, at_ref, s_hbm, h_ref, w0, w1, w2, w3, *refs):
    before, (n0, n1, n2, n3, sums_ref, ht_ref, s_ref, sem) = (() if first else refs[:4]), refs[-8:]
    blocks, half = h_ref.shape[2], h_ref.shape[4]
    rank, span = ht_ref.shape[1], blocks * half
    run = half // 2
    core = at_ref[0 if first else 1]

    def fetch(p, t, i):
        row = ((i % 2 * blocks + i // 2) * 2 + core) * run
        column = lax.rem(at_ref[2] + 2 * p + t, N_Y) * rank
        return pltpu.make_async_copy(
            s_hbm.at[pl.ds(pl.multiple_of(row, run), run), pl.ds(pl.multiple_of(column, rank), rank)],
            s_ref.at[p, i * run : (i + 1) * run, t * rank : (t + 1) * rank],
            sem.at[p, t, i],
        )

    pieces = [(t, i) for t in range(2) for i in range(2 * blocks)]
    for p in range(2):
        for t, i in pieces:
            fetch(p, t, i).start()
    h = [jnp.concatenate([h_ref[x, zh, b] for zh in range(2) for x in range(4)], axis=0) for b in range(blocks)]
    for b in range(blocks):
        ht_ref[b * half : (b + 1) * half, :] = h[b].T
    rowsum = jnp.dot(jnp.ones((8, span), jnp.bfloat16), ht_ref[...], preferred_element_type=jnp.float32)
    colsum = jnp.zeros((rank, 1), jnp.float32)
    for p in range(2):
        wt = jnp.concatenate([w[...] for w in ((w0, w1), (w2, w3))[p]], axis=0).T
        colsum = colsum + jnp.sum(wt.astype(jnp.float32), axis=1, keepdims=True)
        recon = jnp.dot(ht_ref[...], wt, preferred_element_type=jnp.float32)
        for t, i in pieces:
            fetch(p, t, i).wait()
        quotient = (s_ref[p].astype(jnp.float32) / recon).astype(jnp.bfloat16)
        hn = lax.dot_general(wt, quotient, (((1,), (1,)), ((), ())), preferred_element_type=jnp.float32)
        if p == 0:
            sums_ref[:, :span] = hn
        else:
            sums_ref[:, :span] += hn
        wn = None
        for b in range(blocks):
            part = jnp.dot(h[b], quotient[b * half : (b + 1) * half], preferred_element_type=jnp.float32)
            wn = part if wn is None else wn + part
        for t in range(2):
            ref = (n0, n1, n2, n3)[2 * p + t]
            part = wn[:, t * rank : (t + 1) * rank]
            if first:
                ref[:rank, :] = part
                ref[rank:, :] = rowsum
            else:
                ref[:rank, :] = part + before[2 * p + t][:rank, :]
                ref[rank:, :] = rowsum + before[2 * p + t][rank:, :]
    sums_ref[:, span:] = jnp.broadcast_to(colsum, (rank, LANES))


def half_sweep(at, spectra, h, ws, before=()):
    frames, rows = spectra.shape
    blocks, half, rank = h.shape[2], h.shape[4], ws[0].shape[1]
    return pl.pallas_call(
        functools.partial(sweep_kernel, not before),
        in_specs=whole(1, pltpu.SMEM) + whole(1, pl.ANY) + whole(5 + len(before)),
        out_specs=whole(5),
        out_shape=[jax.ShapeDtypeStruct((rank + 8, rank), jnp.float32)] * 4
        + [jax.ShapeDtypeStruct((rank, blocks * half + LANES), jnp.float32)],
        scratch_shapes=[
            pltpu.VMEM((blocks * half, rank), jnp.bfloat16),
            pltpu.VMEM((2, blocks * half, 2 * rank), jnp.bfloat16),
            pltpu.SemaphoreType.DMA((2, 2, 2 * blocks)),
        ],
        compiler_params=pltpu.CompilerParams(vmem_limit_bytes=28 << 20),
        cost_estimate=pl.CostEstimate(flops=3 * frames * rows * rank, bytes_accessed=4 << 20, transcendentals=0),
        name="sweep_a" if not before else "sweep_b",
    )(at, spectra, h, *ws, *before)


def pair_kernel(a_ref, b_ref, out_ref):
    each = (out_ref.shape[1] - TAIL) // 4
    half, span = 4 * LANES, a_ref.shape[1] - LANES
    group = lax.broadcasted_iota(jnp.int32, (TAIL, LANES), 1) // each
    for r in range(N_R):
        rows, at = slice(r * each, (r + 1) * each), (r % 4 * 2 + r // 4) * 2
        sums = a_ref[rows, span:] + b_ref[rows, span:]
        tail = sums[:TAIL]
        for j in range(1, each // TAIL):
            tail = jnp.where(group == j, sums[j * TAIL : (j + 1) * TAIL], tail)
        for zl in range(2):
            for c in range(4):
                columns = slice(zl * half + c * LANES, zl * half + (c + 1) * LANES)
                out_ref[at + zl, c * each : (c + 1) * each, :] = a_ref[rows, columns] + b_ref[rows, columns]
            out_ref[at + zl, 4 * each :, :] = tail


def pair(a, b, each):
    return pl.pallas_call(
        pair_kernel,
        in_specs=whole(2),
        out_specs=whole(1)[0],
        out_shape=jax.ShapeDtypeStruct((N_P, 4 * each + TAIL, LANES), jnp.float32),
        compiler_params=pltpu.CompilerParams(vmem_limit_bytes=12 << 20),
        name="pair",
    )(a, b)


def h_update_kernel(parts_ref, h_ref, new_ref, low_ref):
    each = h_ref.shape[0]
    total = parts_ref[0]
    for i in range(1, N_P):
        total = total + parts_ref[i]
    numer = jnp.concatenate([total[c * each : (c + 1) * each] for c in range(4)], axis=1)
    tail = total[4 * each :]
    colsum = jnp.concatenate([tail[:, j * each : j * each + 1] for j in range(each // TAIL)], axis=0)
    new = h_ref[...] * numer / colsum
    new_ref[...] = new
    low = new.astype(jnp.bfloat16)
    for i in range(N_P):
        low_ref[i] = low


def h_update(parts, h):
    return pl.pallas_call(
        h_update_kernel,
        in_specs=whole(2),
        out_specs=whole(2),
        out_shape=[jax.ShapeDtypeStruct(h.shape, jnp.float32), jax.ShapeDtypeStruct((N_P, *h.shape), jnp.bfloat16)],
        compiler_params=pltpu.CompilerParams(vmem_limit_bytes=12 << 20),
        name="h_update",
    )(parts, h)


def w_update_kernel(p0, p1, p2, p3, w_ref, new_ref, low_ref):
    rank = w_ref.shape[1]
    total = (p0[...] + p1[...]) + (p2[...] + p3[...])
    new = w_ref[...] * total[:rank, :].T / total[rank : rank + 1, :]
    new_ref[...] = new
    low_ref[...] = new.astype(jnp.bfloat16)


def w_update(parts, w):
    return pl.pallas_call(
        w_update_kernel,
        in_specs=whole(5),
        out_specs=whole(2),
        out_shape=[jax.ShapeDtypeStruct(w.shape, jnp.float32), jax.ShapeDtypeStruct(w.shape, jnp.bfloat16)],
        compiler_params=pltpu.CompilerParams(vmem_limit_bytes=12 << 20),
        name="w_update",
    )(*parts, w)


def spread_kernel(h_hbm, out_hbm, h_ref, low_ref, in_sem, out_sem):
    fetch = pltpu.make_async_copy(h_hbm, h_ref, in_sem)
    fetch.start()
    fetch.wait()
    low_ref[...] = h_ref[...].astype(jnp.bfloat16)
    puts = [pltpu.make_async_copy(low_ref, out_hbm.at[i], out_sem.at[i]) for i in range(N_P)]
    for put in puts:
        put.start()
    for put in puts:
        put.wait()


def spread(h):
    return pl.pallas_call(
        spread_kernel,
        in_specs=whole(1, pl.ANY),
        out_specs=whole(1, pl.ANY)[0],
        out_shape=jax.ShapeDtypeStruct((N_P, *h.shape), jnp.bfloat16),
        scratch_shapes=[
            pltpu.VMEM(h.shape, jnp.float32),
            pltpu.VMEM(h.shape, jnp.bfloat16),
            pltpu.SemaphoreType.DMA,
            pltpu.SemaphoreType.DMA((N_P,)),
        ],
        compiler_params=pltpu.CompilerParams(vmem_limit_bytes=56 << 20),
        name="spread",
    )(h)


def exchange(x, axes):
    return lax.all_to_all(x, axes, 0, 0, tiled=True)


def from_sibling(x):
    return lax.ppermute(x, "core", [(0, 1), (1, 0)])


def sent_ahead(x, t):
    return lax.ppermute(x, "y", [(i, (i + t) % N_Y) for i in range(N_Y)])


def taken_ahead(x):
    return [x] + [lax.ppermute(x, "y", [(i, (i - t) % N_Y) for i in range(N_Y)]) for t in range(1, N_Y)]


def local(samples, w, h):
    record = samples.reshape(samples.shape[2], samples.shape[3])
    core, y = lax.axis_index("core"), lax.axis_index("y")
    at = jnp.stack([1 - core, core, y]).astype(jnp.int32)
    h_own = exchange(spread(h), RANKS).reshape(4, 2, 2, *h.shape)
    energy = energies(record, dft_table())
    frames, rows = energy.shape[4:]
    energy, w_low = lax.optimization_barrier((energy, w.astype(jnp.bfloat16)))
    ws = taken_ahead(w_low)
    h_oth = from_sibling(h_own)
    spectra = exchange(energy.reshape(2 * N_P, frames, rows), TILE).reshape(2 * N_P * frames, rows)
    for step in range(ITERS):
        *parts, s_oth = half_sweep(at, spectra, h_oth, ws)
        s_got = from_sibling(s_oth)
        n0, n1, n2, n3, s_own = half_sweep(at, spectra, h_own, ws, parts)
        w_parts = [n0] + [sent_ahead(n, t + 1) for t, n in enumerate((n1, n2, n3))]
        h_parts = exchange(pair(s_own, s_got, h.shape[0]), RANKS)
        h, low = h_update(h_parts, h)
        w_parts, low, h = lax.optimization_barrier((w_parts, low, h))
        w, w_low = w_update(w_parts, w)
        if step + 1 < ITERS:
            ws = taken_ahead(w_low)
            ws, h_own = lax.optimization_barrier((ws, exchange(low, RANKS)))
            h_own = h_own.reshape(4, 2, 2, *h.shape)
            h_oth = from_sibling(h_own)
    return (w, h)


def solution(mesh):
    fine = Mesh(mesh.devices.reshape(SIZES), AXES)
    row, col = ("zh", "x"), ("zl", "y", "core")
    return jax.shard_map(
        local,
        mesh=fine,
        in_specs=(P(col, row, None, None), P(row + col, None), P(row, col)),
        out_specs=(P(row + col, None), P(row, col)),
        check_vma=False,
    )
```

```python
import functools
import math

import jax
import jax.numpy as jnp
import numpy as np
from jax import lax
from jax.experimental import pallas as pl
from jax.experimental.pallas import tpu as pltpu
from jax.sharding import Mesh
from jax.sharding import PartitionSpec as P

BINS = 128
ITERS = 2
WIN = 256

AXES = ("zh", "x", "zl", "y", "core")
SIZES = (2, 4, 2, 4, 2)
TILE = ("zh", "zl", "core", "x")
RANKS = ("x", "zh", "zl")
N_Y = 4
N_R = 8
N_P = 16
LANES = 128
TAIL = 8


def dft_table():
    n = np.arange(WIN, dtype=np.int32)
    k = np.arange(BINS, dtype=np.int32)
    phases = (n[:, None] * k[None, :] % WIN).astype(np.float32) * np.float32(2.0 * math.pi / WIN)
    taper = np.float32(0.5) - np.float32(0.5) * np.cos(n.astype(np.float32) * np.float32(2.0 * math.pi / WIN))
    taper = (taper / np.float32(math.sqrt(3.0 * WIN / 8.0))).astype(np.float32)
    both = np.concatenate([taper[:, None] * np.cos(phases), -taper[:, None] * np.sin(phases)], axis=1)
    return jnp.asarray(both.astype(np.float32)).astype(jnp.bfloat16)


def whole(n, space=pltpu.VMEM):
    return [pl.BlockSpec(memory_space=space)] * n


def energy_kernel(x_hbm, table_ref, out_hbm, x_ref, out_ref, in_sem, out_sem):
    blocks, chans, samples = x_ref.shape
    frames = samples // WIN
    group = 16

    def fetch(r):
        return pltpu.make_async_copy(x_hbm.at[pl.ds(r * chans, chans), :], x_ref.at[r], in_sem.at[r])

    def put(r):
        return pltpu.make_async_copy(out_ref.at[r], out_hbm.at[r // 4, :, :, r % 4], out_sem.at[r])

    for r in range(blocks):
        fetch(r).start()
    table = table_ref[...]

    @pl.loop(0, blocks)
    def _(r):
        fetch(r).wait()
        for g in range(frames // group):
            x = jnp.concatenate(
                [x_ref[r, :, (g * group + f) * WIN : (g * group + f + 1) * WIN] for f in range(group)], axis=0
            )
            spec = jnp.dot(x, table, preferred_element_type=jnp.float32)
            re, im = spec[:, :BINS], spec[:, BINS:]
            energy = (re * re + im * im).reshape(group, chans, BINS)
            energy = pltpu.einshape("fcb->cfb", energy).astype(jnp.bfloat16)
            for c in range(chans):
                zl, y, core, j = c // 16, (c // 4) % 4, (c // 2) % 2, c % 2
                at = (y * 2 + j) * BINS
                out_ref[r, zl, core, g * group : (g + 1) * group, at : at + BINS] = energy[c]
        put(r).start()

    for r in range(blocks):
        put(r).wait()


def energies(record, table):
    channels, samples = record.shape
    frames = samples // WIN
    per_row = channels // N_R
    rows = channels * BINS // (2 * N_P)
    return pl.pallas_call(
        energy_kernel,
        in_specs=[pl.BlockSpec(memory_space=pl.ANY), pl.BlockSpec(memory_space=pltpu.VMEM)],
        out_specs=pl.BlockSpec(memory_space=pl.ANY),
        out_shape=jax.ShapeDtypeStruct((2, 2, 2, 4, frames, rows), jnp.bfloat16),
        scratch_shapes=[
            pltpu.VMEM((N_R, per_row, samples), jnp.bfloat16),
            pltpu.VMEM((N_R, 2, 2, frames, rows), jnp.bfloat16),
            pltpu.SemaphoreType.DMA((N_R,)),
            pltpu.SemaphoreType.DMA((N_R,)),
        ],
        compiler_params=pltpu.CompilerParams(vmem_limit_bytes=58 << 20),
        cost_estimate=pl.CostEstimate(
            flops=2 * channels * frames * WIN * WIN, bytes_accessed=12 << 20, transcendentals=0
        ),
        name="energy",
    )(record, table)


def level(x, high):
    relative = jnp.where(high == 0.0, 0.0, (x - high) / high)
    return jnp.clip(jnp.floor(relative * (7.0 * 256.0) + 0.5), -7.0, 7.0) + 7.0


def coded(a, b):
    high_a, high_b = [x.astype(jnp.bfloat16).astype(jnp.float32) for x in (a, b)]
    return high_a, high_b, level(a, high_a) * 15.0 + level(b, high_b)


def decoded(high_a, high_b, code):
    first = jnp.floor((code + 0.5) * (1.0 / 15.0))
    second = code - 15.0 * first
    return [high + high * ((q - 7.0) * (1.0 / (7.0 * 256.0))) for high, q in ((high_a, first), (high_b, second))]


def hi_lo(x):
    high = x.astype(jnp.bfloat16).astype(jnp.float32)
    return jnp.concatenate([high, x - high], axis=0).astype(jnp.bfloat16)


def sweep_kernel(first, at_ref, s_hbm, h_ref, w0, w1, w2, w3, *refs):
    before, (n0, n1, n2, n3, sums_ref, ht_ref, s_ref, sem) = (() if first else refs[:4]), refs[-8:]
    blocks, half = h_ref.shape[2], h_ref.shape[4]
    rank, span = ht_ref.shape[1], blocks * half
    run = half // 2
    core = at_ref[0 if first else 1]

    def fetch(p, t, i):
        row = ((i % 2 * blocks + i // 2) * 2 + core) * run
        column = lax.rem(at_ref[2] + 2 * p + t, N_Y) * rank
        return pltpu.make_async_copy(
            s_hbm.at[pl.ds(pl.multiple_of(row, run), run), pl.ds(pl.multiple_of(column, rank), rank)],
            s_ref.at[p, i * run : (i + 1) * run, t * rank : (t + 1) * rank],
            sem.at[p, t, i],
        )

    pieces = [(t, i) for t in range(2) for i in range(2 * blocks)]
    for p in range(2):
        for t, i in pieces:
            fetch(p, t, i).start()
    h = [jnp.concatenate([h_ref[x, zh, b] for zh in range(2) for x in range(4)], axis=0) for b in range(blocks)]
    for b in range(blocks):
        ht_ref[b * half : (b + 1) * half, :] = h[b].T
    rowsum = jnp.dot(jnp.ones((8, span), jnp.bfloat16), ht_ref[...], preferred_element_type=jnp.float32)
    colsum = jnp.zeros((rank, 1), jnp.float32)
    for p in range(2):
        wt = jnp.concatenate([w[...] for w in ((w0, w1), (w2, w3))[p]], axis=0).T
        colsum = colsum + jnp.sum(wt.astype(jnp.float32), axis=1, keepdims=True)
        recon = jnp.dot(ht_ref[...], wt, preferred_element_type=jnp.float32)
        for t, i in pieces:
            fetch(p, t, i).wait()
        quotient = (s_ref[p].astype(jnp.float32) / recon).astype(jnp.bfloat16)
        hn = lax.dot_general(wt, quotient, (((1,), (1,)), ((), ())), preferred_element_type=jnp.float32)
        if p == 0:
            sums_ref[:, :span] = hn
        else:
            sums_ref[:, :span] += hn
        wn = None
        for b in range(blocks):
            part = jnp.dot(h[b], quotient[b * half : (b + 1) * half], preferred_element_type=jnp.float32)
            wn = part if wn is None else wn + part
        for t in range(2):
            ref = (n0, n1, n2, n3)[2 * p + t]
            part = wn[:, t * rank : (t + 1) * rank]
            if first:
                ref[:rank, :] = part
                ref[rank:, :] = rowsum
                continue
            part = part + before[2 * p + t][:rank, :]
            total = rowsum + before[2 * p + t][rank:, :]
            if p == 0 and t == 0:
                ref[:rank, :] = part
                ref[rank:, :] = total
                continue
            high_a, high_b, code = coded(part[: rank // 2], part[rank // 2 :])
            ref[: rank // 2, :] = high_a.astype(jnp.bfloat16)
            ref[rank // 2 : rank, :] = high_b.astype(jnp.bfloat16)
            ref[rank : rank + rank // 2, :] = code.astype(jnp.bfloat16)
            ref[rank + rank // 2 :, :] = hi_lo(total)
    sums_ref[:, span:] = jnp.broadcast_to(colsum, (rank, LANES))


def half_sweep(at, spectra, h, ws, before=()):
    frames, rows = spectra.shape
    blocks, half, rank = h.shape[2], h.shape[4], ws[0].shape[1]
    return pl.pallas_call(
        functools.partial(sweep_kernel, not before),
        in_specs=whole(1, pltpu.SMEM) + whole(1, pl.ANY) + whole(5 + len(before)),
        out_specs=whole(5),
        out_shape=[jax.ShapeDtypeStruct((rank + 8, rank), jnp.float32)]
        + [
            jax.ShapeDtypeStruct((rank + rank // 2 + 16, rank), jnp.bfloat16)
            if before
            else jax.ShapeDtypeStruct((rank + 8, rank), jnp.float32)
        ]
        * 3
        + [jax.ShapeDtypeStruct((rank, blocks * half + LANES), jnp.float32)],
        scratch_shapes=[
            pltpu.VMEM((blocks * half, rank), jnp.bfloat16),
            pltpu.VMEM((2, blocks * half, 2 * rank), jnp.bfloat16),
            pltpu.SemaphoreType.DMA((2, 2, 2 * blocks)),
        ],
        compiler_params=pltpu.CompilerParams(vmem_limit_bytes=28 << 20),
        cost_estimate=pl.CostEstimate(flops=3 * frames * rows * rank, bytes_accessed=4 << 20, transcendentals=0),
        name="sweep_a" if not before else "sweep_b",
    )(at, spectra, h, *ws, *before)


def pair_kernel(a_ref, b_ref, out_ref):
    each = (out_ref.shape[1] - 2 * TAIL) // 6
    half, span = 4 * LANES, a_ref.shape[1] - LANES
    group = lax.broadcasted_iota(jnp.int32, (TAIL, LANES), 1) // each
    for r in range(N_R):
        rows, at = slice(r * each, (r + 1) * each), (r % 4 * 2 + r // 4) * 2
        sums = a_ref[rows, span:] + b_ref[rows, span:]
        tail = sums[:TAIL]
        for j in range(1, each // TAIL):
            tail = jnp.where(group == j, sums[j * TAIL : (j + 1) * TAIL], tail)
        for zl in range(2):
            parts = []
            for c in range(4):
                columns = slice(zl * half + c * LANES, zl * half + (c + 1) * LANES)
                parts.append(a_ref[rows, columns] + b_ref[rows, columns])
            codes = []
            for c in (0, 2):
                high_a, high_b, code = coded(parts[c], parts[c + 1])
                out_ref[at + zl, c * each : (c + 1) * each, :] = high_a.astype(jnp.bfloat16)
                out_ref[at + zl, (c + 1) * each : (c + 2) * each, :] = high_b.astype(jnp.bfloat16)
                codes.append(code.astype(jnp.bfloat16))
            out_ref[at + zl, 4 * each : 6 * each, :] = jnp.concatenate(codes, axis=0)
            out_ref[at + zl, 6 * each :, :] = hi_lo(tail)


def pair(a, b, each):
    return pl.pallas_call(
        pair_kernel,
        in_specs=whole(2),
        out_specs=whole(1)[0],
        out_shape=jax.ShapeDtypeStruct((N_P, 6 * each + 2 * TAIL, LANES), jnp.bfloat16),
        compiler_params=pltpu.CompilerParams(vmem_limit_bytes=12 << 20),
        name="pair",
    )(a, b)


def h_update_kernel(parts_ref, h_ref, new_ref, low_ref):
    each = h_ref.shape[0]
    blocks, tail = [0.0] * 4, 0.0
    for i in range(N_P):
        part = parts_ref[i].astype(jnp.float32)
        pieces = [part[c * each : (c + 1) * each] for c in range(6)]
        values = decoded(*pieces[0:2], pieces[4]) + decoded(*pieces[2:4], pieces[5])
        blocks = [block + value for block, value in zip(blocks, values)]
        tail = tail + part[6 * each :]
    numer = jnp.concatenate(blocks, axis=1)
    tail = tail[:TAIL] + tail[TAIL:]
    colsum = jnp.concatenate([tail[:, j * each : j * each + 1] for j in range(each // TAIL)], axis=0)
    new = h_ref[...] * numer / colsum
    new_ref[...] = new
    low = new.astype(jnp.bfloat16)
    for i in range(N_P):
        low_ref[i] = low


def h_update(parts, h):
    return pl.pallas_call(
        h_update_kernel,
        in_specs=whole(2),
        out_specs=whole(2),
        out_shape=[jax.ShapeDtypeStruct(h.shape, jnp.float32), jax.ShapeDtypeStruct((N_P, *h.shape), jnp.bfloat16)],
        compiler_params=pltpu.CompilerParams(vmem_limit_bytes=12 << 20),
        name="h_update",
    )(parts, h)


def w_update_kernel(p0, p1, p2, p3, w_ref, new_ref, low_ref):
    rank = w_ref.shape[1]
    cut = rank // 2
    tops, bottoms, rowsum = p0[:cut, :], p0[cut:rank, :], p0[rank : rank + 1, :]
    for ref in (p1, p2, p3):
        part = ref[...].astype(jnp.float32)
        top, bottom = decoded(part[:cut], part[cut:rank], part[rank : rank + cut])
        tops, bottoms = tops + top, bottoms + bottom
        rowsum = rowsum + part[rank + cut : rank + cut + 1] + part[rank + cut + 8 : rank + cut + 9]
    new = w_ref[...] * jnp.concatenate([tops, bottoms], axis=0).T / rowsum
    new_ref[...] = new
    low_ref[...] = new.astype(jnp.bfloat16)


def w_update(parts, w):
    return pl.pallas_call(
        w_update_kernel,
        in_specs=whole(5),
        out_specs=whole(2),
        out_shape=[jax.ShapeDtypeStruct(w.shape, jnp.float32), jax.ShapeDtypeStruct(w.shape, jnp.bfloat16)],
        compiler_params=pltpu.CompilerParams(vmem_limit_bytes=12 << 20),
        name="w_update",
    )(*parts, w)


def spread_kernel(h_hbm, out_hbm, h_ref, low_ref, in_sem, out_sem):
    fetch = pltpu.make_async_copy(h_hbm, h_ref, in_sem)
    fetch.start()
    fetch.wait()
    low_ref[...] = h_ref[...].astype(jnp.bfloat16)
    puts = [pltpu.make_async_copy(low_ref, out_hbm.at[i], out_sem.at[i]) for i in range(N_P)]
    for put in puts:
        put.start()
    for put in puts:
        put.wait()


def spread(h):
    return pl.pallas_call(
        spread_kernel,
        in_specs=whole(1, pl.ANY),
        out_specs=whole(1, pl.ANY)[0],
        out_shape=jax.ShapeDtypeStruct((N_P, *h.shape), jnp.bfloat16),
        scratch_shapes=[
            pltpu.VMEM(h.shape, jnp.float32),
            pltpu.VMEM(h.shape, jnp.bfloat16),
            pltpu.SemaphoreType.DMA,
            pltpu.SemaphoreType.DMA((N_P,)),
        ],
        compiler_params=pltpu.CompilerParams(vmem_limit_bytes=56 << 20),
        name="spread",
    )(h)


def exchange(x, axes):
    return lax.all_to_all(x, axes, 0, 0, tiled=True)


def from_sibling(x):
    return lax.ppermute(x, "core", [(0, 1), (1, 0)])


def sent_ahead(x, t):
    return lax.ppermute(x, "y", [(i, (i + t) % N_Y) for i in range(N_Y)])


def taken_ahead(x):
    return [x] + [lax.ppermute(x, "y", [(i, (i - t) % N_Y) for i in range(N_Y)]) for t in range(1, N_Y)]


def local(samples, w, h):
    record = samples.reshape(samples.shape[2], samples.shape[3])
    core, y = lax.axis_index("core"), lax.axis_index("y")
    at = jnp.stack([1 - core, core, y]).astype(jnp.int32)
    h_own = exchange(spread(h), RANKS).reshape(4, 2, 2, *h.shape)
    energy = energies(record, dft_table())
    frames, rows = energy.shape[4:]
    energy, w_low = lax.optimization_barrier((energy, w.astype(jnp.bfloat16)))
    ws = taken_ahead(w_low)
    h_oth = from_sibling(h_own)
    spectra = exchange(energy.reshape(2 * N_P, frames, rows), TILE).reshape(2 * N_P * frames, rows)
    for step in range(ITERS):
        *parts, s_oth = half_sweep(at, spectra, h_oth, ws)
        s_got = from_sibling(s_oth)
        n0, n1, n2, n3, s_own = half_sweep(at, spectra, h_own, ws, parts)
        w_parts = [n0] + [sent_ahead(n, t + 1) for t, n in enumerate((n1, n2, n3))]
        h_parts = exchange(pair(s_own, s_got, h.shape[0]), RANKS)
        h, low = h_update(h_parts, h)
        w_parts, low, h = lax.optimization_barrier((w_parts, low, h))
        w, w_low = w_update(w_parts, w)
        if step + 1 < ITERS:
            ws = taken_ahead(w_low)
            ws, h_own = lax.optimization_barrier((ws, exchange(low, RANKS)))
            h_own = h_own.reshape(4, 2, 2, *h.shape)
            h_oth = from_sibling(h_own)
    return (w, h)


def solution(mesh):
    fine = Mesh(mesh.devices.reshape(SIZES), AXES)
    row, col = ("zh", "x"), ("zl", "y", "core")
    return jax.shard_map(
        local,
        mesh=fine,
        in_specs=(P(col, row, None, None), P(row + col, None), P(row, col)),
        out_specs=(P(row + col, None), P(row, col)),
        check_vma=False,
    )
```

```python
import functools
import math

import jax
import jax.numpy as jnp
import numpy as np
from jax import lax
from jax.experimental import pallas as pl
from jax.experimental.pallas import tpu as pltpu
from jax.sharding import Mesh
from jax.sharding import PartitionSpec as P

BINS = 128
ITERS = 2
WIN = 256

AXES = ("zh", "x", "zl", "y", "core")
SIZES = (2, 4, 2, 4, 2)
TILE = ("zh", "zl", "core", "x")
RANKS = ("x", "zh", "zl")
N_Y = 4
N_R = 8
N_P = 16
LANES = 128
TAIL = 8


def dft_table():
    n = np.arange(WIN, dtype=np.int32)
    k = np.arange(BINS, dtype=np.int32)
    phases = (n[:, None] * k[None, :] % WIN).astype(np.float32) * np.float32(2.0 * math.pi / WIN)
    taper = np.float32(0.5) - np.float32(0.5) * np.cos(n.astype(np.float32) * np.float32(2.0 * math.pi / WIN))
    taper = (taper / np.float32(math.sqrt(3.0 * WIN / 8.0))).astype(np.float32)
    both = np.concatenate([taper[:, None] * np.cos(phases), -taper[:, None] * np.sin(phases)], axis=1)
    return jnp.asarray(both.astype(np.float32)).astype(jnp.bfloat16)


def whole(n, space=pltpu.VMEM):
    return [pl.BlockSpec(memory_space=space)] * n


def energy_kernel(x_hbm, table_ref, out_hbm, x_ref, out_ref, in_sem, out_sem):
    blocks, chans, samples = x_ref.shape
    frames = samples // WIN
    group = 16

    def fetch(r):
        return pltpu.make_async_copy(x_hbm.at[pl.ds(r * chans, chans), :], x_ref.at[r], in_sem.at[r])

    def put(r):
        return pltpu.make_async_copy(out_ref.at[r], out_hbm.at[r // 4, :, :, r % 4], out_sem.at[r])

    for r in range(blocks):
        fetch(r).start()
    table = table_ref[...]

    @pl.loop(0, blocks)
    def _(r):
        fetch(r).wait()
        for g in range(frames // group):
            x = jnp.concatenate(
                [x_ref[r, :, (g * group + f) * WIN : (g * group + f + 1) * WIN] for f in range(group)], axis=0
            )
            spec = jnp.dot(x, table, preferred_element_type=jnp.float32)
            re, im = spec[:, :BINS], spec[:, BINS:]
            energy = (re * re + im * im).reshape(group, chans, BINS)
            energy = pltpu.einshape("fcb->cfb", energy).astype(jnp.bfloat16)
            for c in range(chans):
                zl, y, core, j = c // 16, (c // 4) % 4, (c // 2) % 2, c % 2
                at = (y * 2 + j) * BINS
                out_ref[r, zl, core, g * group : (g + 1) * group, at : at + BINS] = energy[c]
        put(r).start()

    for r in range(blocks):
        put(r).wait()


def energies(record, table):
    channels, samples = record.shape
    frames = samples // WIN
    per_row = channels // N_R
    rows = channels * BINS // (2 * N_P)
    return pl.pallas_call(
        energy_kernel,
        in_specs=[pl.BlockSpec(memory_space=pl.ANY), pl.BlockSpec(memory_space=pltpu.VMEM)],
        out_specs=pl.BlockSpec(memory_space=pl.ANY),
        out_shape=jax.ShapeDtypeStruct((2, 2, 2, 4, frames, rows), jnp.bfloat16),
        scratch_shapes=[
            pltpu.VMEM((N_R, per_row, samples), jnp.bfloat16),
            pltpu.VMEM((N_R, 2, 2, frames, rows), jnp.bfloat16),
            pltpu.SemaphoreType.DMA((N_R,)),
            pltpu.SemaphoreType.DMA((N_R,)),
        ],
        compiler_params=pltpu.CompilerParams(vmem_limit_bytes=58 << 20),
        cost_estimate=pl.CostEstimate(
            flops=2 * channels * frames * WIN * WIN, bytes_accessed=12 << 20, transcendentals=0
        ),
        name="energy",
    )(record, table)


def level(x, high):
    relative = jnp.where(high == 0.0, 0.0, (x - high) / high)
    return jnp.clip(jnp.floor(relative * (7.0 * 256.0) + 0.5), -7.0, 7.0) + 7.0


def coded(a, b):
    high_a, high_b = [x.astype(jnp.bfloat16).astype(jnp.float32) for x in (a, b)]
    return high_a, high_b, level(a, high_a) * 15.0 + level(b, high_b)


def decoded(high_a, high_b, code):
    first = jnp.floor((code + 0.5) * (1.0 / 15.0))
    second = code - 15.0 * first
    return [high + high * ((q - 7.0) * (1.0 / (7.0 * 256.0))) for high, q in ((high_a, first), (high_b, second))]


def hi_lo(x):
    high = x.astype(jnp.bfloat16).astype(jnp.float32)
    return jnp.concatenate([high, x - high], axis=0).astype(jnp.bfloat16)


def sweep_kernel(first, at_ref, s_hbm, h_ref, w0, w1, w2, w3, *refs):
    before, (n0, n1, n2, n3, sums_ref, ht_ref, s_ref, sem) = (() if first else refs[:4]), refs[-8:]
    blocks, half = h_ref.shape[2], h_ref.shape[4]
    rank, span = ht_ref.shape[1], blocks * half
    run = half // 2
    core = at_ref[0 if first else 1]

    def fetch(p, t, i):
        row = ((i % 2 * blocks + i // 2) * 2 + core) * run
        column = lax.rem(at_ref[2] + 2 * p + t, N_Y) * rank
        return pltpu.make_async_copy(
            s_hbm.at[pl.ds(pl.multiple_of(row, run), run), pl.ds(pl.multiple_of(column, rank), rank)],
            s_ref.at[p, i * run : (i + 1) * run, t * rank : (t + 1) * rank],
            sem.at[p, t, i],
        )

    pieces = [(t, i) for t in range(2) for i in range(2 * blocks)]
    for p in range(2):
        for t, i in pieces:
            fetch(p, t, i).start()
    h = [jnp.concatenate([h_ref[x, zh, b] for zh in range(2) for x in range(4)], axis=0) for b in range(blocks)]
    for b in range(blocks):
        ht_ref[b * half : (b + 1) * half, :] = h[b].T
    rowsum = jnp.dot(jnp.ones((8, span), jnp.bfloat16), ht_ref[...], preferred_element_type=jnp.float32)
    colsum = jnp.zeros((rank, 1), jnp.float32)
    for p in range(2):
        wt = jnp.concatenate([w[...] for w in ((w0, w1), (w2, w3))[p]], axis=0).T
        colsum = colsum + jnp.sum(wt.astype(jnp.float32), axis=1, keepdims=True)
        recon = jnp.dot(ht_ref[...], wt, preferred_element_type=jnp.float32)
        for t, i in pieces:
            fetch(p, t, i).wait()
        quotient = (s_ref[p].astype(jnp.float32) / recon).astype(jnp.bfloat16)
        hn = lax.dot_general(wt, quotient, (((1,), (1,)), ((), ())), preferred_element_type=jnp.float32)
        if p == 0:
            sums_ref[:, :span] = hn
        else:
            sums_ref[:, :span] += hn
        wn = None
        for b in range(blocks):
            part = jnp.dot(h[b], quotient[b * half : (b + 1) * half], preferred_element_type=jnp.float32)
            wn = part if wn is None else wn + part
        for t in range(2):
            ref = (n0, n1, n2, n3)[2 * p + t]
            part = wn[:, t * rank : (t + 1) * rank]
            if first:
                ref[:rank, :] = part
                ref[rank:, :] = rowsum
                continue
            part = part + before[2 * p + t][:rank, :]
            total = rowsum + before[2 * p + t][rank:, :]
            if p == 0 and t == 0:
                ref[:rank, :] = part
                ref[rank:, :] = total
                continue
            high_a, high_b, code = coded(part[: rank // 2], part[rank // 2 :])
            ref[: rank // 2, :] = high_a.astype(jnp.bfloat16)
            ref[rank // 2 : rank, :] = high_b.astype(jnp.bfloat16)
            ref[rank : rank + rank // 2, :] = code.astype(jnp.bfloat16)
            ref[rank + rank // 2 :, :] = hi_lo(total)
    sums_ref[:, span:] = jnp.broadcast_to(colsum, (rank, LANES))


def half_sweep(at, spectra, h, ws, before=()):
    frames, rows = spectra.shape
    blocks, half, rank = h.shape[2], h.shape[4], ws[0].shape[1]
    return pl.pallas_call(
        functools.partial(sweep_kernel, not before),
        in_specs=whole(1, pltpu.SMEM) + whole(1, pl.ANY) + whole(5 + len(before)),
        out_specs=whole(5),
        out_shape=[jax.ShapeDtypeStruct((rank + 8, rank), jnp.float32)]
        + [
            jax.ShapeDtypeStruct((rank + rank // 2 + 16, rank), jnp.bfloat16)
            if before
            else jax.ShapeDtypeStruct((rank + 8, rank), jnp.float32)
        ]
        * 3
        + [jax.ShapeDtypeStruct((rank, blocks * half + LANES), jnp.float32)],
        scratch_shapes=[
            pltpu.VMEM((blocks * half, rank), jnp.bfloat16),
            pltpu.VMEM((2, blocks * half, 2 * rank), jnp.bfloat16),
            pltpu.SemaphoreType.DMA((2, 2, 2 * blocks)),
        ],
        compiler_params=pltpu.CompilerParams(vmem_limit_bytes=28 << 20),
        cost_estimate=pl.CostEstimate(flops=3 * frames * rows * rank, bytes_accessed=4 << 20, transcendentals=0),
        name="sweep_a" if not before else "sweep_b",
    )(at, spectra, h, *ws, *before)


def pair_kernel(a_ref, b_ref, out_ref):
    each = (out_ref.shape[1] - 2 * TAIL) // 6
    half, span = 4 * LANES, a_ref.shape[1] - LANES
    group = lax.broadcasted_iota(jnp.int32, (TAIL, LANES), 1) // each
    for r in range(N_R):
        rows, at = slice(r * each, (r + 1) * each), (r % 4 * 2 + r // 4) * 2
        sums = a_ref[rows, span:] + b_ref[rows, span:]
        tail = sums[:TAIL]
        for j in range(1, each // TAIL):
            tail = jnp.where(group == j, sums[j * TAIL : (j + 1) * TAIL], tail)
        for zl in range(2):
            parts = []
            for c in range(4):
                columns = slice(zl * half + c * LANES, zl * half + (c + 1) * LANES)
                parts.append(a_ref[rows, columns] + b_ref[rows, columns])
            codes = []
            for c in (0, 2):
                high_a, high_b, code = coded(parts[c], parts[c + 1])
                out_ref[at + zl, c * each : (c + 1) * each, :] = high_a.astype(jnp.bfloat16)
                out_ref[at + zl, (c + 1) * each : (c + 2) * each, :] = high_b.astype(jnp.bfloat16)
                codes.append(code.astype(jnp.bfloat16))
            out_ref[at + zl, 4 * each : 6 * each, :] = jnp.concatenate(codes, axis=0)
            out_ref[at + zl, 6 * each :, :] = hi_lo(tail)


def pair(a, b, each):
    return pl.pallas_call(
        pair_kernel,
        in_specs=whole(2),
        out_specs=whole(1)[0],
        out_shape=jax.ShapeDtypeStruct((N_P, 6 * each + 2 * TAIL, LANES), jnp.bfloat16),
        compiler_params=pltpu.CompilerParams(vmem_limit_bytes=12 << 20),
        name="pair",
    )(a, b)


def h_update_kernel(parts_ref, h_ref, new_ref, *low_refs):
    each = h_ref.shape[0]
    blocks, tail = [0.0] * 4, 0.0
    for i in range(N_P):
        part = parts_ref[i].astype(jnp.float32)
        pieces = [part[c * each : (c + 1) * each] for c in range(6)]
        values = decoded(*pieces[0:2], pieces[4]) + decoded(*pieces[2:4], pieces[5])
        blocks = [block + value for block, value in zip(blocks, values)]
        tail = tail + part[6 * each :]
    numer = jnp.concatenate(blocks, axis=1)
    tail = tail[:TAIL] + tail[TAIL:]
    colsum = jnp.concatenate([tail[:, j * each : j * each + 1] for j in range(each // TAIL)], axis=0)
    new = h_ref[...] * numer / colsum
    new_ref[...] = new
    low = new.astype(jnp.bfloat16)
    for low_ref in low_refs:
        for i in range(N_P):
            low_ref[i] = low


def h_update(parts, h, more):
    return pl.pallas_call(
        h_update_kernel,
        in_specs=whole(2),
        out_specs=whole(1 + more),
        out_shape=[jax.ShapeDtypeStruct(h.shape, jnp.float32)]
        + [jax.ShapeDtypeStruct((N_P, *h.shape), jnp.bfloat16)] * more,
        compiler_params=pltpu.CompilerParams(vmem_limit_bytes=12 << 20),
        name="h_update",
    )(parts, h)


def w_update_kernel(p0, p1, p2, p3, w_ref, new_ref, *low_refs):
    rank = w_ref.shape[1]
    cut = rank // 2
    tops, bottoms, rowsum = p0[:cut, :], p0[cut:rank, :], p0[rank : rank + 1, :]
    for ref in (p1, p2, p3):
        part = ref[...].astype(jnp.float32)
        top, bottom = decoded(part[:cut], part[cut:rank], part[rank : rank + cut])
        tops, bottoms = tops + top, bottoms + bottom
        rowsum = rowsum + part[rank + cut : rank + cut + 1] + part[rank + cut + 8 : rank + cut + 9]
    new = w_ref[...] * jnp.concatenate([tops, bottoms], axis=0).T / rowsum
    new_ref[...] = new
    for low_ref in low_refs:
        low_ref[...] = new.astype(jnp.bfloat16)


def w_update(parts, w, more):
    return pl.pallas_call(
        w_update_kernel,
        in_specs=whole(5),
        out_specs=whole(1 + more),
        out_shape=[jax.ShapeDtypeStruct(w.shape, jnp.float32)] + [jax.ShapeDtypeStruct(w.shape, jnp.bfloat16)] * more,
        compiler_params=pltpu.CompilerParams(vmem_limit_bytes=12 << 20),
        name="w_update",
    )(*parts, w)


def spread_kernel(h_hbm, out_hbm, h_ref, low_ref, in_sem, out_sem):
    fetch = pltpu.make_async_copy(h_hbm, h_ref, in_sem)
    fetch.start()
    fetch.wait()
    low_ref[...] = h_ref[...].astype(jnp.bfloat16)
    puts = [pltpu.make_async_copy(low_ref, out_hbm.at[i], out_sem.at[i]) for i in range(N_P)]
    for put in puts:
        put.start()
    for put in puts:
        put.wait()


def spread(h):
    return pl.pallas_call(
        spread_kernel,
        in_specs=whole(1, pl.ANY),
        out_specs=whole(1, pl.ANY)[0],
        out_shape=jax.ShapeDtypeStruct((N_P, *h.shape), jnp.bfloat16),
        scratch_shapes=[
            pltpu.VMEM(h.shape, jnp.float32),
            pltpu.VMEM(h.shape, jnp.bfloat16),
            pltpu.SemaphoreType.DMA,
            pltpu.SemaphoreType.DMA((N_P,)),
        ],
        compiler_params=pltpu.CompilerParams(vmem_limit_bytes=56 << 20),
        name="spread",
    )(h)


def exchange(x, axes):
    return lax.all_to_all(x, axes, 0, 0, tiled=True)


def from_sibling(x):
    return lax.ppermute(x, "core", [(0, 1), (1, 0)])


def sent_ahead(x, t):
    return lax.ppermute(x, "y", [(i, (i + t) % N_Y) for i in range(N_Y)])


def taken_ahead(x):
    return [x] + [lax.ppermute(x, "y", [(i, (i - t) % N_Y) for i in range(N_Y)]) for t in range(1, N_Y)]


def local(samples, w, h):
    record = samples.reshape(samples.shape[2], samples.shape[3])
    core, y = lax.axis_index("core"), lax.axis_index("y")
    at = jnp.stack([1 - core, core, y]).astype(jnp.int32)
    h_own = exchange(spread(h), RANKS).reshape(4, 2, 2, *h.shape)
    energy = energies(record, dft_table())
    frames, rows = energy.shape[4:]
    energy, w_low = lax.optimization_barrier((energy, w.astype(jnp.bfloat16)))
    ws = taken_ahead(w_low)
    h_oth = from_sibling(h_own)
    spectra = exchange(energy.reshape(2 * N_P, frames, rows), TILE).reshape(2 * N_P * frames, rows)
    for step in range(ITERS):
        *parts, s_oth = half_sweep(at, spectra, h_oth, ws)
        s_got = from_sibling(s_oth)
        n0, n1, n2, n3, s_own = half_sweep(at, spectra, h_own, ws, parts)
        w_parts = [n0] + [sent_ahead(n, t + 1) for t, n in enumerate((n1, n2, n3))]
        h_parts = exchange(pair(s_own, s_got, h.shape[0]), RANKS)
        more = step + 1 < ITERS
        h, *low = h_update(h_parts, h, more)
        if low:
            w_parts, low, h = lax.optimization_barrier((w_parts, low, h))
        w, *w_low = w_update(w_parts, w, more)
        if more:
            ws = taken_ahead(*w_low)
            ws, h_own = lax.optimization_barrier((ws, exchange(*low, RANKS)))
            h_own = h_own.reshape(4, 2, 2, *h.shape)
            h_oth = from_sibling(h_own)
    return (w, h)


def solution(mesh):
    fine = Mesh(mesh.devices.reshape(SIZES), AXES)
    row, col = ("zh", "x"), ("zl", "y", "core")
    return jax.shard_map(
        local,
        mesh=fine,
        in_specs=(P(col, row, None, None), P(row + col, None), P(row, col)),
        out_specs=(P(row + col, None), P(row, col)),
        check_vma=False,
    )
```

```python
import functools
import math

import jax
import jax.numpy as jnp
import numpy as np
from jax import lax
from jax.experimental import pallas as pl
from jax.experimental.pallas import tpu as pltpu
from jax.sharding import Mesh
from jax.sharding import PartitionSpec as P

BINS = 128
ITERS = 2
WIN = 256

AXES = ("zh", "x", "zl", "y", "core")
SIZES = (2, 4, 2, 4, 2)
TILE = ("zh", "zl", "core", "x")
RANKS = ("x", "zh", "zl")
N_Y = 4
N_R = 8
N_P = 16
LANES = 128
TAIL = 8


def dft_table():
    n = np.arange(WIN, dtype=np.int32)
    k = np.arange(BINS, dtype=np.int32)
    phases = (n[:, None] * k[None, :] % WIN).astype(np.float32) * np.float32(2.0 * math.pi / WIN)
    taper = np.float32(0.5) - np.float32(0.5) * np.cos(n.astype(np.float32) * np.float32(2.0 * math.pi / WIN))
    taper = (taper / np.float32(math.sqrt(3.0 * WIN / 8.0))).astype(np.float32)
    both = np.concatenate([taper[:, None] * np.cos(phases), -taper[:, None] * np.sin(phases)], axis=1)
    return jnp.asarray(both.astype(np.float32)).astype(jnp.bfloat16)


def whole(n, space=pltpu.VMEM):
    return [pl.BlockSpec(memory_space=space)] * n


def energy_kernel(x_hbm, table_ref, out_hbm, x_ref, out_ref, in_sem, out_sem):
    blocks, chans, samples = x_ref.shape
    frames = samples // WIN
    group = 16

    def fetch(r):
        return pltpu.make_async_copy(x_hbm.at[pl.ds(r * chans, chans), :], x_ref.at[r], in_sem.at[r])

    def put(r):
        return pltpu.make_async_copy(out_ref.at[r], out_hbm.at[r // 4, :, :, r % 4], out_sem.at[r])

    for r in range(blocks):
        fetch(r).start()
    table = table_ref[...]

    @pl.loop(0, blocks)
    def _(r):
        fetch(r).wait()
        for g in range(frames // group):
            x = jnp.concatenate(
                [x_ref[r, :, (g * group + f) * WIN : (g * group + f + 1) * WIN] for f in range(group)], axis=0
            )
            spec = jnp.dot(x, table, preferred_element_type=jnp.float32)
            re, im = spec[:, :BINS], spec[:, BINS:]
            energy = (re * re + im * im).reshape(group, chans, BINS)
            energy = pltpu.einshape("fcb->cfb", energy).astype(jnp.bfloat16)
            for c in range(chans):
                zl, y, core, j = c // 16, (c // 4) % 4, (c // 2) % 2, c % 2
                at = (y * 2 + j) * BINS
                out_ref[r, zl, core, g * group : (g + 1) * group, at : at + BINS] = energy[c]
        put(r).start()

    for r in range(blocks):
        put(r).wait()


def energies(record, table):
    channels, samples = record.shape
    frames = samples // WIN
    per_row = channels // N_R
    rows = channels * BINS // (2 * N_P)
    return pl.pallas_call(
        energy_kernel,
        in_specs=[pl.BlockSpec(memory_space=pl.ANY), pl.BlockSpec(memory_space=pltpu.VMEM)],
        out_specs=pl.BlockSpec(memory_space=pl.ANY),
        out_shape=jax.ShapeDtypeStruct((2, 2, 2, 4, frames, rows), jnp.bfloat16),
        scratch_shapes=[
            pltpu.VMEM((N_R, per_row, samples), jnp.bfloat16),
            pltpu.VMEM((N_R, 2, 2, frames, rows), jnp.bfloat16),
            pltpu.SemaphoreType.DMA((N_R,)),
            pltpu.SemaphoreType.DMA((N_R,)),
        ],
        compiler_params=pltpu.CompilerParams(vmem_limit_bytes=58 << 20),
        cost_estimate=pl.CostEstimate(
            flops=2 * channels * frames * WIN * WIN, bytes_accessed=12 << 20, transcendentals=0
        ),
        name="energy",
    )(record, table)


def level(x, high):
    relative = jnp.where(high == 0.0, 0.0, (x - high) / high)
    return jnp.clip(jnp.floor(relative * (7.0 * 256.0) + 0.5), -7.0, 7.0) + 7.0


def coded(a, b):
    high_a, high_b = [x.astype(jnp.bfloat16).astype(jnp.float32) for x in (a, b)]
    return high_a, high_b, level(a, high_a) * 15.0 + level(b, high_b)


def decoded(high_a, high_b, code):
    first = jnp.floor((code + 0.5) * (1.0 / 15.0))
    second = code - 15.0 * first
    return [high + high * ((q - 7.0) * (1.0 / (7.0 * 256.0))) for high, q in ((high_a, first), (high_b, second))]


def hi_lo(x):
    high = x.astype(jnp.bfloat16).astype(jnp.float32)
    return jnp.concatenate([high, x - high], axis=0).astype(jnp.bfloat16)


def sweep_kernel(first, at_ref, s_hbm, h_ref, w0, w1, w2, w3, *refs):
    before, (n0, n1, n2, n3, sums_ref, ht_ref, s_ref, sem) = (() if first else refs[:4]), refs[-8:]
    blocks, half = h_ref.shape[2], h_ref.shape[4]
    rank, span = ht_ref.shape[1], blocks * half
    run = half // 2
    core = at_ref[0 if first else 1]

    def fetch(p, t, i):
        row = ((i % 2 * blocks + i // 2) * 2 + core) * run
        column = lax.rem(at_ref[2] + 2 * p + t, N_Y) * rank
        return pltpu.make_async_copy(
            s_hbm.at[pl.ds(pl.multiple_of(row, run), run), pl.ds(pl.multiple_of(column, rank), rank)],
            s_ref.at[p, i * run : (i + 1) * run, t * rank : (t + 1) * rank],
            sem.at[p, t, i],
        )

    pieces = [(t, i) for t in range(2) for i in range(2 * blocks)]
    for p in range(2):
        for t, i in pieces:
            fetch(p, t, i).start()
    h = [jnp.concatenate([h_ref[x, zh, b] for zh in range(2) for x in range(4)], axis=0) for b in range(blocks)]
    for b in range(blocks):
        ht_ref[b * half : (b + 1) * half, :] = h[b].T
    rowsum = jnp.dot(jnp.ones((8, span), jnp.bfloat16), ht_ref[...], preferred_element_type=jnp.float32)
    colsum = jnp.zeros((rank, 1), jnp.float32)
    for p in range(2):
        wt = jnp.concatenate([w[...] for w in ((w0, w1), (w2, w3))[p]], axis=0).T
        colsum = colsum + jnp.sum(wt.astype(jnp.float32), axis=1, keepdims=True)
        recon = jnp.dot(ht_ref[...], wt, preferred_element_type=jnp.float32)
        for t, i in pieces:
            fetch(p, t, i).wait()
        quotient = (s_ref[p].astype(jnp.float32) / recon).astype(jnp.bfloat16)
        hn = lax.dot_general(wt, quotient, (((1,), (1,)), ((), ())), preferred_element_type=jnp.float32)
        if p == 0:
            sums_ref[:, :span] = hn
        else:
            sums_ref[:, :span] += hn
        wn = None
        for b in range(blocks):
            part = jnp.dot(h[b], quotient[b * half : (b + 1) * half], preferred_element_type=jnp.float32)
            wn = part if wn is None else wn + part
        for t in range(2):
            ref = (n0, n1, n2, n3)[2 * p + t]
            part = wn[:, t * rank : (t + 1) * rank]
            if first:
                ref[:rank, :] = part
                ref[rank:, :] = rowsum
                continue
            part = part + before[2 * p + t][:rank, :]
            total = rowsum + before[2 * p + t][rank:, :]
            if p == 0 and t == 0:
                ref[:rank, :] = part
                ref[rank:, :] = total
                continue
            high_a, high_b, code = coded(part[: rank // 2], part[rank // 2 :])
            ref[: rank // 2, :] = high_a.astype(jnp.bfloat16)
            ref[rank // 2 : rank, :] = high_b.astype(jnp.bfloat16)
            ref[rank : rank + rank // 2, :] = code.astype(jnp.bfloat16)
            ref[rank + rank // 2 :, :] = hi_lo(total)
    sums_ref[:, span:] = jnp.broadcast_to(colsum, (rank, LANES))


def half_sweep(at, spectra, h, ws, before=()):
    frames, rows = spectra.shape
    blocks, half, rank = h.shape[2], h.shape[4], ws[0].shape[1]
    return pl.pallas_call(
        functools.partial(sweep_kernel, not before),
        in_specs=whole(1, pltpu.SMEM) + whole(1, pl.ANY) + whole(5 + len(before)),
        out_specs=whole(5),
        out_shape=[jax.ShapeDtypeStruct((rank + 8, rank), jnp.float32)]
        + [
            jax.ShapeDtypeStruct((rank + rank // 2 + 16, rank), jnp.bfloat16)
            if before
            else jax.ShapeDtypeStruct((rank + 8, rank), jnp.float32)
        ]
        * 3
        + [jax.ShapeDtypeStruct((rank, blocks * half + LANES), jnp.float32)],
        scratch_shapes=[
            pltpu.VMEM((blocks * half, rank), jnp.bfloat16),
            pltpu.VMEM((2, blocks * half, 2 * rank), jnp.bfloat16),
            pltpu.SemaphoreType.DMA((2, 2, 2 * blocks)),
        ],
        compiler_params=pltpu.CompilerParams(vmem_limit_bytes=28 << 20),
        cost_estimate=pl.CostEstimate(flops=3 * frames * rows * rank, bytes_accessed=4 << 20, transcendentals=0),
        name="sweep_a" if not before else "sweep_b",
    )(at, spectra, h, *ws, *before)


def pair_kernel(a_ref, b_ref, out_ref):
    each = (out_ref.shape[1] - 2 * TAIL) // 6
    half, span = 4 * LANES, a_ref.shape[1] - LANES
    group = lax.broadcasted_iota(jnp.int32, (TAIL, LANES), 1) // each
    for r in range(N_R):
        rows, at = slice(r * each, (r + 1) * each), (r % 4 * 2 + r // 4) * 2
        sums = a_ref[rows, span:] + b_ref[rows, span:]
        tail = sums[:TAIL]
        for j in range(1, each // TAIL):
            tail = jnp.where(group == j, sums[j * TAIL : (j + 1) * TAIL], tail)
        for zl in range(2):
            parts = []
            for c in range(4):
                columns = slice(zl * half + c * LANES, zl * half + (c + 1) * LANES)
                parts.append(a_ref[rows, columns] + b_ref[rows, columns])
            codes = []
            for c in (0, 2):
                high_a, high_b, code = coded(parts[c], parts[c + 1])
                out_ref[at + zl, c * each : (c + 1) * each, :] = high_a.astype(jnp.bfloat16)
                out_ref[at + zl, (c + 1) * each : (c + 2) * each, :] = high_b.astype(jnp.bfloat16)
                codes.append(code.astype(jnp.bfloat16))
            out_ref[at + zl, 4 * each : 6 * each, :] = jnp.concatenate(codes, axis=0)
            out_ref[at + zl, 6 * each :, :] = hi_lo(tail)


def pair(a, b, each):
    return pl.pallas_call(
        pair_kernel,
        in_specs=whole(2),
        out_specs=whole(1)[0],
        out_shape=jax.ShapeDtypeStruct((N_P, 6 * each + 2 * TAIL, LANES), jnp.bfloat16),
        compiler_params=pltpu.CompilerParams(vmem_limit_bytes=12 << 20),
        name="pair",
    )(a, b)


def h_update_kernel(parts_ref, h_ref, new_ref, *low_refs):
    each = h_ref.shape[0]
    blocks, tail = [0.0] * 4, 0.0
    for i in range(N_P):
        part = parts_ref[i].astype(jnp.float32)
        pieces = [part[c * each : (c + 1) * each] for c in range(6)]
        values = decoded(*pieces[0:2], pieces[4]) + decoded(*pieces[2:4], pieces[5])
        blocks = [block + value for block, value in zip(blocks, values)]
        tail = tail + part[6 * each :]
    numer = jnp.concatenate(blocks, axis=1)
    tail = tail[:TAIL] + tail[TAIL:]
    colsum = jnp.concatenate([tail[:, j * each : j * each + 1] for j in range(each // TAIL)], axis=0)
    new = h_ref[...] * numer / colsum
    new_ref[...] = new
    low = new.astype(jnp.bfloat16)
    for low_ref in low_refs:
        for i in range(N_P):
            low_ref[i] = low


def h_update(parts, h, more):
    return pl.pallas_call(
        h_update_kernel,
        in_specs=whole(2),
        out_specs=whole(1 + more),
        out_shape=[jax.ShapeDtypeStruct(h.shape, jnp.float32)]
        + [jax.ShapeDtypeStruct((N_P, *h.shape), jnp.bfloat16)] * more,
        compiler_params=pltpu.CompilerParams(vmem_limit_bytes=12 << 20),
        name="h_update",
    )(parts, h)


def w_update_kernel(p0, p1, p2, p3, w_ref, new_ref, *low_refs):
    rank = w_ref.shape[1]
    cut = rank // 2
    tops, bottoms, rowsum = p0[:cut, :], p0[cut:rank, :], p0[rank : rank + 1, :]
    for ref in (p1, p2, p3):
        part = ref[...].astype(jnp.float32)
        top, bottom = decoded(part[:cut], part[cut:rank], part[rank : rank + cut])
        tops, bottoms = tops + top, bottoms + bottom
        rowsum = rowsum + part[rank + cut : rank + cut + 1] + part[rank + cut + 8 : rank + cut + 9]
    new = w_ref[...] * jnp.concatenate([tops, bottoms], axis=0).T / rowsum
    new_ref[...] = new
    for low_ref in low_refs:
        low_ref[...] = new.astype(jnp.bfloat16)


def w_update(parts, w, more):
    return pl.pallas_call(
        w_update_kernel,
        in_specs=whole(5),
        out_specs=whole(1 + more),
        out_shape=[jax.ShapeDtypeStruct(w.shape, jnp.float32)] + [jax.ShapeDtypeStruct(w.shape, jnp.bfloat16)] * more,
        compiler_params=pltpu.CompilerParams(vmem_limit_bytes=12 << 20),
        name="w_update",
    )(*parts, w)


def spread_kernel(h_hbm, out_hbm, h_ref, low_ref, in_sem, out_sem):
    fetch = pltpu.make_async_copy(h_hbm, h_ref, in_sem)
    fetch.start()
    fetch.wait()
    low_ref[...] = h_ref[...].astype(jnp.bfloat16)
    puts = [pltpu.make_async_copy(low_ref, out_hbm.at[i], out_sem.at[i]) for i in range(N_P)]
    for put in puts:
        put.start()
    for put in puts:
        put.wait()


def spread(h):
    return pl.pallas_call(
        spread_kernel,
        in_specs=whole(1, pl.ANY),
        out_specs=whole(1, pl.ANY)[0],
        out_shape=jax.ShapeDtypeStruct((N_P, *h.shape), jnp.bfloat16),
        scratch_shapes=[
            pltpu.VMEM(h.shape, jnp.float32),
            pltpu.VMEM(h.shape, jnp.bfloat16),
            pltpu.SemaphoreType.DMA,
            pltpu.SemaphoreType.DMA((N_P,)),
        ],
        compiler_params=pltpu.CompilerParams(vmem_limit_bytes=56 << 20),
        name="spread",
    )(h)


def exchange(x, axes):
    return lax.all_to_all(x, axes, 0, 0, tiled=True)


def from_sibling(x):
    return lax.ppermute(x, "core", [(0, 1), (1, 0)])


def sent_ahead(x, t):
    return lax.ppermute(x, "y", [(i, (i + t) % N_Y) for i in range(N_Y)])


def taken_ahead(x):
    return [x] + [lax.ppermute(x, "y", [(i, (i - t) % N_Y) for i in range(N_Y)]) for t in range(1, N_Y)]


def local(samples, w, h):
    record = samples.reshape(samples.shape[2], samples.shape[3])
    core, y = lax.axis_index("core"), lax.axis_index("y")
    at = jnp.stack([1 - core, core, y]).astype(jnp.int32)
    h_own = exchange(spread(h), RANKS).reshape(4, 2, 2, *h.shape)
    energy = energies(record, dft_table())
    frames, rows = energy.shape[4:]
    energy, ws = lax.optimization_barrier((energy, taken_ahead(w.astype(jnp.bfloat16))))
    h_oth = from_sibling(h_own)
    spectra = exchange(energy.reshape(2 * N_P, frames, rows), TILE).reshape(2 * N_P * frames, rows)
    for step in range(ITERS):
        *parts, s_oth = half_sweep(at, spectra, h_oth, ws)
        s_got = from_sibling(s_oth)
        n0, n1, n2, n3, s_own = half_sweep(at, spectra, h_own, ws, parts)
        w_parts = [n0] + [sent_ahead(n, t + 1) for t, n in enumerate((n1, n2, n3))]
        h_parts = exchange(pair(s_own, s_got, h.shape[0]), RANKS)
        more = step + 1 < ITERS
        h, *low = h_update(h_parts, h, more)
        if low:
            w_parts, low, h = lax.optimization_barrier((w_parts, low, h))
        w, *w_low = w_update(w_parts, w, more)
        if more:
            ws = taken_ahead(*w_low)
            ws, h_own = lax.optimization_barrier((ws, exchange(*low, RANKS)))
            h_own = h_own.reshape(4, 2, 2, *h.shape)
            h_oth = from_sibling(h_own)
    return (w, h)


def solution(mesh):
    fine = Mesh(mesh.devices.reshape(SIZES), AXES)
    row, col = ("zh", "x"), ("zl", "y", "core")
    return jax.shard_map(
        local,
        mesh=fine,
        in_specs=(P(col, row, None, None), P(row + col, None), P(row, col)),
        out_specs=(P(row + col, None), P(row, col)),
        check_vma=False,
    )
```

```python
import functools
import math

import jax
import jax.numpy as jnp
import numpy as np
from jax import lax
from jax.experimental import pallas as pl
from jax.experimental.pallas import tpu as pltpu
from jax.sharding import Mesh
from jax.sharding import PartitionSpec as P

BINS = 128
ITERS = 2
WIN = 256

AXES = ("zh", "x", "zl", "y", "core")
SIZES = (2, 4, 2, 4, 2)
TILE = ("zh", "zl", "core", "x")
RANKS = ("x", "zh", "zl")
N_Y = 4
N_R = 8
N_P = 16
LANES = 128
TAIL = 8


def dft_table():
    n = np.arange(WIN, dtype=np.int32)
    k = np.arange(BINS, dtype=np.int32)
    phases = (n[:, None] * k[None, :] % WIN).astype(np.float32) * np.float32(2.0 * math.pi / WIN)
    taper = np.float32(0.5) - np.float32(0.5) * np.cos(n.astype(np.float32) * np.float32(2.0 * math.pi / WIN))
    taper = (taper / np.float32(math.sqrt(3.0 * WIN / 8.0))).astype(np.float32)
    both = np.concatenate([taper[:, None] * np.cos(phases), -taper[:, None] * np.sin(phases)], axis=1)
    return jnp.asarray(both.astype(np.float32)).astype(jnp.bfloat16)


def whole(n, space=pltpu.VMEM):
    return [pl.BlockSpec(memory_space=space)] * n


def energy_kernel(x_hbm, table_ref, out_hbm, x_ref, out_ref, in_sem, out_sem):
    blocks, chans, samples = x_ref.shape
    frames = samples // WIN
    group = 16

    def fetch(r):
        return pltpu.make_async_copy(x_hbm.at[pl.ds(r * chans, chans), :], x_ref.at[r], in_sem.at[r])

    def put(r):
        return pltpu.make_async_copy(out_ref.at[r], out_hbm.at[r // 4, :, :, r % 4], out_sem.at[r])

    for r in range(blocks):
        fetch(r).start()
    table = table_ref[...]

    @pl.loop(0, blocks)
    def _(r):
        fetch(r).wait()
        for g in range(frames // group):
            x = jnp.concatenate(
                [x_ref[r, :, (g * group + f) * WIN : (g * group + f + 1) * WIN] for f in range(group)], axis=0
            )
            spec = jnp.dot(x, table, preferred_element_type=jnp.float32)
            re, im = spec[:, :BINS], spec[:, BINS:]
            energy = (re * re + im * im).reshape(group, chans, BINS)
            energy = pltpu.einshape("fcb->cfb", energy).astype(jnp.bfloat16)
            for c in range(chans):
                zl, y, core, j = c // 16, (c // 4) % 4, (c // 2) % 2, c % 2
                at = (y * 2 + j) * BINS
                out_ref[r, zl, core, g * group : (g + 1) * group, at : at + BINS] = energy[c]
        put(r).start()

    for r in range(blocks):
        put(r).wait()


def energies(record, table):
    channels, samples = record.shape
    frames = samples // WIN
    per_row = channels // N_R
    rows = channels * BINS // (2 * N_P)
    return pl.pallas_call(
        energy_kernel,
        in_specs=[pl.BlockSpec(memory_space=pl.ANY), pl.BlockSpec(memory_space=pltpu.VMEM)],
        out_specs=pl.BlockSpec(memory_space=pl.ANY),
        out_shape=jax.ShapeDtypeStruct((2, 2, 2, 4, frames, rows), jnp.bfloat16),
        scratch_shapes=[
            pltpu.VMEM((N_R, per_row, samples), jnp.bfloat16),
            pltpu.VMEM((N_R, 2, 2, frames, rows), jnp.bfloat16),
            pltpu.SemaphoreType.DMA((N_R,)),
            pltpu.SemaphoreType.DMA((N_R,)),
        ],
        compiler_params=pltpu.CompilerParams(vmem_limit_bytes=58 << 20),
        cost_estimate=pl.CostEstimate(
            flops=2 * channels * frames * WIN * WIN, bytes_accessed=12 << 20, transcendentals=0
        ),
        name="energy",
    )(record, table)


def level(x, high):
    relative = jnp.where(high == 0.0, 0.0, (x - high) / high)
    return jnp.clip(jnp.floor(relative * (7.0 * 256.0) + 0.5), -7.0, 7.0) + 7.0


def coded(a, b):
    high_a, high_b = [x.astype(jnp.bfloat16).astype(jnp.float32) for x in (a, b)]
    return high_a, high_b, level(a, high_a) * 15.0 + level(b, high_b)


def decoded(high_a, high_b, code):
    first = jnp.floor((code + 0.5) * (1.0 / 15.0))
    second = code - 15.0 * first
    return [high + high * ((q - 7.0) * (1.0 / (7.0 * 256.0))) for high, q in ((high_a, first), (high_b, second))]


def hi_lo(x):
    high = x.astype(jnp.bfloat16).astype(jnp.float32)
    return jnp.concatenate([high, x - high], axis=0).astype(jnp.bfloat16)


def sweep_kernel(first, at_ref, s_hbm, h_ref, w0, w1, w2, w3, *refs):
    before, (n0, n1, n2, n3, sums_ref, ht_ref, s_ref, sem) = (() if first else refs[:4]), refs[-8:]
    blocks, half = h_ref.shape[2], h_ref.shape[4]
    rank, span = ht_ref.shape[1], blocks * half
    run = half // 2
    core = at_ref[0 if first else 1]

    def fetch(p, t, i):
        row = ((i % 2 * blocks + i // 2) * 2 + core) * run
        column = lax.rem(at_ref[2] + 2 * p + t, N_Y) * rank
        return pltpu.make_async_copy(
            s_hbm.at[pl.ds(pl.multiple_of(row, run), run), pl.ds(pl.multiple_of(column, rank), rank)],
            s_ref.at[p, i * run : (i + 1) * run, t * rank : (t + 1) * rank],
            sem.at[p, t, i],
        )

    pieces = [(t, i) for t in range(2) for i in range(2 * blocks)]
    for p in range(2):
        for t, i in pieces:
            fetch(p, t, i).start()
    h = [jnp.concatenate([h_ref[x, zh, b] for zh in range(2) for x in range(4)], axis=0) for b in range(blocks)]
    for b in range(blocks):
        ht_ref[b * half : (b + 1) * half, :] = h[b].T
    rowsum = jnp.dot(jnp.ones((8, span), jnp.bfloat16), ht_ref[...], preferred_element_type=jnp.float32)
    colsum = jnp.zeros((rank, 1), jnp.float32)
    for p in range(2):
        wt = jnp.concatenate([w[...] for w in ((w0, w1), (w2, w3))[p]], axis=0).T
        colsum = colsum + jnp.sum(wt.astype(jnp.float32), axis=1, keepdims=True)
        recon = jnp.dot(ht_ref[...], wt, preferred_element_type=jnp.float32)
        for t, i in pieces:
            fetch(p, t, i).wait()
        quotient = (s_ref[p].astype(jnp.float32) / recon).astype(jnp.bfloat16)
        hn = lax.dot_general(wt, quotient, (((1,), (1,)), ((), ())), preferred_element_type=jnp.float32)
        if p == 0:
            sums_ref[:, :span] = hn
        else:
            sums_ref[:, :span] += hn
        wn = None
        for b in range(blocks):
            part = jnp.dot(h[b], quotient[b * half : (b + 1) * half], preferred_element_type=jnp.float32)
            wn = part if wn is None else wn + part
        for t in range(2):
            ref = (n0, n1, n2, n3)[2 * p + t]
            part = wn[:, t * rank : (t + 1) * rank]
            if first:
                ref[:rank, :] = part
                ref[rank:, :] = rowsum
                continue
            part = part + before[2 * p + t][:rank, :]
            total = rowsum + before[2 * p + t][rank:, :]
            if p == 0 and t == 0:
                ref[:rank, :] = part
                ref[rank:, :] = total
                continue
            high_a, high_b, code = coded(part[: rank // 2], part[rank // 2 :])
            ref[: rank // 2, :] = high_a.astype(jnp.bfloat16)
            ref[rank // 2 : rank, :] = high_b.astype(jnp.bfloat16)
            ref[rank : rank + rank // 2, :] = code.astype(jnp.bfloat16)
            ref[rank + rank // 2 :, :] = hi_lo(total)
    sums_ref[:, span:] = jnp.broadcast_to(colsum, (rank, LANES))


def half_sweep(at, spectra, h, ws, before=()):
    frames, rows = spectra.shape
    blocks, half, rank = h.shape[2], h.shape[4], ws[0].shape[1]
    return pl.pallas_call(
        functools.partial(sweep_kernel, not before),
        in_specs=whole(1, pltpu.SMEM) + whole(1, pl.ANY) + whole(5 + len(before)),
        out_specs=whole(5),
        out_shape=[jax.ShapeDtypeStruct((rank + 8, rank), jnp.float32)]
        + [
            jax.ShapeDtypeStruct((rank + rank // 2 + 16, rank), jnp.bfloat16)
            if before
            else jax.ShapeDtypeStruct((rank + 8, rank), jnp.float32)
        ]
        * 3
        + [jax.ShapeDtypeStruct((rank, blocks * half + LANES), jnp.float32)],
        scratch_shapes=[
            pltpu.VMEM((blocks * half, rank), jnp.bfloat16),
            pltpu.VMEM((2, blocks * half, 2 * rank), jnp.bfloat16),
            pltpu.SemaphoreType.DMA((2, 2, 2 * blocks)),
        ],
        compiler_params=pltpu.CompilerParams(vmem_limit_bytes=28 << 20),
        cost_estimate=pl.CostEstimate(flops=3 * frames * rows * rank, bytes_accessed=4 << 20, transcendentals=0),
        name="sweep_a" if not before else "sweep_b",
    )(at, spectra, h, *ws, *before)


def pair_kernel(a_ref, b_ref, out_ref):
    each = (out_ref.shape[1] - 2 * TAIL) // 6
    half, span = 4 * LANES, a_ref.shape[1] - LANES
    group = lax.broadcasted_iota(jnp.int32, (TAIL, LANES), 1) // each
    for r in range(N_R):
        rows, at = slice(r * each, (r + 1) * each), (r % 4 * 2 + r // 4) * 2
        sums = a_ref[rows, span:] + b_ref[rows, span:]
        tail = sums[:TAIL]
        for j in range(1, each // TAIL):
            tail = jnp.where(group == j, sums[j * TAIL : (j + 1) * TAIL], tail)
        for zl in range(2):
            parts = []
            for c in range(4):
                columns = slice(zl * half + c * LANES, zl * half + (c + 1) * LANES)
                parts.append(a_ref[rows, columns] + b_ref[rows, columns])
            codes = []
            for c in (0, 2):
                high_a, high_b, code = coded(parts[c], parts[c + 1])
                out_ref[at + zl, c * each : (c + 1) * each, :] = high_a.astype(jnp.bfloat16)
                out_ref[at + zl, (c + 1) * each : (c + 2) * each, :] = high_b.astype(jnp.bfloat16)
                codes.append(code.astype(jnp.bfloat16))
            out_ref[at + zl, 4 * each : 6 * each, :] = jnp.concatenate(codes, axis=0)
            out_ref[at + zl, 6 * each :, :] = hi_lo(tail)


def pair(a, b, each):
    return pl.pallas_call(
        pair_kernel,
        in_specs=whole(2),
        out_specs=whole(1)[0],
        out_shape=jax.ShapeDtypeStruct((N_P, 6 * each + 2 * TAIL, LANES), jnp.bfloat16),
        compiler_params=pltpu.CompilerParams(vmem_limit_bytes=12 << 20),
        name="pair",
    )(a, b)


def h_update_kernel(parts_ref, h_ref, new_ref, *low_refs):
    each = h_ref.shape[0]
    blocks, tail = [0.0] * 4, 0.0
    for i in range(N_P):
        part = parts_ref[i].astype(jnp.float32)
        pieces = [part[c * each : (c + 1) * each] for c in range(6)]
        values = decoded(*pieces[0:2], pieces[4]) + decoded(*pieces[2:4], pieces[5])
        blocks = [block + value for block, value in zip(blocks, values)]
        tail = tail + part[6 * each :]
    numer = jnp.concatenate(blocks, axis=1)
    tail = tail[:TAIL] + tail[TAIL:]
    colsum = jnp.concatenate([tail[:, j * each : j * each + 1] for j in range(each // TAIL)], axis=0)
    new = h_ref[...] * numer / colsum
    new_ref[...] = new
    low = new.astype(jnp.bfloat16)
    for low_ref in low_refs:
        for i in range(N_P):
            low_ref[i] = low


def h_update(parts, h, more):
    return pl.pallas_call(
        h_update_kernel,
        in_specs=whole(2),
        out_specs=whole(1 + more),
        out_shape=[jax.ShapeDtypeStruct(h.shape, jnp.float32)]
        + [jax.ShapeDtypeStruct((N_P, *h.shape), jnp.bfloat16)] * more,
        compiler_params=pltpu.CompilerParams(vmem_limit_bytes=12 << 20),
        name="h_update",
    )(parts, h)


def w_update_kernel(p0, p1, p2, p3, w_ref, new_ref, *low_refs):
    rank = w_ref.shape[1]
    cut = rank // 2
    tops, bottoms, rowsum = p0[:cut, :], p0[cut:rank, :], p0[rank : rank + 1, :]
    for ref in (p1, p2, p3):
        part = ref[...].astype(jnp.float32)
        top, bottom = decoded(part[:cut], part[cut:rank], part[rank : rank + cut])
        tops, bottoms = tops + top, bottoms + bottom
        rowsum = rowsum + part[rank + cut : rank + cut + 1] + part[rank + cut + 8 : rank + cut + 9]
    new = w_ref[...] * jnp.concatenate([tops, bottoms], axis=0).T / rowsum
    new_ref[...] = new
    for low_ref in low_refs:
        low_ref[...] = new.astype(jnp.bfloat16)


def w_update(parts, w, more):
    return pl.pallas_call(
        w_update_kernel,
        in_specs=whole(5),
        out_specs=whole(1 + more),
        out_shape=[jax.ShapeDtypeStruct(w.shape, jnp.float32)] + [jax.ShapeDtypeStruct(w.shape, jnp.bfloat16)] * more,
        compiler_params=pltpu.CompilerParams(vmem_limit_bytes=12 << 20),
        name="w_update",
    )(*parts, w)


def spread_kernel(h_hbm, out_hbm, h_ref, low_ref, in_sem, out_sem):
    fetch = pltpu.make_async_copy(h_hbm, h_ref, in_sem)
    fetch.start()
    fetch.wait()
    low_ref[...] = h_ref[...].astype(jnp.bfloat16)
    puts = [pltpu.make_async_copy(low_ref, out_hbm.at[i], out_sem.at[i]) for i in range(N_P)]
    for put in puts:
        put.start()
    for put in puts:
        put.wait()


def spread(h):
    return pl.pallas_call(
        spread_kernel,
        in_specs=whole(1, pl.ANY),
        out_specs=whole(1, pl.ANY)[0],
        out_shape=jax.ShapeDtypeStruct((N_P, *h.shape), jnp.bfloat16),
        scratch_shapes=[
            pltpu.VMEM(h.shape, jnp.float32),
            pltpu.VMEM(h.shape, jnp.bfloat16),
            pltpu.SemaphoreType.DMA,
            pltpu.SemaphoreType.DMA((N_P,)),
        ],
        compiler_params=pltpu.CompilerParams(vmem_limit_bytes=56 << 20),
        name="spread",
    )(h)


def exchange(x, axes):
    return lax.all_to_all(x, axes, 0, 0, tiled=True)


def from_sibling(x):
    return lax.ppermute(x, "core", [(0, 1), (1, 0)])


def sent_ahead(x, t):
    return lax.ppermute(x, "y", [(i, (i + t) % N_Y) for i in range(N_Y)])


def taken_ahead(x):
    return [x] + [lax.ppermute(x, "y", [(i, (i - t) % N_Y) for i in range(N_Y)]) for t in range(1, N_Y)]


def local(samples, w, h):
    record = samples.reshape(samples.shape[2], samples.shape[3])
    core, y = lax.axis_index("core"), lax.axis_index("y")
    ats = [jnp.stack(order).astype(jnp.int32) for order in ([1 - core, core, y], [core, 1 - core, y])]
    h_own = exchange(spread(h), RANKS).reshape(4, 2, 2, *h.shape)
    energy = energies(record, dft_table())
    frames, rows = energy.shape[4:]
    energy, w_low = lax.optimization_barrier((energy, w.astype(jnp.bfloat16)))
    ws = taken_ahead(w_low)
    h_oth = from_sibling(h_own)
    spectra = exchange(energy.reshape(2 * N_P, frames, rows), TILE).reshape(2 * N_P * frames, rows)
    for step in range(ITERS):
        sibling_first = step == 0
        halves = (h_oth, h_own) if sibling_first else (h_own, h_oth)
        at = ats[0 if sibling_first else 1]
        *parts, s_first = half_sweep(at, spectra, halves[0], ws)
        n0, n1, n2, n3, s_second = half_sweep(at, spectra, halves[1], ws, parts)
        s_oth, s_own = (s_first, s_second) if sibling_first else (s_second, s_first)
        s_got = from_sibling(s_oth)
        w_parts = [n0] + [sent_ahead(n, t + 1) for t, n in enumerate((n1, n2, n3))]
        h_parts = exchange(pair(s_own, s_got, h.shape[0]), RANKS)
        more = step + 1 < ITERS
        h, *low = h_update(h_parts, h, more)
        if low:
            w_parts, low, h = lax.optimization_barrier((w_parts, low, h))
        w, *w_low = w_update(w_parts, w, more)
        if more:
            ws = taken_ahead(*w_low)
            ws, h_own = lax.optimization_barrier((ws, exchange(*low, RANKS)))
            h_own = h_own.reshape(4, 2, 2, *h.shape)
            h_oth = from_sibling(h_own)
    return (w, h)


def solution(mesh):
    fine = Mesh(mesh.devices.reshape(SIZES), AXES)
    row, col = ("zh", "x"), ("zl", "y", "core")
    return jax.shard_map(
        local,
        mesh=fine,
        in_specs=(P(col, row, None, None), P(row + col, None), P(row, col)),
        out_specs=(P(row + col, None), P(row, col)),
        check_vma=False,
    )
```

```python
import functools
import math

import jax
import jax.numpy as jnp
import numpy as np
from jax import lax
from jax.experimental import pallas as pl
from jax.experimental.pallas import tpu as pltpu
from jax.sharding import Mesh
from jax.sharding import PartitionSpec as P

BINS = 128
ITERS = 2
WIN = 256

AXES = ("zh", "x", "zl", "y", "core")
SIZES = (2, 4, 2, 4, 2)
TILE = ("zh", "zl", "core", "x")
RANKS = ("x", "zh", "zl")
N_Y = 4
N_R = 8
N_P = 16
LANES = 128
TAIL = 8


def dft_table():
    n = np.arange(WIN, dtype=np.int32)
    k = np.arange(BINS, dtype=np.int32)
    phases = (n[:, None] * k[None, :] % WIN).astype(np.float32) * np.float32(2.0 * math.pi / WIN)
    taper = np.float32(0.5) - np.float32(0.5) * np.cos(n.astype(np.float32) * np.float32(2.0 * math.pi / WIN))
    taper = (taper / np.float32(math.sqrt(3.0 * WIN / 8.0))).astype(np.float32)
    both = np.concatenate([taper[:, None] * np.cos(phases), -taper[:, None] * np.sin(phases)], axis=1)
    return jnp.asarray(both.astype(np.float32)).astype(jnp.bfloat16)


def whole(n, space=pltpu.VMEM):
    return [pl.BlockSpec(memory_space=space)] * n


def energy_kernel(x_hbm, table_ref, out_hbm, x_ref, out_ref, in_sem, out_sem):
    blocks, chans, samples = x_ref.shape
    frames = samples // WIN
    group = 16

    def fetch(r):
        return pltpu.make_async_copy(x_hbm.at[pl.ds(r * chans, chans), :], x_ref.at[r], in_sem.at[r])

    def put(r):
        return pltpu.make_async_copy(out_ref.at[r], out_hbm.at[r // 4, :, :, r % 4], out_sem.at[r])

    for r in range(blocks):
        fetch(r).start()
    table = table_ref[...]

    @pl.loop(0, blocks)
    def _(r):
        fetch(r).wait()
        for g in range(frames // group):
            x = jnp.concatenate(
                [x_ref[r, :, (g * group + f) * WIN : (g * group + f + 1) * WIN] for f in range(group)], axis=0
            )
            spec = jnp.dot(x, table, preferred_element_type=jnp.float32)
            re, im = spec[:, :BINS], spec[:, BINS:]
            energy = (re * re + im * im).reshape(group, chans, BINS)
            energy = pltpu.einshape("fcb->cfb", energy).astype(jnp.bfloat16)
            for c in range(chans):
                zl, y, core, j = c // 16, (c // 4) % 4, (c // 2) % 2, c % 2
                at = (y * 2 + j) * BINS
                out_ref[r, zl, core, g * group : (g + 1) * group, at : at + BINS] = energy[c]
        put(r).start()

    for r in range(blocks):
        put(r).wait()


def energies(record, table):
    channels, samples = record.shape
    frames = samples // WIN
    per_row = channels // N_R
    rows = channels * BINS // (2 * N_P)
    return pl.pallas_call(
        energy_kernel,
        in_specs=[pl.BlockSpec(memory_space=pl.ANY), pl.BlockSpec(memory_space=pltpu.VMEM)],
        out_specs=pl.BlockSpec(memory_space=pl.ANY),
        out_shape=jax.ShapeDtypeStruct((2, 2, 2, 4, frames, rows), jnp.bfloat16),
        scratch_shapes=[
            pltpu.VMEM((N_R, per_row, samples), jnp.bfloat16),
            pltpu.VMEM((N_R, 2, 2, frames, rows), jnp.bfloat16),
            pltpu.SemaphoreType.DMA((N_R,)),
            pltpu.SemaphoreType.DMA((N_R,)),
        ],
        compiler_params=pltpu.CompilerParams(vmem_limit_bytes=58 << 20),
        cost_estimate=pl.CostEstimate(
            flops=2 * channels * frames * WIN * WIN, bytes_accessed=12 << 20, transcendentals=0
        ),
        name="energy",
    )(record, table)


def level(x, high):
    relative = jnp.where(high == 0.0, 0.0, (x - high) / high)
    return jnp.clip(jnp.floor(relative * (7.0 * 256.0) + 0.5), -7.0, 7.0) + 7.0


def coded(a, b):
    high_a, high_b = [x.astype(jnp.bfloat16).astype(jnp.float32) for x in (a, b)]
    return high_a, high_b, level(a, high_a) * 15.0 + level(b, high_b)


def decoded(high_a, high_b, code):
    first = jnp.floor((code + 0.5) * (1.0 / 15.0))
    second = code - 15.0 * first
    return [high + high * ((q - 7.0) * (1.0 / (7.0 * 256.0))) for high, q in ((high_a, first), (high_b, second))]


def hi_lo(x):
    high = x.astype(jnp.bfloat16).astype(jnp.float32)
    return jnp.concatenate([high, x - high], axis=0).astype(jnp.bfloat16)


def sweep_kernel(first, at_ref, s_hbm, h_ref, w0, w1, w2, w3, *refs):
    before, (n0, n1, n2, n3, sums_ref, ht_ref, s_ref, sem) = (() if first else refs[:4]), refs[-8:]
    blocks, half = h_ref.shape[2], h_ref.shape[4]
    rank, span = ht_ref.shape[1], blocks * half
    run = half // 2
    core = at_ref[0 if first else 1]

    def fetch(p, t, i):
        row = ((i % 2 * blocks + i // 2) * 2 + core) * run
        column = lax.rem(at_ref[2] + 2 * p + t, N_Y) * rank
        return pltpu.make_async_copy(
            s_hbm.at[pl.ds(pl.multiple_of(row, run), run), pl.ds(pl.multiple_of(column, rank), rank)],
            s_ref.at[p, i * run : (i + 1) * run, t * rank : (t + 1) * rank],
            sem.at[p, t, i],
        )

    pieces = [(t, i) for t in range(2) for i in range(2 * blocks)]
    for p in range(2):
        for t, i in pieces:
            fetch(p, t, i).start()
    h = [jnp.concatenate([h_ref[x, zh, b] for zh in range(2) for x in range(4)], axis=0) for b in range(blocks)]
    for b in range(blocks):
        ht_ref[b * half : (b + 1) * half, :] = h[b].T
    rowsum = jnp.dot(jnp.ones((8, span), jnp.bfloat16), ht_ref[...], preferred_element_type=jnp.float32)
    colsum = jnp.zeros((rank, 1), jnp.float32)
    for p in range(2):
        wt = jnp.concatenate([w[...] for w in ((w0, w1), (w2, w3))[p]], axis=0).T
        colsum = colsum + jnp.sum(wt.astype(jnp.float32), axis=1, keepdims=True)
        recon = jnp.dot(ht_ref[...], wt, preferred_element_type=jnp.float32)
        for t, i in pieces:
            fetch(p, t, i).wait()
        quotient = (s_ref[p].astype(jnp.float32) / recon).astype(jnp.bfloat16)
        hn = lax.dot_general(wt, quotient, (((1,), (1,)), ((), ())), preferred_element_type=jnp.float32)
        if p == 0:
            sums_ref[:, :span] = hn
        else:
            sums_ref[:, :span] += hn
        wn = None
        for b in range(blocks):
            part = jnp.dot(h[b], quotient[b * half : (b + 1) * half], preferred_element_type=jnp.float32)
            wn = part if wn is None else wn + part
        for t in range(2):
            ref = (n0, n1, n2, n3)[2 * p + t]
            part = wn[:, t * rank : (t + 1) * rank]
            if first:
                ref[:rank, :] = part
                ref[rank:, :] = rowsum
                continue
            part = part + before[2 * p + t][:rank, :]
            total = rowsum + before[2 * p + t][rank:, :]
            if p == 0 and t == 0:
                ref[:rank, :] = part
                ref[rank:, :] = total
                continue
            high_a, high_b, code = coded(part[: rank // 2], part[rank // 2 :])
            ref[: rank // 2, :] = high_a.astype(jnp.bfloat16)
            ref[rank // 2 : rank, :] = high_b.astype(jnp.bfloat16)
            ref[rank : rank + rank // 2, :] = code.astype(jnp.bfloat16)
            ref[rank + rank // 2 :, :] = hi_lo(total)
    sums_ref[:, span:] = jnp.broadcast_to(colsum, (rank, LANES))


def half_sweep(at, spectra, h, ws, before=()):
    frames, rows = spectra.shape
    blocks, half, rank = h.shape[2], h.shape[4], ws[0].shape[1]
    return pl.pallas_call(
        functools.partial(sweep_kernel, not before),
        in_specs=whole(1, pltpu.SMEM) + whole(1, pl.ANY) + whole(5 + len(before)),
        out_specs=whole(5),
        out_shape=[jax.ShapeDtypeStruct((rank + 8, rank), jnp.float32)]
        + [
            jax.ShapeDtypeStruct((rank + rank // 2 + 16, rank), jnp.bfloat16)
            if before
            else jax.ShapeDtypeStruct((rank + 8, rank), jnp.float32)
        ]
        * 3
        + [jax.ShapeDtypeStruct((rank, blocks * half + LANES), jnp.float32)],
        scratch_shapes=[
            pltpu.VMEM((blocks * half, rank), jnp.bfloat16),
            pltpu.VMEM((2, blocks * half, 2 * rank), jnp.bfloat16),
            pltpu.SemaphoreType.DMA((2, 2, 2 * blocks)),
        ],
        compiler_params=pltpu.CompilerParams(vmem_limit_bytes=28 << 20),
        cost_estimate=pl.CostEstimate(flops=3 * frames * rows * rank, bytes_accessed=4 << 20, transcendentals=0),
        name="sweep_a" if not before else "sweep_b",
    )(at, spectra, h, *ws, *before)


def pair_kernel(a_ref, b_ref, out_ref):
    each = (out_ref.shape[1] - 2 * TAIL) // 6
    half, span = 4 * LANES, a_ref.shape[1] - LANES
    group = lax.broadcasted_iota(jnp.int32, (TAIL, LANES), 1) // each
    for r in range(N_R):
        rows, at = slice(r * each, (r + 1) * each), (r % 4 * 2 + r // 4) * 2
        sums = a_ref[rows, span:] + b_ref[rows, span:]
        tail = sums[:TAIL]
        for j in range(1, each // TAIL):
            tail = jnp.where(group == j, sums[j * TAIL : (j + 1) * TAIL], tail)
        for zl in range(2):
            parts = []
            for c in range(4):
                columns = slice(zl * half + c * LANES, zl * half + (c + 1) * LANES)
                parts.append(a_ref[rows, columns] + b_ref[rows, columns])
            codes = []
            for c in (0, 2):
                high_a, high_b, code = coded(parts[c], parts[c + 1])
                out_ref[at + zl, c * each : (c + 1) * each, :] = high_a.astype(jnp.bfloat16)
                out_ref[at + zl, (c + 1) * each : (c + 2) * each, :] = high_b.astype(jnp.bfloat16)
                codes.append(code.astype(jnp.bfloat16))
            out_ref[at + zl, 4 * each : 6 * each, :] = jnp.concatenate(codes, axis=0)
            out_ref[at + zl, 6 * each :, :] = hi_lo(tail)


def pair(a, b, each):
    return pl.pallas_call(
        pair_kernel,
        in_specs=whole(2),
        out_specs=whole(1)[0],
        out_shape=jax.ShapeDtypeStruct((N_P, 6 * each + 2 * TAIL, LANES), jnp.bfloat16),
        compiler_params=pltpu.CompilerParams(vmem_limit_bytes=12 << 20),
        name="pair",
    )(a, b)


def h_update_kernel(parts_ref, h_ref, new_ref, *refs):
    each = h_ref.shape[0]
    blocks, tail = [0.0] * 4, 0.0
    for i in range(N_P):
        part = parts_ref[i].astype(jnp.float32)
        pieces = [part[c * each : (c + 1) * each] for c in range(6)]
        values = decoded(*pieces[0:2], pieces[4]) + decoded(*pieces[2:4], pieces[5])
        blocks = [block + value for block, value in zip(blocks, values)]
        tail = tail + part[6 * each :]
    numer = jnp.concatenate(blocks, axis=1)
    tail = tail[:TAIL] + tail[TAIL:]
    colsum = jnp.concatenate([tail[:, j * each : j * each + 1] for j in range(each // TAIL)], axis=0)
    new = h_ref[...] * numer / colsum
    new_ref[...] = new
    if refs:
        out_hbm, low_ref, sem = refs
        low_ref[...] = new.astype(jnp.bfloat16)
        puts = [pltpu.make_async_copy(low_ref, out_hbm.at[i], sem.at[i]) for i in range(N_P)]
        for put in puts:
            put.start()
        for put in puts:
            put.wait()


def h_update(parts, h, more):
    return pl.pallas_call(
        h_update_kernel,
        in_specs=whole(2),
        out_specs=whole(1) + whole(1, pl.ANY) * more,
        out_shape=[jax.ShapeDtypeStruct(h.shape, jnp.float32)]
        + [jax.ShapeDtypeStruct((N_P, *h.shape), jnp.bfloat16)] * more,
        scratch_shapes=[pltpu.VMEM(h.shape, jnp.bfloat16), pltpu.SemaphoreType.DMA((N_P,))] * more,
        compiler_params=pltpu.CompilerParams(vmem_limit_bytes=12 << 20),
        name="h_update",
    )(parts, h)


def w_update_kernel(p0, p1, p2, p3, w_ref, new_ref, *low_refs):
    rank = w_ref.shape[1]
    cut = rank // 2
    tops, bottoms, rowsum = p0[:cut, :], p0[cut:rank, :], p0[rank : rank + 1, :]
    for ref in (p1, p2, p3):
        part = ref[...].astype(jnp.float32)
        top, bottom = decoded(part[:cut], part[cut:rank], part[rank : rank + cut])
        tops, bottoms = tops + top, bottoms + bottom
        rowsum = rowsum + part[rank + cut : rank + cut + 1] + part[rank + cut + 8 : rank + cut + 9]
    new = w_ref[...] * jnp.concatenate([tops, bottoms], axis=0).T / rowsum
    new_ref[...] = new
    for low_ref in low_refs:
        low_ref[...] = new.astype(jnp.bfloat16)


def w_update(parts, w, more):
    return pl.pallas_call(
        w_update_kernel,
        in_specs=whole(5),
        out_specs=whole(1 + more),
        out_shape=[jax.ShapeDtypeStruct(w.shape, jnp.float32)] + [jax.ShapeDtypeStruct(w.shape, jnp.bfloat16)] * more,
        compiler_params=pltpu.CompilerParams(vmem_limit_bytes=12 << 20),
        name="w_update",
    )(*parts, w)


def spread_kernel(h_hbm, out_hbm, h_ref, low_ref, in_sem, out_sem):
    fetch = pltpu.make_async_copy(h_hbm, h_ref, in_sem)
    fetch.start()
    fetch.wait()
    low_ref[...] = h_ref[...].astype(jnp.bfloat16)
    puts = [pltpu.make_async_copy(low_ref, out_hbm.at[i], out_sem.at[i]) for i in range(N_P)]
    for put in puts:
        put.start()
    for put in puts:
        put.wait()


def spread(h):
    return pl.pallas_call(
        spread_kernel,
        in_specs=whole(1, pl.ANY),
        out_specs=whole(1, pl.ANY)[0],
        out_shape=jax.ShapeDtypeStruct((N_P, *h.shape), jnp.bfloat16),
        scratch_shapes=[
            pltpu.VMEM(h.shape, jnp.float32),
            pltpu.VMEM(h.shape, jnp.bfloat16),
            pltpu.SemaphoreType.DMA,
            pltpu.SemaphoreType.DMA((N_P,)),
        ],
        compiler_params=pltpu.CompilerParams(vmem_limit_bytes=56 << 20),
        name="spread",
    )(h)


def exchange(x, axes):
    return lax.all_to_all(x, axes, 0, 0, tiled=True)


def from_sibling(x):
    return lax.ppermute(x, "core", [(0, 1), (1, 0)])


def sent_ahead(x, t):
    return lax.ppermute(x, "y", [(i, (i + t) % N_Y) for i in range(N_Y)])


def taken_ahead(x):
    return [x] + [lax.ppermute(x, "y", [(i, (i - t) % N_Y) for i in range(N_Y)]) for t in range(1, N_Y)]


def local(samples, w, h):
    record = samples.reshape(samples.shape[2], samples.shape[3])
    core, y = lax.axis_index("core"), lax.axis_index("y")
    at = jnp.stack([1 - core, core, y]).astype(jnp.int32)
    h_own = exchange(spread(h), RANKS).reshape(4, 2, 2, *h.shape)
    energy = energies(record, dft_table())
    frames, rows = energy.shape[4:]
    energy, w_low = lax.optimization_barrier((energy, w.astype(jnp.bfloat16)))
    ws = taken_ahead(w_low)
    h_oth = from_sibling(h_own)
    spectra = exchange(energy.reshape(2 * N_P, frames, rows), TILE).reshape(2 * N_P * frames, rows)
    for step in range(ITERS):
        *parts, s_oth = half_sweep(at, spectra, h_oth, ws)
        s_got = from_sibling(s_oth)
        n0, n1, n2, n3, s_own = half_sweep(at, spectra, h_own, ws, parts)
        w_parts = [n0] + [sent_ahead(n, t + 1) for t, n in enumerate((n1, n2, n3))]
        h_parts = exchange(pair(s_own, s_got, h.shape[0]), RANKS)
        more = step + 1 < ITERS
        h, *low = h_update(h_parts, h, more)
        if low:
            w_parts, low, h = lax.optimization_barrier((w_parts, low, h))
        w, *w_low = w_update(w_parts, w, more)
        if more:
            ws = taken_ahead(*w_low)
            ws, h_own = lax.optimization_barrier((ws, exchange(*low, RANKS)))
            h_own = h_own.reshape(4, 2, 2, *h.shape)
            h_oth = from_sibling(h_own)
    return (w, h)


def solution(mesh):
    fine = Mesh(mesh.devices.reshape(SIZES), AXES)
    row, col = ("zh", "x"), ("zl", "y", "core")
    return jax.shard_map(
        local,
        mesh=fine,
        in_specs=(P(col, row, None, None), P(row + col, None), P(row, col)),
        out_specs=(P(row + col, None), P(row, col)),
        check_vma=False,
    )
```
